32 devices in a mesh: expert: 8 (over z, core), shard: 4 (over y, x).
Axes of the slice: x: 2, y: 2, z: 4, core: 2. Of those that a mesh axis runs over, the one named last changes fastest.
Arguments:
- layer_input: bfloat16 [16384, 1536], P(('expert', 'shard')), may hold values from -6 to 6
- out_cotangent: bfloat16 [16384, 1536], P(('expert', 'shard')), may hold values from -6 to 6
- parents: int32 [128], P(('expert', 'shard')), may hold values from 0 to 2, as said below
- routes: int32 [16384, 8], P(('expert', 'shard')), may hold values from 0 to 15, all different within a row; in each aligned block of 512 rows (0 to 511, 512 to 1023, ...) at most 320 rows name the same one
- norm1_gain: bfloat16 [1536], P('shard'), may hold values from 0.099609375 to 1.8984375
- qkv_weight: bfloat16 [1536, 2560], P('shard'), may hold values from -0.15625 to 0.15625
- out_weight: bfloat16 [1536, 1536], P('shard'), may hold values from -0.875 to 0.875
- norm2_gain: bfloat16 [1536], P('shard'), may hold values from 0.099609375 to 1.8984375
- router_weight: bfloat16 [1536, 16], P('shard'), may hold values from -0.078125 to 0.078125
- gate_weight: bfloat16 [16, 1536, 512], P('expert', 'shard'), may hold values from -0.15625 to 0.15625
- up_weight: bfloat16 [16, 1536, 512], P('expert', 'shard'), may hold values from -0.15625 to 0.15625
- down_weight: bfloat16 [16, 512, 1536], P('expert', None, 'shard'), may hold values from -0.75 to 0.75
Outputs:
- output: bfloat16 [16384, 1536], P(('expert', 'shard'))
- input_grad: bfloat16 [16384, 1536], P(('expert', 'shard'))
- grad_norm1_gain: float32 [1536], P('shard')
- grad_qkv_weight: float32 [1536, 2560], P('shard')
- grad_out_weight: float32 [1536, 1536], P('shard')
- grad_norm2_gain: float32 [1536], P('shard')
- grad_router_weight: float32 [1536, 16], P('shard')
- grad_gate_weight: float32 [16, 1536, 512], P('expert', 'shard')
- grad_up_weight: float32 [16, 1536, 512], P('expert', 'shard')
- grad_down_weight: float32 [16, 512, 1536], P('expert', None, 'shard')
The draws below stay inside these ranges and needn't reach their ends.
Inputs may be any that keep to these rules, and one draw needn't show every extreme that they name: `parents`: within each tree's block of 4 entries, entry s names a segment before s, entry 0 names 0, and the last entry names its predecessor. `routes`: each row names 8 different experts; in the rows of one device each expert is named by at most 320 rows, a bound that some block reaches.
All inputs are finite; a program needn't handle non-finite values.
Results may differ from the reference program's by a relative error of at most 0.02.
Values may be sent and summed in bfloat16 or wider, within the bound.
No kernel may reach another device: no remote copies, remote signals or barrier semaphores. Data moves between devices by JAX's collectives and lax.ppermute only.
A program may use at most 320 MiB of HBM per device.

```python
import math
import jax
import jax.numpy as jnp
import numpy as np
from jax import lax

D = 1536
HEADS = 24
KV_HEADS = 8
HEAD_DIM = 64
FF_E = 512
TOP = 8
TOK_DEV = 512
SEG = 128
SEGS = 4
TREES = 32
TOKENS = 16384
EXPERTS = 16
CAP = 320


def draw_parents(key, part):
    seg_ids = jnp.arange(SEGS, dtype=jnp.int32)
    raw_bits = jax.random.randint(key, (TREES, SEGS), 0, 1 << 30, dtype=jnp.int32)
    picked = raw_bits % jnp.maximum(seg_ids, 1)[None, :]
    picked = jnp.where(seg_ids[None, :] == SEGS - 1, SEGS - 2, picked)
    return picked.reshape(-1).astype(jnp.int32)


def steps_of(own_key, dims, split, least, largest):
    gain = 1.0
    for dim, parts in split:
        heights = jax.random.uniform(jax.random.fold_in(jax.random.fold_in(own_key, 6), dim), (parts,), jnp.float32, least / len(split), largest / len(split))
        gain = gain * jnp.repeat(jnp.exp(heights), dims[dim] // parts).reshape((-1,) + (1,) * (len(dims) - 1 - dim))
    return gain


def assign_block(stream_key, own, number, rows, number_of, top, most, slope):
    sequence = jax.random.permutation(stream_key, number_of)
    heavy_load, common = shares(number_of, rows * top, most, slope, True), shares(number_of, rows * top, most, slope, False)
    places = jnp.arange(number_of)

    def named(lengths, offset_by):
        used = int((lengths > 0).sum())
        fixed = max(1, used // 4)
        passed = fixed + (places - fixed + offset_by * (used - fixed)) % max(1, number_of - fixed)
        return jnp.zeros((number_of,), jnp.int32).at[sequence[jnp.where(places < fixed, places, passed)]].set(jnp.asarray(lengths, jnp.int32))

    lengths = jnp.where(number % 4 == 0, named(heavy_load, number // 4), named(common, number - number // 4 - 1))
    mixed = jax.random.permutation(jax.random.fold_in(own, 3), number_of)
    giver, sink = mixed[0:number_of // 2 * 2:2], mixed[1:number_of // 2 * 2:2]
    slack = jnp.minimum(lengths[giver] - 1, most - lengths[sink]) // 2
    slack = jnp.where((giver == sequence[0]) | (sink == sequence[0]) | (lengths[sink] == 0), 0, jnp.maximum(slack, 0))
    passed = jax.random.randint(jax.random.fold_in(own, 4), (number_of // 2,), 0, 1 << 20) % (slack + 1)
    lengths = lengths.at[giver].add(-passed).at[sink].add(passed)
    items = jnp.searchsorted(jnp.cumsum(lengths), jnp.arange(rows * top), side="right").astype(jnp.int32)
    table = items.reshape(top, rows).T
    table = table[jax.random.permutation(jax.random.fold_in(own, 1), rows)]
    offset_by = jax.random.randint(jax.random.fold_in(own, 2), (rows, 1), 0, top)
    return jnp.take_along_axis(table, (jnp.arange(top)[None, :] + offset_by) % top, axis=1)


def shares(count, total, most, skew, full):
    weights = [(1 << 20) // math.isqrt(rank ** skew) + 1 for rank in range(1, count + 1)]
    largest = most if full else min(most, max(-(-total // count), total * weights[0] // sum(weights)))
    least = 1 if total - largest >= count - 1 else 0
    given, spare = [largest] + [least] * (count - 1), total - largest - least * (count - 1)
    while spare > 0:
        candidates = [i for i in range(1, count) if given[i] < largest] or [i for i in range(1, count) if given[i] < most]
        mass, left = sum([weights[i] for i in candidates]), spare
        for i in candidates:
            more = min(most - given[i], max(1, left * weights[i] // mass), spare)
            given[i] = given[i] + more
            spare = spare - more
    return np.array(given)


def gaussian(rng, shape, deviation, limit, cuts=(), held_as=jnp.bfloat16):
    values = deviation * jax.random.normal(rng, shape, jnp.float32)
    if cuts:
        values = values * steps_of(rng, shape, cuts, -0.22, 0.18)
    return jnp.clip(values, -limit, limit).astype(held_as)


def setup_inputs(seed: int = 0) -> dict:
    arg_keys = jax.random.split(jax.random.key(seed), 13)
    layer_input = gaussian(arg_keys[0], (TOKENS, D), 1.0, 6.0, ((0, 32),))
    out_cotangent = gaussian(arg_keys[1], (TOKENS, D), 1.0, 6.0, ((0, 32),))
    parents = draw_parents(jax.random.fold_in(arg_keys[12], 71), 0)
    routes_keys = jax.random.split(jax.random.fold_in(arg_keys[3], 1), TOKENS // TOK_DEV)
    routes_turns = jax.random.permutation(jax.random.fold_in(arg_keys[3], 3), TOKENS // TOK_DEV)
    routes = jax.vmap(lambda own, number: assign_block(jax.random.fold_in(arg_keys[3], 2), own, number, TOK_DEV, EXPERTS, TOP, CAP, 1))(routes_keys, routes_turns).reshape((TOKENS, TOP))
    norm1_gain = jnp.clip(1.0 + 0.18 * jax.random.normal(arg_keys[4], (D,), jnp.float32), 0.099609375, 1.8984375).astype(jnp.bfloat16)
    qkv_weight = gaussian(arg_keys[5], (D, (HEADS + 2 * KV_HEADS) * HEAD_DIM), D ** -0.5, 0.15625, ((0, 4),))
    out_weight = gaussian(arg_keys[6], (HEADS * HEAD_DIM, D), (D // 32) ** -0.5, 0.875, ((0, 4),))
    norm2_gain = jnp.clip(1.0 + 0.18 * jax.random.normal(arg_keys[7], (D,), jnp.float32), 0.099609375, 1.8984375).astype(jnp.bfloat16)
    router_weight = gaussian(arg_keys[8], (D, EXPERTS), (4 * D) ** -0.5, 0.078125, ((0, 4),))
    gate_weight = gaussian(arg_keys[9], (EXPERTS, D, FF_E), D ** -0.5, 0.15625, ((0, 8), (1, 4)))
    up_weight = gaussian(arg_keys[10], (EXPERTS, D, FF_E), D ** -0.5, 0.15625, ((0, 8), (1, 4)))
    down_weight = gaussian(arg_keys[11], (EXPERTS, FF_E, D), (FF_E // 8) ** -0.5, 0.75, ((0, 8), (2, 4)))
    return dict(layer_input=layer_input, out_cotangent=out_cotangent, parents=parents, routes=routes, norm1_gain=norm1_gain, qkv_weight=qkv_weight, out_weight=out_weight, norm2_gain=norm2_gain, router_weight=router_weight, gate_weight=gate_weight, up_weight=up_weight, down_weight=down_weight)


EPSILON = 1e-06
THETA = 10000.0
NEGATIVE = -1e+30

@jax.custom_vjp
def low(v):
    return lax.optimization_barrier(v.astype(jnp.bfloat16)).astype(jnp.float32)

@jax.custom_vjp
def low_back(v):
    return v

def low_keep(v):
    return (low(v), None)

def low_pass(kept, grad):
    return (grad,)

def back_keep(v):
    return (v, None)

def back_low(kept, grad):
    return (low(grad),)
low.defvjp(low_keep, low_pass)
low_back.defvjp(back_keep, back_low)

def tree_tables(parents, seg_len):
    seg_count = parents.shape[0]
    seg_ids = jnp.arange(seg_count, dtype=jnp.int32)

    def follow(step_index, state_pair):
        pointer, ancestry = state_pair
        landed = pointer[:, None] == seg_ids[None, :]
        ancestry = jnp.maximum(ancestry, landed.astype(jnp.float32))
        pointer = lax.optimization_barrier(jnp.sum(jnp.where(landed, parents[None, :], 0), axis=1)).astype(jnp.int32)
        return (pointer, ancestry)
    start_state = (seg_ids, jnp.zeros((seg_count, seg_count), jnp.float32))
    pointer, ancestry = lax.fori_loop(0, seg_count, follow, start_state)
    depth = lax.optimization_barrier(jnp.sum(ancestry, axis=1)) - 1.0
    row_count = seg_count * seg_len
    token_ids = jnp.arange(row_count, dtype=jnp.int32)
    offsets = (token_ids % seg_len).astype(jnp.float32)
    positions = jnp.repeat(depth, seg_len) * seg_len + offsets
    reach = jnp.repeat(jnp.repeat(ancestry, seg_len, axis=0), seg_len, axis=1)
    allowed = (reach > 0.5) & (token_ids[None, :] <= token_ids[:, None])
    return (allowed, positions)

def rope_tables(positions, head_size):
    half_size = head_size // 2
    frequency = THETA ** (-(jnp.arange(half_size, dtype=jnp.float32) * 2.0) / head_size)
    angles = positions[:, None] * frequency[None, :]
    cosine = jnp.cos(angles)
    sine = jnp.sin(angles)
    return (jnp.concatenate([cosine, cosine], axis=1), jnp.concatenate([sine, sine], axis=1))

def turn_half(values):
    half_size = values.shape[-1] // 2
    return jnp.concatenate([-values[..., half_size:], values[..., :half_size]], axis=-1)

def rotate(values, cosine, sine):
    return values * cosine[:, None, :] + turn_half(values) * sine[:, None, :]

def place_rows(routes, expert_count, capacity):
    token_count, top_count = routes.shape
    flat_routes = routes.reshape(-1)
    hot_table = (flat_routes[:, None] == jnp.arange(expert_count, dtype=jnp.int32)[None, :]).astype(jnp.int32)
    earlier = jnp.cumsum(hot_table, axis=0) - hot_table
    slots = lax.optimization_barrier(jnp.sum(earlier * hot_table, axis=1)).astype(jnp.int32)
    table = jnp.full((expert_count, capacity), token_count * top_count, jnp.int32)
    table = table.at[flat_routes, slots].set(jnp.arange(token_count * top_count, dtype=jnp.int32))
    return (slots.reshape(token_count, top_count), table)

def softly(scores, axis_index):
    highest = lax.optimization_barrier(jnp.max(scores, axis=axis_index, keepdims=True))
    powers = jnp.exp(scores - highest)
    return powers / lax.optimization_barrier(jnp.sum(powers, axis=axis_index, keepdims=True))

def inverse_rms(values):
    return lax.rsqrt(lax.optimization_barrier(jnp.mean(values * values, axis=1, keepdims=True)) + EPSILON)

def reference(layer_input, out_cotangent, parents, routes, norm1_gain, qkv_weight, out_weight, norm2_gain, router_weight, gate_weight, up_weight, down_weight):
    highest = lax.Precision.HIGHEST
    groups = HEADS // KV_HEADS
    query_width = HEADS * HEAD_DIM
    key_width = KV_HEADS * HEAD_DIM
    scaling = HEAD_DIM ** (-0.5)
    expert_count = router_weight.shape[1]
    tree_count = layer_input.shape[0] // TOK_DEV
    tree_parents = parents.reshape(tree_count, SEGS)
    tree_routes = routes.reshape(tree_count, TOK_DEV, TOP)
    slots, tables = jax.vmap(lambda routed: place_rows(routed, expert_count, CAP))(tree_routes)
    owners = tables // TOP
    tree_ids = jnp.arange(tree_count, dtype=jnp.int32)[:, None, None]
    gather_ids = jnp.where(owners < TOK_DEV, tree_ids * TOK_DEV + owners, tree_count * TOK_DEV).astype(jnp.int32)
    gather_ids = jnp.transpose(gather_ids, (1, 0, 2)).reshape(expert_count, tree_count * CAP)
    location = (tree_routes * (tree_count * CAP) + tree_ids * CAP + slots).reshape(tree_count * TOK_DEV, TOP).astype(jnp.int32)

    def forward(activity, gain_one, mixer, projector, gain_two, router, gate_all, up_all, down_all):

        def tree_block(inputs_pair):
            tree_rows, tree_parent = inputs_pair
            allowed, positions = tree_tables(tree_parent, SEG)
            cosine, sine = rope_tables(positions, HEAD_DIM)
            token_count = tree_rows.shape[0]
            hidden_one = low(tree_rows * inverse_rms(tree_rows) * gain_one[None, :])
            mixed = low_back(jnp.dot(hidden_one, mixer, precision=highest))
            query = low(rotate(mixed[:, :query_width].reshape(token_count, HEADS, HEAD_DIM), cosine, sine))
            keys_rot = low(rotate(mixed[:, query_width:query_width + key_width].reshape(token_count, KV_HEADS, HEAD_DIM), cosine, sine))
            values = low(mixed[:, query_width + key_width:].reshape(token_count, KV_HEADS, HEAD_DIM))
            query = query.reshape(token_count, KV_HEADS, groups, HEAD_DIM)
            scores = low_back(jnp.einsum('tkgd,skd->kgts', query, keys_rot, precision=highest) * scaling)
            scores = jnp.where(allowed[None, None], scores, NEGATIVE)
            probs = low(softly(scores, 3))
            attended = jnp.einsum('kgts,skd->tkgd', probs, values, precision=highest).reshape(token_count, query_width)
            attended = low(low_back(attended))
            branch = low_back(jnp.dot(attended, projector, precision=highest))
            return tree_rows + branch
        width = activity.shape[1]
        resid = lax.map(jax.checkpoint(tree_block), (activity.reshape(tree_count, TOK_DEV, width), tree_parents))
        resid = resid.reshape(tree_count * TOK_DEV, width)
        hidden_two = low(resid * inverse_rms(resid) * gain_two[None, :])
        logits = jnp.dot(hidden_two, router, precision=highest)
        gates = softly(jnp.take_along_axis(logits, routes, axis=1), 1)
        padded = jnp.concatenate([hidden_two, jnp.zeros((1, width), jnp.float32)], axis=0)

        def expert_block(inputs_four):
            gate_one, up_one, down_one, row_ids = inputs_four
            taken = low_back(padded[row_ids])
            gate_in = low_back(jnp.dot(taken, gate_one, precision=highest))
            up_in = low_back(jnp.dot(taken, up_one, precision=highest))
            hidden_mid = low(jax.nn.silu(gate_in) * up_in)
            return low(low_back(jnp.dot(hidden_mid, down_one, precision=highest)))
        produced = lax.map(jax.checkpoint(expert_block), (gate_all, up_all, down_all, gather_ids)).reshape(-1, width)
        total = resid
        for pick_index in range(TOP):
            total = total + gates[:, pick_index:pick_index + 1] * produced[location[:, pick_index]]
        return total
    primals = tuple((value.astype(jnp.float32) for value in (layer_input, norm1_gain, qkv_weight, out_weight, norm2_gain, router_weight, gate_weight, up_weight, down_weight)))
    result, pullback = jax.vjp(forward, *primals)
    grads = pullback(out_cotangent.astype(jnp.float32))
    return (result.astype(jnp.bfloat16), grads[0].astype(jnp.bfloat16), grads[1], grads[2], grads[3], grads[4], grads[5], grads[6], grads[7], grads[8])
```

```python
import jax
import jax.numpy as jnp
from jax import lax
from jax.experimental import pallas as pl
from jax.experimental.pallas import tpu as pltpu
from jax.sharding import PartitionSpec as P

HEADS = 24
KV_HEADS = 8
HEAD_DIM = 64
SEG = 128

EPSILON = 1e-06
THETA = 10000.0
NEGATIVE = -1e30

NT = (((1,), (1,)), ((), ()))
NN = (((1,), (0,)), ((), ()))
TN = (((0,), (0,)), ((), ()))
def dot(left, right, dims):
    return lax.dot_general(left, right, dims, preferred_element_type=jnp.float32)

def turned(values):
    lane = lax.broadcasted_iota(jnp.int32, values.shape, 1)
    first = lane % HEAD_DIM < HEAD_DIM // 2
    ahead = pltpu.roll(values, 128 - HEAD_DIM // 2, 1)
    behind = pltpu.roll(values, HEAD_DIM // 2, 1)
    return jnp.where(first, -ahead, behind)


def tree_tables(parents):
    segs = parents.shape[0]
    ids = jnp.arange(segs, dtype=jnp.int32)
    pointer = ids
    ancestry = jnp.zeros((segs, segs), jnp.bool_)
    for _ in range(segs):
        landed = pointer[:, None] == ids[None, :]
        ancestry = ancestry | landed
        pointer = jnp.sum(jnp.where(landed, parents[None, :], 0), axis=1)
    depth = jnp.sum(ancestry.astype(jnp.float32), axis=1) - 1.0
    token_ids = jnp.arange(segs * SEG, dtype=jnp.int32)
    positions = jnp.repeat(depth, SEG) * SEG + (token_ids % SEG).astype(jnp.float32)
    reach = jnp.repeat(jnp.repeat(ancestry.astype(jnp.float32), SEG, axis=0), SEG, axis=1)
    allowed = (reach > 0.5) & (token_ids[None, :] <= token_ids[:, None])
    half = HEAD_DIM // 2
    frequency = THETA ** (-(jnp.arange(half, dtype=jnp.float32) * 2.0) / HEAD_DIM)
    angles = positions[:, None] * frequency[None, :]
    cosine, sine = jnp.cos(angles), jnp.sin(angles)
    return (
        jnp.where(allowed, 0.0, NEGATIVE),
        jnp.concatenate([cosine] * 4, axis=1),
        jnp.concatenate([sine] * 4, axis=1),
    )


def inverse_rms(values):
    return lax.rsqrt(jnp.mean(values * values, axis=1, keepdims=True) + EPSILON)


def swap_core(value):
    count = lax.axis_size("expert")
    return lax.ppermute(value, "expert", [(i, i ^ 1) for i in range(count)])


def next_chip(value):
    count = lax.axis_size("expert")
    return lax.ppermute(value, "expert", [(i, (i + 2) % count) for i in range(count)])


def across(value, mask):
    return lax.ppermute(value, "shard", [(i, i ^ mask) for i in range(4)])


def after(value, *earlier):
    return lax.optimization_barrier((value,) + earlier)[0]


def gather_first(block, on_lanes=False):
    if lax.axis_size("shard") != 4:
        if on_lanes:
            return [lax.all_gather(block, "shard", axis=block.ndim - 1, tiled=True)[None]]
        return [lax.all_gather(block, "shard", axis=0, tiled=False)]
    return [block[None], across(block, 1)[None], across(block, 2)[None]]


def gather_second(pieces, split):
    if len(pieces) == 1:
        return pieces
    axis = split + 1
    half = pieces[1].shape[axis] // 2
    first = lax.slice_in_dim(pieces[2], 0, half, axis=axis)
    last = lax.slice_in_dim(pieces[1], half, 2 * half, axis=axis)
    return pieces + [across(first, 1), across(last, 2)]


def gather_small(value):
    if lax.axis_size("shard") != 4:
        return lax.all_gather(value, "shard", axis=1, tiled=True)
    me = lax.axis_index("shard")
    parts = [value, across(value, 1), across(value, 2), across(value, 3)]
    odd = me % 2 == 1
    parts = [jnp.where(odd, parts[i ^ 1], parts[i]) for i in range(4)]
    high = me >= 2
    parts = [jnp.where(high, parts[i ^ 2], parts[i]) for i in range(4)]
    return jnp.concatenate(parts, axis=1)


def shard_order():
    shards = lax.axis_size("shard")
    me = lax.axis_index("shard")
    core = lax.axis_index("expert") % 2
    if shards != 4:
        return jnp.concatenate([jnp.arange(shards, dtype=jnp.int32), core[None].astype(jnp.int32)])
    return jnp.stack([me, me ^ 1, me ^ 2, me ^ 3, me ^ 3, core]).astype(jnp.int32)


def add_low(*terms):
    total = terms[0].astype(jnp.float32)
    for term in terms[1:]:
        total = total + term.astype(jnp.float32)
    return total.astype(jnp.bfloat16)


def reduce_first(blocks):
    if lax.axis_size("shard") != 4:
        return (lax.psum_scatter(blocks, "shard", scatter_dimension=0, tiled=False),)
    me = lax.axis_index("shard")
    own, beside, above, far = (
        lax.dynamic_index_in_dim(blocks, me ^ r, 0, keepdims=False) for r in range(4)
    )
    half = own.shape[0] // 2
    from_x = across(jnp.concatenate([far[:half], beside[:half]]), 1)
    from_y = across(jnp.concatenate([far[half:], above[half:]]), 2)
    return own, beside[half:], above[:half], from_x, from_y


def reduce_second(state):
    if len(state) == 1:
        return state
    own, beside, above, from_x, from_y = state
    half = own.shape[0] // 2
    last_x = across(add_low(beside, from_y[:half]), 1)
    last_y = across(add_low(above, from_x[:half]), 2)
    return own, from_x[half:], from_y[half:], last_x, last_y


def reduce_last(state, dtype=jnp.bfloat16):
    if len(state) == 1:
        return state[0].astype(dtype)
    own, from_x, from_y, last_x, last_y = (v.astype(jnp.float32) for v in state)
    half = own.shape[0] // 2
    return jnp.concatenate([own[:half] + from_x + last_y, own[half:] + last_x + from_y]).astype(dtype)


def reduce_chips(value):
    count = lax.axis_size("expert")
    mask = 2
    while mask < count:
        value = add_low(value, lax.ppermute(value, "expert", [(i, i ^ mask) for i in range(count)]))
        mask *= 2
    return value


def piece_copies(pieces, order_ref, target, sem, axis, split, base=0, stride=None, window=None):
    copies = []
    slot = 0
    block = pieces[0].shape[1:]
    stride = block[axis] if stride is None else stride
    align = 128 if axis == len(block) - 1 else 16
    for piece in pieces:
        for c in range(piece.shape[0]):
            shape = piece.shape[1:]
            start = [0] * len(shape)
            if slot == 4 and shape[split] < block[split]:
                start[split] = block[split] - shape[split]
            start[axis] = pl.multiple_of(order_ref[slot] * stride + base + start[axis], align)
            index = tuple(pl.ds(first, size) for first, size in zip(start, shape))
            source = piece.at[c]
            if window is not None:
                cols = shape[-1] // 2
                source = source.at[:, window * cols : (window + 1) * cols]
                index = index[:-1] + (slice(None),)
            copies.append(pltpu.make_async_copy(source, target.at[index], sem))
            slot += 1
    return copies


def attend_kernel(count, call, order_ref, group_ref, hidden_ref, cos_ref, sin_ref, bias_ref, *rest):
    mine, other = rest[:count], rest[count : 2 * count]
    att_ref, q_ref, k_ref, v_ref, lse_ref, weight_ref, sems = rest[-7:]
    step = pl.program_id(0)
    first = piece_copies(mine, order_ref, weight_ref.at[0], sems.at[0], 0, 0, window=call)
    second = piece_copies(other, order_ref, weight_ref.at[1], sems.at[1], 0, 0, window=call)

    @pl.when(step == 0)
    def _():
        for copy in first + second:
            copy.start()
        for copy in first:
            copy.wait()

    @pl.when(step == 1)
    def _():
        for copy in second:
            copy.wait()

    hidden = hidden_ref[...]
    cosine, sine = cos_ref[...], sin_ref[...]
    mixed = dot(hidden, weight_ref[step], NN)
    low = jnp.bfloat16
    for p in range(3):
        part = mixed[:, 128 * p : 128 * p + 128]
        q_ref[:, 128 * p : 128 * p + 128] = (part * cosine + turned(part) * sine).astype(low)
    part = mixed[:, 384:512]
    k_ref[...] = (part * cosine + turned(part) * sine).astype(low)
    v_ref[...] = mixed[:, 512:640].astype(low)
    scaling = HEAD_DIM ** (-0.5)
    tokens = hidden.shape[0]
    for seg in range(tokens // SEG):
        rows = pl.ds(seg * SEG, SEG)
        span = (seg + 1) * SEG
        bias = bias_ref[rows, :span]
        outs = []
        logs = []
        for h in range(6):
            kv = h // 3
            keys = k_ref[:span, HEAD_DIM * kv : HEAD_DIM * (kv + 1)]
            vals = v_ref[:span, HEAD_DIM * kv : HEAD_DIM * (kv + 1)]
            query = q_ref[rows, HEAD_DIM * h : HEAD_DIM * (h + 1)]
            scores = dot(query, keys, NT) * scaling + bias
            highest = jnp.max(scores, axis=1, keepdims=True)
            powers = jnp.exp(scores - highest)
            total = jnp.sum(powers, axis=1, keepdims=True)
            probs = (powers * (1.0 / total)).astype(low)
            outs.append(dot(probs, vals, NN))
            logs.append(highest + jnp.log(total))
        att_ref[rows, :] = jnp.concatenate(outs, axis=1).astype(low)
        lse_ref[rows, :] = jnp.concatenate(logs + [logs[-1]] * 2, axis=1)


def attend(hidden, mixer_p, call, order, groups, cosine, sine, bias, kept):
    tokens, width = hidden.shape
    low = jnp.bfloat16
    whole = lambda a: pl.BlockSpec(a.shape, lambda j, o, g: (0, 0))
    anywhere = pl.BlockSpec(memory_space=pl.ANY)
    col = lambda w: pl.BlockSpec((tokens, w), lambda j, o, g: (0, g[j]))
    shape = lambda w: jax.ShapeDtypeStruct((tokens, w), low)
    operands = [order, groups, hidden, cosine, sine, bias, *mixer_p]
    in_specs = [whole(hidden), whole(cosine), whole(sine), whole(bias)]
    in_specs += [anywhere] * len(mixer_p)
    aliases = {}
    if kept is not None:
        aliases = {len(operands) + i: i for i in range(5)}
        operands += list(kept)
        in_specs += [anywhere] * 5
    cols = mixer_p[0].shape[-1] // 2
    return pl.pallas_call(
        lambda *refs: attend_kernel(len(mixer_p) // 2, call, *refs),
        grid_spec=pltpu.PrefetchScalarGridSpec(
            num_scalar_prefetch=2,
            grid=(2,),
            in_specs=in_specs,
            out_specs=[col(384), col(384), col(128), col(128)]
            + [pl.BlockSpec((None, tokens, 8), lambda j, o, g: (g[j], 0, 0))],
            scratch_shapes=[pltpu.VMEM((2, width, cols), low), pltpu.SemaphoreType.DMA((2,))],
        ),
        out_shape=[shape(1536), shape(1536), shape(512), shape(512)]
        + [jax.ShapeDtypeStruct((4, tokens, 8), jnp.float32)],
        input_output_aliases=aliases,
        compiler_params=pltpu.CompilerParams(vmem_limit_bytes=40 * 2**20),
        cost_estimate=pl.CostEstimate(flops=16 * 10**9, bytes_accessed=8 * 10**6, transcendentals=0),
        name="attend",
    )(*operands)


def projector_copies(count, pieces, order_ref, target, sem):
    rows = pieces[0].shape[1]
    slots = order_ref.shape[0] - 1
    core = order_ref[slots]
    copies = piece_copies(pieces[:count], order_ref, target, sem, 0, 0, core * rows, 2 * rows)
    return copies + piece_copies(
        pieces[count:], order_ref, target, sem, 0, 0, (1 - core) * rows, 2 * rows
    )


def attend_back_kernel(mine, counts, call, group_ref, order_ref, branch_ref, hidden_ref, q_ref, k_ref, v_ref, lse_ref, cos_ref, sin_ref, bias_ref, *rest):
    first, second = counts
    pieces, mixer_p = rest[:first], rest[first : first + second]
    wide_ref, input_ref, proj_ref, weight_ref, mixed_ref, grad_ref, dk_ref, dv_ref, sems = rest[first + second :]
    step = pl.program_id(0)
    load = projector_copies(mine, pieces, order_ref, proj_ref, sems.at[0])
    half = second // 2
    more = [
        piece_copies(mixer_p[c * half : (c + 1) * half], order_ref, weight_ref.at[c], sems.at[1 + c], 0, 0, window=call)
        for c in range(2)
    ]

    @pl.when(step == 0)
    def _():
        for copy in load + more[0] + more[1]:
            copy.start()
        for copy in load:
            copy.wait()

    group = group_ref[step]
    low = jnp.bfloat16
    rows = pl.ds(pl.multiple_of(group * 384, 128), 384)
    grad_ref[...] = dot(branch_ref[...], proj_ref[rows, :], NT).astype(low)
    cosine, sine = cos_ref[...], sin_ref[...]
    scaling = HEAD_DIM ** (-0.5)
    tokens = branch_ref.shape[0]
    for seg in reversed(range(tokens // SEG)):
        rows = pl.ds(seg * SEG, SEG)
        span = (seg + 1) * SEG
        bias = bias_ref[rows, :span]
        gqs = []
        gks = []
        gvs = []
        for kv in range(2):
            keys = k_ref[:span, HEAD_DIM * kv : HEAD_DIM * (kv + 1)]
            vals = v_ref[:span, HEAD_DIM * kv : HEAD_DIM * (kv + 1)]
            gscore = []
            probs_all = []
            queries = []
            grads = []
            for h in range(3 * kv, 3 * kv + 3):
                query = q_ref[rows, HEAD_DIM * h : HEAD_DIM * (h + 1)]
                grad = grad_ref[rows, HEAD_DIM * h : HEAD_DIM * (h + 1)]
                scores = dot(query, keys, NT) * scaling + bias
                probs = jnp.exp(scores - lse_ref[rows, h : h + 1])
                gprobs = dot(grad, vals, NT)
                centre = jnp.sum(probs * gprobs, axis=1, keepdims=True)
                gs = (probs * (gprobs - centre)).astype(low)
                gqs.append(dot(gs, keys, NN) * scaling)
                gscore.append(gs)
                probs_all.append(probs.astype(low))
                queries.append(query)
                grads.append(grad)
            gks.append(dot(jnp.concatenate(gscore, 0), jnp.concatenate(queries, 0), TN) * scaling)
            gvs.append(dot(jnp.concatenate(probs_all, 0), jnp.concatenate(grads, 0), TN))
        gq = jnp.concatenate(gqs, axis=1)
        cos_rows, sin_rows = cosine[seg * SEG : span], sine[seg * SEG : span]
        for p in range(3):
            part = gq[:, 128 * p : 128 * p + 128]
            mixed_ref[rows, 128 * p : 128 * p + 128] = (
                part * cos_rows - turned(part * sin_rows)
            ).astype(low)
        gk = jnp.concatenate(gks, axis=1)
        gv = jnp.concatenate(gvs, axis=1)
        if span == tokens:
            dk_ref[...] = gk
            dv_ref[...] = gv
        else:
            dk_ref[:span, :] += gk
            dv_ref[:span, :] += gv
    gk = dk_ref[...]
    mixed_ref[:, 384:512] = (gk * cosine - turned(gk * sine)).astype(low)
    mixed_ref[:, 512:640] = dv_ref[...].astype(low)
    for c in range(2):

        @pl.when(step == c)
        def _():
            for copy in more[c]:
                copy.wait()

    wide_ref[...] = dot(hidden_ref[...], mixed_ref[...], TN).astype(low)
    part = dot(mixed_ref[...], weight_ref[step], NT)

    @pl.when(step == 0)
    def _():
        input_ref[...] = part

    @pl.when(step > 0)
    def _():
        input_ref[...] += part


def attend_back(call, branch, hidden, proj, mixer_p, order, groups, q, k, v, lse, cosine, sine, bias):
    tokens, width = branch.shape
    low = jnp.bfloat16
    whole = lambda a: pl.BlockSpec(a.shape, lambda j, g, o: (0, 0))
    col = lambda w: pl.BlockSpec((tokens, w), lambda j, g, o: (0, g[j]))
    cols = mixer_p[0].shape[-1] // 2
    mine = len(mixer_p) // 2
    return pl.pallas_call(
        lambda *refs: attend_back_kernel(mine, (len(proj), len(mixer_p)), call, *refs),
        grid_spec=pltpu.PrefetchScalarGridSpec(
            num_scalar_prefetch=2,
            grid=(2,),
            in_specs=[whole(branch), whole(hidden), col(384), col(128), col(128)]
            + [pl.BlockSpec((None, tokens, 8), lambda j, g, o: (g[j], 0, 0))]
            + [whole(cosine), whole(sine), whole(bias)]
            + [pl.BlockSpec(memory_space=pl.ANY)] * (len(proj) + len(mixer_p)),
            out_specs=[
                pl.BlockSpec((None, width, cols), lambda j, g, o: (j, 0, 0)),
                pl.BlockSpec((tokens, width), lambda j, g, o: (0, 0)),
            ],
            scratch_shapes=[
                pltpu.VMEM((width, width), low),
                pltpu.VMEM((2, width, cols), low),
                pltpu.VMEM((tokens, cols), low),
                pltpu.VMEM((tokens, 384), low),
                pltpu.VMEM((tokens, 128), jnp.float32),
                pltpu.VMEM((tokens, 128), jnp.float32),
                pltpu.SemaphoreType.DMA((3,)),
            ],
        ),
        out_shape=[
            jax.ShapeDtypeStruct((2, width, cols), low),
            jax.ShapeDtypeStruct((tokens, width), jnp.float32),
        ],
        compiler_params=pltpu.CompilerParams(vmem_limit_bytes=50 * 2**20),
        cost_estimate=pl.CostEstimate(flops=20 * 10**9, bytes_accessed=8 * 10**6, transcendentals=0),
        name="attend_back",
    )(groups, order, branch, hidden, q, k, v, lse, cosine, sine, bias, *proj, *mixer_p)


def project_kernel(mine, count, order_ref, left_ref, *rest):
    pieces = rest[:count]
    out_ref, weight_ref, sem = rest[count:]
    copies = projector_copies(mine, pieces, order_ref, weight_ref, sem)
    for copy in copies:
        copy.start()
    for copy in copies:
        copy.wait()
    out_ref[...] = dot(left_ref[...], weight_ref[...], NN)


def project(left, proj, mine, order):
    tokens, width = left.shape
    return pl.pallas_call(
        lambda *refs: project_kernel(mine, len(proj), *refs),
        grid_spec=pltpu.PrefetchScalarGridSpec(
            num_scalar_prefetch=1,
            grid=(1,),
            in_specs=[pl.BlockSpec((tokens, width), lambda i, o: (0, 0))]
            + [pl.BlockSpec(memory_space=pl.ANY)] * len(proj),
            out_specs=pl.BlockSpec((tokens, width), lambda i, o: (0, 0)),
            scratch_shapes=[pltpu.VMEM((width, width), jnp.bfloat16), pltpu.SemaphoreType.DMA],
        ),
        out_shape=jax.ShapeDtypeStruct((tokens, width), jnp.float32),
        compiler_params=pltpu.CompilerParams(vmem_limit_bytes=40 * 2**20),
        cost_estimate=pl.CostEstimate(flops=5 * 10**9, bytes_accessed=8 * 10**6, transcendentals=0),
        name="project",
    )(order, left, *proj)


TILE = 256


def extra_rows(expert_count):
    return 8 if expert_count <= 24 else 16


def with_table(rows, table):
    tokens, width = rows.shape
    expert_count = table.shape[1]
    extra = extra_rows(expert_count)
    tiles = tokens // TILE
    high = table.astype(jnp.bfloat16)
    rest = (table - high.astype(jnp.float32)).astype(jnp.bfloat16)
    both = jnp.stack([high.T, rest.T], axis=1)
    both = both.reshape(expert_count // extra, extra, 2, tiles, TILE)
    both = jnp.transpose(both, (3, 1, 0, 2, 4)).reshape(tiles, extra, -1)
    both = jnp.pad(both, ((0, 0), (0, 0), (0, width - both.shape[2])))
    return jnp.concatenate([rows.reshape(tiles, TILE, width), both], axis=1).reshape(-1, width)


def table_of(rows, tokens, expert_count):
    extra = extra_rows(expert_count)
    tiles = tokens // TILE
    both = rows.reshape(tiles, TILE + extra, -1)[:, TILE:, : expert_count // extra * 2 * TILE]
    both = both.reshape(tiles, extra, expert_count // extra, 2, TILE)
    return jnp.transpose(jnp.sum(both.astype(jnp.float32), axis=3), (0, 3, 2, 1)).reshape(tokens, -1)


def rows_of(rows, tokens):
    tiles = tokens // TILE
    return rows.reshape(tiles, rows.shape[0] // tiles, -1)[:, :TILE].reshape(tokens, -1)


def expert_kernel(counts, expert_count, order_ref, place_ref, xa_ref, xb_ref, u_ref, *rest):
    pieces, more = counts
    sides_p, downs_p = rest[:pieces], rest[pieces : 2 * pieces]
    rest = rest[2 * pieces + more :]
    (gta_ref, gtb_ref, out_ref, x_ref, mid_ref, sides_ref, ws_ref, wd_ref, sems) = rest
    low = jnp.bfloat16
    extra = extra_rows(expert_count)
    step = pl.program_id(0)
    half = pl.num_programs(0) // 2
    load = piece_copies(sides_p, order_ref, ws_ref, sems.at[0], 1, 0)
    load_down = piece_copies(downs_p, order_ref, wd_ref, sems.at[1], 2, 0)

    @pl.when(step == 0)
    def _():
        for copy in load + load_down:
            copy.start()

    first = step < half
    table = jnp.where(first, xa_ref[TILE:, :], xb_ref[TILE:, :])

    @pl.when(first)
    def _():
        x_ref[...] = xa_ref[:TILE, :]

    @pl.when(jnp.logical_not(first))
    def _():
        x_ref[...] = xb_ref[:TILE, :]

    @pl.when(step == 0)
    def _():
        for copy in load + load_down:
            copy.wait()

    rows, cots = x_ref[...], u_ref[...]
    row = lax.broadcasted_iota(jnp.int32, (extra, 128), 0)
    lane = lax.broadcasted_iota(jnp.int32, (extra, 128), 1)
    expert = place_ref[2] * 2 + lane
    picks = []
    for block in range(expert_count // extra):
        hit = (lane < 2) & (row == expert - block * extra)
        picks.append(jnp.where(hit, 1.0, 0.0).astype(low))
    gates_wide = None
    for block, pick in enumerate(picks):
        for part in range(2):
            at = (2 * block + part) * TILE
            value = dot(table[:, at : at + TILE], pick, TN)
            gates_wide = value if gates_wide is None else gates_wide + value
    out = None
    taken = None
    sums = []
    for l in range(2):
        gates = gates_wide[:, l : l + 1]
        gate_in = dot(rows, ws_ref[2 * l], NN)
        up_in = dot(rows, ws_ref[2 * l + 1], NN)
        back = dot(cots, wd_ref[l], NT)
        sigma = 1.0 / (1.0 + jnp.exp(-gate_in))
        active = gate_in * sigma
        mid = active * up_in
        sums.append(jnp.sum(mid * back, axis=1, keepdims=True))
        mid_low = (mid * gates).astype(low)
        mid_ref[l] = mid_low
        part = dot(mid_low, wd_ref[l], NN)
        out = part if out is None else out + part
        back = back * gates
        grad_gate = (back * up_in * sigma * (1.0 + gate_in * (1.0 - sigma))).astype(low)
        grad_up = (back * active).astype(low)
        sides_ref[2 * l] = grad_gate
        sides_ref[2 * l + 1] = grad_up
        part = dot(grad_gate, ws_ref[2 * l], NT) + dot(grad_up, ws_ref[2 * l + 1], NT)
        taken = part if taken is None else taken + part
    out_ref[...] = out.astype(low)
    taken_low = taken.astype(low)
    wide = lax.broadcasted_iota(jnp.int32, (TILE, 128), 1)
    sums = jnp.where(wide == 0, sums[0], jnp.where(wide == 1, sums[1], 0.0))
    high = sums.astype(low)
    parts = (high, (sums - high.astype(jnp.float32)).astype(low))
    columns = [dot(pick, value, NT).astype(low) for pick in picks for value in parts]
    left = rows.shape[1] - TILE * len(columns)
    if left:
        columns.append(jnp.zeros((extra, left), low))
    columns = jnp.concatenate(columns, axis=1)

    @pl.when(first)
    def _():
        gta_ref[:TILE, :] = taken_low
        gta_ref[TILE:, :] = columns

    @pl.when(jnp.logical_not(first))
    def _():
        gtb_ref[:TILE, :] = taken_low
        gtb_ref[TILE:, :] = columns


def expert_chunk(order, place, xa, xb, cots, sides, downs, expert_count, kept):
    total, width = cots.shape
    devices = lax.axis_size("expert")
    tokens = total // devices
    hidden = sides[0].shape[-1]
    half = tokens // TILE
    steps = 2 * half
    low = jnp.bfloat16
    tall = TILE + extra_rows(expert_count)
    first = pl.BlockSpec((tall, width), lambda i, o, p: (jnp.minimum(i, half - 1), 0))
    second = pl.BlockSpec((tall, width), lambda i, o, p: (jnp.maximum(i - half, 0), 0))
    where = lambda i, p: jnp.where(i < half, p[0] * half + i, p[1] * half + i - half)
    anywhere = pl.BlockSpec(memory_space=pl.ANY)
    big_row = pl.BlockSpec((TILE, width), lambda i, o, p: (where(i, p), 0))
    big = lambda n: pl.BlockSpec((n, TILE, hidden), lambda i, o, p: (0, where(i, p), 0))
    single = jax.ShapeDtypeStruct((half * tall, width), low)
    shapes = [jax.ShapeDtypeStruct((total, width), low)] * 2
    shapes += [jax.ShapeDtypeStruct((n, total, hidden), low) for n in (2, 4)]
    operands = [order, place, xa, xb, cots, *sides, *downs]
    in_specs = [first, second, big_row] + [anywhere] * (2 * len(sides))
    aliases = {}
    more = 0
    if kept is not None:
        more = len(shapes)
        aliases = {len(operands) + i: 2 + i for i in range(more)}
        operands += list(kept)
        in_specs += [anywhere] * more
    res = pl.pallas_call(
        lambda *refs: expert_kernel((len(sides), more), expert_count, *refs),
        grid_spec=pltpu.PrefetchScalarGridSpec(
            num_scalar_prefetch=2,
            grid=(steps,),
            in_specs=in_specs,
            out_specs=[first, second, big_row, big_row, big(2), big(4)],
            scratch_shapes=[
                pltpu.VMEM((4, width, hidden), low),
                pltpu.VMEM((2, hidden, width), low),
                pltpu.SemaphoreType.DMA((2,)),
            ],
        ),
        out_shape=[single] * 2 + shapes,
        input_output_aliases=aliases,
        compiler_params=pltpu.CompilerParams(vmem_limit_bytes=58 * 2**20),
        cost_estimate=pl.CostEstimate(flops=27 * 10**9, bytes_accessed=8 * 10**6, transcendentals=0),
        name="expert_chunk",
    )(*operands)
    return res[:2], res[2:]


def wide_grad_kernel(on_rows, left_ref, right_ref, out_ref, acc_ref):
    step = pl.program_id(1)
    value = dot(left_ref[...], right_ref[...], TN)

    @pl.when(step == 0)
    def _():
        acc_ref[...] = value

    @pl.when(step > 0)
    def _():
        acc_ref[...] += value

    @pl.when(step == pl.num_programs(1) - 1)
    def _():
        rows, cols = out_ref.shape[-2:]
        for j in range(out_ref.shape[0]):
            if on_rows:
                part = acc_ref[j * rows : (j + 1) * rows, :]
            else:
                part = acc_ref[:, j * cols : (j + 1) * cols]
            out_ref[j] = part.astype(out_ref.dtype)


def weight_grad(left, right, parts, on_rows):
    count = left.shape[0] if left.ndim == 3 else right.shape[0]
    total, size_m = left.shape[-2:]
    size_n = right.shape[-1]
    block = 1024
    spec = lambda a: (
        pl.BlockSpec((None, block, a.shape[-1]), lambda l, k: (l, k, 0))
        if a.ndim == 3
        else pl.BlockSpec((block, a.shape[-1]), lambda l, k: (k, 0))
    )
    shape = (size_m // parts, size_n) if on_rows else (size_m, size_n // parts)
    return pl.pallas_call(
        lambda *refs: wide_grad_kernel(on_rows, *refs),
        grid=(count, total // block),
        in_specs=[spec(left), spec(right)],
        out_specs=pl.BlockSpec((parts, None) + shape, lambda l, k: (0, l, 0, 0)),
        out_shape=jax.ShapeDtypeStruct((parts, count) + shape, jnp.bfloat16),
        scratch_shapes=[pltpu.VMEM((size_m, size_n), jnp.float32)],
        compiler_params=pltpu.CompilerParams(vmem_limit_bytes=48 * 2**20),
        cost_estimate=pl.CostEstimate(flops=20 * 10**9, bytes_accessed=8 * 10**6, transcendentals=0),
        name="weight_grad",
    )(left, right)


def per_device(
    layer_input,
    out_cotangent,
    parents,
    routes,
    norm1_gain,
    qkv_weight,
    out_weight,
    norm2_gain,
    router_weight,
    gate_weight,
    up_weight,
    down_weight,
):
    low = jnp.bfloat16
    shards = lax.axis_size("shard")
    tokens, width = layer_input.shape
    expert_count = router_weight.shape[1]
    local_count = gate_weight.shape[0]
    chips = lax.axis_size("expert") // 2
    me = lax.axis_index("expert")
    core = me % 2
    order = shard_order()
    queries = HEADS * HEAD_DIM

    by_group = [
        jnp.concatenate(
            [
                qkv_weight[:, 384 * g : 384 * (g + 1)],
                qkv_weight[:, queries + 128 * g : queries + 128 * (g + 1)],
                qkv_weight[:, queries + 512 + 128 * g : queries + 512 + 128 * (g + 1)],
            ],
            axis=1,
        )
        for g in range(4)
    ]
    half_columns = lambda g, h: jnp.concatenate([by_group[g], by_group[h]], axis=1)
    block = jnp.where(core == 0, half_columns(0, 2), half_columns(1, 3))
    small = jnp.concatenate([router_weight, norm1_gain[:, None], norm2_gain[:, None]], axis=1).T
    small = gather_small(small)
    mixer_first = gather_first(block)
    mine = gather_second(mixer_first, 0)
    mixer_p = mine + [swap_core(p) for p in mine]
    router = small[:expert_count].T
    gain_one = small[expert_count].astype(jnp.float32)[None, :]
    gain_two = small[expert_count + 1].astype(jnp.float32)[None, :]
    block = lax.dynamic_slice_in_dim(out_weight, core * (out_weight.shape[0] // 2), out_weight.shape[0] // 2, 0)
    project_first = gather_first(after(block, *mine))
    sides = jnp.stack([gate_weight, up_weight], axis=1).reshape(4, -1, gate_weight.shape[2])
    sides_first = gather_first(after(sides, *mine))

    cots = lax.all_gather(out_cotangent, "expert", axis=0, tiled=True)

    bias, cosine, sine = tree_tables(parents)
    activity = layer_input.astype(jnp.float32)
    scale_one = inverse_rms(activity)
    normed_one = activity * scale_one
    hidden_one = (normed_one * gain_one).astype(low)
    saved = None
    groups = []
    for call in range(2):
        groups.append(jnp.stack([2 * call + core, 2 * call + 1 - core]).astype(jnp.int32))
        saved = attend(hidden_one, mixer_p, call, order, groups[call], cosine, sine, bias, saved)
        if call == 0:
            project_first, saved = lax.optimization_barrier((project_first, saved))
            proj = gather_second(project_first, 0)
            near = swap_core(jnp.concatenate(proj[:3], axis=0))
    proj, near, sides_first, saved = lax.optimization_barrier((proj, near, sides_first, saved))
    far = [swap_core(p) for p in proj[3:]]
    sides_p = gather_second(sides_first, 0)
    downs_first = gather_first(after(down_weight, *far), True)
    proj = proj + [near] + far
    attended, query, keys, values, log_total = saved
    resid = activity + project(attended, proj, len(mixer_p) // 2, order)
    scale_two = inverse_rms(resid)
    normed_two = resid * scale_two
    hidden_two = (normed_two * gain_two).astype(low)
    logits = jnp.dot(hidden_two, router, preferred_element_type=jnp.float32)
    routed = jnp.any(
        routes[:, :, None] == jnp.arange(expert_count, dtype=jnp.int32)[None, None, :], axis=1
    )
    masked = jnp.where(routed, logits, NEGATIVE)
    powers = jnp.exp(masked - jnp.max(masked, axis=1, keepdims=True))
    gates = powers / jnp.sum(powers, axis=1, keepdims=True)
    upstream = out_cotangent.astype(jnp.float32)

    downs_p = gather_second(downs_first, 0)
    rows = [with_table(hidden_two, gates)]
    rows.append(next_chip(rows[0]))
    beside = swap_core(rows[0])
    rows[0], rows[1], beside = lax.optimization_barrier((rows[0], rows[1], beside))
    kept = total = None
    for step in range(chips):
        ahead = next_chip(rows[step + 1]) if step + 2 < chips else None
        beside_next = swap_core(rows[step + 1]) if step + 1 < chips else None
        here = rows[step]
        if step > 1:
            here, total = lax.optimization_barrier((here, total))
        sent = next_chip(total) if step > 1 else None
        place = jnp.stack([(me - 2 * step) % (2 * chips), (me - 2 * step) % (2 * chips) ^ 1, me])
        parts, kept = expert_chunk(
            order, place.astype(jnp.int32), here, beside, cots, sides_p, downs_p, expert_count, kept
        )
        parts, kept, ahead, beside, sent = lax.optimization_barrier((parts, kept, ahead, beside_next, sent))
        if ahead is not None:
            rows.append(ahead)
        pair = (parts[0], swap_core(parts[1]))
        if step == 0:
            last = pair
        else:
            total = add_low(*pair, *(() if sent is None else (sent,)))
    out_all, all_rows, all_mid, all_sides = kept
    all_rows, total = lax.optimization_barrier((all_rows, total))
    sent = next_chip(total)
    wide_sides = weight_grad(all_rows, all_sides, shards, True)
    sent, wide_sides = lax.optimization_barrier((sent, wide_sides))
    sides_state = reduce_first(wide_sides)
    final = sum(v.astype(jnp.float32) for v in (*last, sent))
    grad_hidden_two = rows_of(final, tokens)
    grad_gates = table_of(final, tokens, expert_count)
    branch_out = lax.psum_scatter(after(out_all, final), "expert", scatter_dimension=0, tiled=True)

    mean_gate = jnp.sum(gates * grad_gates, axis=1, keepdims=True)
    grad_logits = gates * (grad_gates - mean_gate)
    grad_hidden_two = grad_hidden_two + jnp.dot(
        grad_logits, router.astype(jnp.float32).T, precision=lax.Precision.HIGHEST
    )
    grad_router = jnp.dot(
        hidden_two.astype(jnp.float32).T, grad_logits, precision=lax.Precision.HIGHEST
    )
    grad_gain_two = jnp.sum(grad_hidden_two * normed_two, axis=0)
    grad_normed_two = grad_hidden_two * gain_two
    grad_resid = upstream + scale_two * (
        grad_normed_two - normed_two * jnp.mean(grad_normed_two * normed_two, axis=1, keepdims=True)
    )
    grad_branch = grad_resid.astype(low)

    def spread_sum(blocks):
        return reduce_chips(reduce_last(reduce_second(reduce_first(blocks))))

    grad_projector = jnp.dot(attended.T, grad_branch, preferred_element_type=jnp.float32).astype(low)
    halves = grad_projector.reshape(shards, 2, -1, width)
    mine = lax.dynamic_index_in_dim(halves, core, 1, keepdims=False)
    other = lax.dynamic_index_in_dim(halves, 1 - core, 1, keepdims=False)
    half_projector = (mine, swap_core(other))

    def small_sum(value):
        value = add_low(value, swap_core(value))
        if shards == 4:
            value = add_low(value, across(value, 1))
            value = add_low(value, across(value, 2))
        else:
            value = lax.psum(value, "shard")
        value = reduce_chips(value)
        size = width // shards
        return lax.dynamic_slice_in_dim(value, lax.axis_index("shard") * size, size, 1).astype(jnp.float32)

    first_small = jnp.concatenate([grad_router, grad_gain_two[:, None]], axis=1).T.astype(low)

    finals = []
    parts = []
    for call in range(2):
        wide, part = attend_back(
            call, grad_branch, hidden_one, proj, mixer_p, order, groups[call],
            query, keys, values, log_total, cosine, sine, bias,
        )
        parts.append(part)
        if call == 0:
            grad_branch, wide, sides_state, first_small, half_projector = lax.optimization_barrier(
                (grad_branch, wide, sides_state, first_small, half_projector)
            )
            sides_state = reduce_second(sides_state)
        wide = wide.reshape(2, shards, -1, wide.shape[-1])
        finals.append((wide[0], swap_core(wide[1])))
    parts, finals[0], sides_state, all_mid = lax.optimization_barrier((parts, finals[0], sides_state, all_mid))
    wide_down = weight_grad(all_mid, cots, shards, False)
    down_state = reduce_second(reduce_first(wide_down))
    finals = [spread_sum(add_low(*v)) for v in finals]
    finals = [(v, swap_core(v)) for v in finals]
    grad_hidden_one = parts[0] + parts[1]
    first_small = small_sum(first_small)
    mine = spread_sum(add_low(*half_projector))
    other = swap_core(mine)
    grad_projector = jnp.where(
        core == 0, jnp.concatenate([mine, other]), jnp.concatenate([other, mine])
    ).astype(jnp.float32)
    grad_sides = reduce_last(sides_state, jnp.float32)
    grad_sides = grad_sides.reshape(2, 2, *grad_sides.shape[1:])
    grad_gate, grad_up = grad_sides[:, 0], grad_sides[:, 1]
    grad_down = reduce_last(down_state, jnp.float32)
    output = (resid + after(branch_out, wide_down).astype(jnp.float32)).astype(low)
    grad_gain_one = jnp.sum(grad_hidden_one * normed_one, axis=0)
    grad_normed_one = grad_hidden_one * gain_one
    grad_input = grad_resid + scale_one * (
        grad_normed_one - normed_one * jnp.mean(grad_normed_one * normed_one, axis=1, keepdims=True)
    )
    last_small = small_sum(grad_gain_one[None].astype(low))
    ordered = []
    for mine, other in finals:
        ordered.append(jnp.where(core == 0, mine, other))
        ordered.append(jnp.where(core == 0, other, mine))
    grad_mixer = jnp.concatenate(
        [g[:, :384] for g in ordered] + [g[:, 384:512] for g in ordered] + [g[:, 512:] for g in ordered],
        axis=1,
    ).astype(jnp.float32)
    return (
        output,
        grad_input.astype(low),
        last_small[0],
        grad_mixer,
        grad_projector,
        first_small[expert_count],
        first_small[:expert_count].T,
        grad_gate,
        grad_up,
        grad_down,
    )


def solution(mesh):
    return jax.shard_map(
        per_device,
        mesh=mesh,
        in_specs=(
            P(("expert", "shard"), None),
            P(("expert", "shard"), None),
            P(("expert", "shard")),
            P(("expert", "shard"), None),
            P("shard"),
            P("shard", None),
            P("shard", None),
            P("shard"),
            P("shard", None),
            P("expert", "shard", None),
            P("expert", "shard", None),
            P("expert", None, "shard"),
        ),
        out_specs=(
            P(("expert", "shard"), None),
            P(("expert", "shard"), None),
            P("shard"),
            P("shard", None),
            P("shard", None),
            P("shard"),
            P("shard", None),
            P("expert", "shard", None),
            P("expert", "shard", None),
            P("expert", None, "shard"),
        ),
        check_vma=False,
    )
```

```python
import jax
import jax.numpy as jnp
from jax import lax
from jax.experimental import pallas as pl
from jax.experimental.pallas import tpu as pltpu
from jax.sharding import PartitionSpec as P

HEADS = 24
KV_HEADS = 8
HEAD_DIM = 64
SEG = 128

EPSILON = 1e-06
THETA = 10000.0
NEGATIVE = -1e30

NT = (((1,), (1,)), ((), ()))
NN = (((1,), (0,)), ((), ()))
TN = (((0,), (0,)), ((), ()))
def dot(left, right, dims):
    return lax.dot_general(left, right, dims, preferred_element_type=jnp.float32)

def turned(values):
    lane = lax.broadcasted_iota(jnp.int32, values.shape, 1)
    first = lane % HEAD_DIM < HEAD_DIM // 2
    ahead = pltpu.roll(values, 128 - HEAD_DIM // 2, 1)
    behind = pltpu.roll(values, HEAD_DIM // 2, 1)
    return jnp.where(first, -ahead, behind)


def tree_tables(parents):
    segs = parents.shape[0]
    ids = jnp.arange(segs, dtype=jnp.int32)
    pointer = ids
    ancestry = jnp.zeros((segs, segs), jnp.bool_)
    for _ in range(segs):
        landed = pointer[:, None] == ids[None, :]
        ancestry = ancestry | landed
        pointer = jnp.sum(jnp.where(landed, parents[None, :], 0), axis=1)
    depth = jnp.sum(ancestry.astype(jnp.float32), axis=1) - 1.0
    token_ids = jnp.arange(segs * SEG, dtype=jnp.int32)
    positions = jnp.repeat(depth, SEG) * SEG + (token_ids % SEG).astype(jnp.float32)
    reach = jnp.repeat(jnp.repeat(ancestry.astype(jnp.float32), SEG, axis=0), SEG, axis=1)
    allowed = (reach > 0.5) & (token_ids[None, :] <= token_ids[:, None])
    half = HEAD_DIM // 2
    frequency = THETA ** (-(jnp.arange(half, dtype=jnp.float32) * 2.0) / HEAD_DIM)
    angles = positions[:, None] * frequency[None, :]
    cosine, sine = jnp.cos(angles), jnp.sin(angles)
    return (
        jnp.where(allowed, 0.0, NEGATIVE),
        jnp.concatenate([cosine] * 4, axis=1),
        jnp.concatenate([sine] * 4, axis=1),
    )


def inverse_rms(values):
    return lax.rsqrt(jnp.mean(values * values, axis=1, keepdims=True) + EPSILON)


def swap_core(value):
    count = lax.axis_size("expert")
    return lax.ppermute(value, "expert", [(i, i ^ 1) for i in range(count)])


def next_chip(value):
    count = lax.axis_size("expert")
    return lax.ppermute(value, "expert", [(i, (i + 2) % count) for i in range(count)])


def across(value, mask):
    return lax.ppermute(value, "shard", [(i, i ^ mask) for i in range(4)])


def after(value, *earlier):
    return lax.optimization_barrier((value,) + earlier)[0]


def gather_first(block, on_lanes=False):
    if lax.axis_size("shard") != 4:
        if on_lanes:
            return [lax.all_gather(block, "shard", axis=block.ndim - 1, tiled=True)[None]]
        return [lax.all_gather(block, "shard", axis=0, tiled=False)]
    return [block[None], across(block, 1)[None], across(block, 2)[None]]


def gather_second(pieces, split):
    if len(pieces) == 1:
        return pieces
    axis = split + 1
    half = pieces[1].shape[axis] // 2
    first = lax.slice_in_dim(pieces[2], 0, half, axis=axis)
    last = lax.slice_in_dim(pieces[1], half, 2 * half, axis=axis)
    return pieces + [across(first, 1), across(last, 2)]


def gather_small(value):
    if lax.axis_size("shard") != 4:
        return lax.all_gather(value, "shard", axis=1, tiled=True)
    me = lax.axis_index("shard")
    parts = [value, across(value, 1), across(value, 2), across(value, 3)]
    odd = me % 2 == 1
    parts = [jnp.where(odd, parts[i ^ 1], parts[i]) for i in range(4)]
    high = me >= 2
    parts = [jnp.where(high, parts[i ^ 2], parts[i]) for i in range(4)]
    return jnp.concatenate(parts, axis=1)


def shard_order():
    shards = lax.axis_size("shard")
    me = lax.axis_index("shard")
    core = lax.axis_index("expert") % 2
    if shards != 4:
        return jnp.concatenate([jnp.arange(shards, dtype=jnp.int32), core[None].astype(jnp.int32)])
    return jnp.stack([me, me ^ 1, me ^ 2, me ^ 3, me ^ 3, core]).astype(jnp.int32)


def add_low(*terms):
    total = terms[0].astype(jnp.float32)
    for term in terms[1:]:
        total = total + term.astype(jnp.float32)
    return total.astype(jnp.bfloat16)


def reduce_first(blocks):
    if lax.axis_size("shard") != 4:
        return (lax.psum_scatter(blocks, "shard", scatter_dimension=0, tiled=False),)
    me = lax.axis_index("shard")
    own, beside, above, far = (
        lax.dynamic_index_in_dim(blocks, me ^ r, 0, keepdims=False) for r in range(4)
    )
    half = own.shape[0] // 2
    from_x = across(jnp.concatenate([far[:half], beside[:half]]), 1)
    from_y = across(jnp.concatenate([far[half:], above[half:]]), 2)
    return own, beside[half:], above[:half], from_x, from_y


def reduce_second(state):
    if len(state) == 1:
        return state
    own, beside, above, from_x, from_y = state
    half = own.shape[0] // 2
    last_x = across(add_low(beside, from_y[:half]), 1)
    last_y = across(add_low(above, from_x[:half]), 2)
    return own, from_x, from_y, last_x, last_y


def reduce_last(state, dtype=jnp.bfloat16):
    if len(state) == 1:
        return state[0].astype(dtype)
    own, from_x, from_y, last_x, last_y = (v.astype(jnp.float32) for v in state)
    half = own.shape[0] // 2
    low_half, high_half = own[:half] + from_x[half:] + last_y, own[half:] + last_x + from_y[half:]
    return jnp.concatenate([low_half, high_half]).astype(dtype)


def reduce_chips(value):
    count = lax.axis_size("expert")
    me = lax.axis_index("expert")
    masks = [1 << i for i in range(1, count.bit_length() - 1)]
    swap = lambda v, mask: lax.ppermute(v, "expert", [(i, i ^ mask) for i in range(count)])
    for mask in masks:
        half = value.shape[0] // 2
        upper = (me & mask) != 0
        keep = jnp.where(upper, value[half:], value[:half])
        send = jnp.where(upper, value[:half], value[half:])
        value = add_low(keep, swap(send, mask))
    for mask in reversed(masks):
        other = swap(value, mask)
        upper = (me & mask) != 0
        value = jnp.concatenate([jnp.where(upper, other, value), jnp.where(upper, value, other)])
    return value


def piece_copies(pieces, order_ref, target, sem, axis, split, base=0, stride=None, window=None):
    copies = []
    slot = 0
    block = pieces[0].shape[1:]
    stride = block[axis] if stride is None else stride
    align = 128 if axis == len(block) - 1 else 16
    for piece in pieces:
        for c in range(piece.shape[0]):
            shape = piece.shape[1:]
            start = [0] * len(shape)
            if slot == 4 and shape[split] < block[split]:
                start[split] = block[split] - shape[split]
            start[axis] = pl.multiple_of(order_ref[slot] * stride + base + start[axis], align)
            index = tuple(pl.ds(first, size) for first, size in zip(start, shape))
            source = piece.at[c]
            if window is not None:
                cols = shape[-1] // 2
                source = source.at[:, window * cols : (window + 1) * cols]
                index = index[:-1] + (slice(None),)
            copies.append(pltpu.make_async_copy(source, target.at[index], sem))
            slot += 1
    return copies


def attend_kernel(count, call, order_ref, group_ref, hidden_ref, cos_ref, sin_ref, bias_ref, *rest):
    mine, other = rest[:count], rest[count : 2 * count]
    att_ref, q_ref, k_ref, v_ref, lse_ref, weight_ref, sems = rest[-7:]
    step = pl.program_id(0)
    first = piece_copies(mine, order_ref, weight_ref.at[0], sems.at[0], 0, 0, window=call)
    second = piece_copies(other, order_ref, weight_ref.at[1], sems.at[1], 0, 0, window=call)

    @pl.when(step == 0)
    def _():
        for copy in first + second:
            copy.start()
        for copy in first:
            copy.wait()

    @pl.when(step == 1)
    def _():
        for copy in second:
            copy.wait()

    hidden = hidden_ref[...]
    cosine, sine = cos_ref[...], sin_ref[...]
    mixed = dot(hidden, weight_ref[step], NN)
    low = jnp.bfloat16
    scaling = HEAD_DIM ** (-0.5)
    for p in range(3):
        part = mixed[:, 128 * p : 128 * p + 128]
        turned_part = (part * cosine + turned(part) * sine).astype(low)
        q_ref[:, 128 * p : 128 * p + 128] = turned_part * scaling
    part = mixed[:, 384:512]
    k_ref[...] = (part * cosine + turned(part) * sine).astype(low)
    v_ref[...] = mixed[:, 512:640].astype(low)
    tokens = hidden.shape[0]
    for seg in range(tokens // SEG):
        rows = pl.ds(seg * SEG, SEG)
        span = (seg + 1) * SEG
        bias = bias_ref[rows, :span]
        keys = [k_ref[:span, HEAD_DIM * kv : HEAD_DIM * (kv + 1)] for kv in range(2)]
        vals = [v_ref[:span, HEAD_DIM * kv : HEAD_DIM * (kv + 1)] for kv in range(2)]
        queries = [q_ref[rows, HEAD_DIM * h : HEAD_DIM * (h + 1)] for h in range(6)]
        scores = [dot(queries[h], keys[h // 3], NT) + bias for h in range(6)]
        highest = [jnp.max(v, axis=1, keepdims=True) for v in scores]
        powers = [jnp.exp(v - m) for v, m in zip(scores, highest)]
        totals = [jnp.sum(v, axis=1, keepdims=True) for v in powers]
        probs = [(v * (1.0 / t)).astype(low) for v, t in zip(powers, totals)]
        outs = [dot(v, vals[h // 3], NN) for h, v in enumerate(probs)]
        logs = [m + jnp.log(t) for m, t in zip(highest, totals)]
        att_ref[rows, :] = jnp.concatenate(outs, axis=1).astype(low)
        lse_ref[rows, :] = jnp.concatenate(logs + [logs[-1]] * 2, axis=1)


def attend(hidden, mixer_p, call, order, groups, cosine, sine, bias, kept):
    tokens, width = hidden.shape
    low = jnp.bfloat16
    whole = lambda a: pl.BlockSpec(a.shape, lambda j, o, g: (0, 0))
    anywhere = pl.BlockSpec(memory_space=pltpu.HBM)
    col = lambda w: pl.BlockSpec((tokens, w), lambda j, o, g: (0, g[j]))
    shape = lambda w: pltpu.HBM((tokens, w), low)
    operands = [order, groups, hidden, cosine, sine, bias, *mixer_p]
    in_specs = [whole(hidden), whole(cosine), whole(sine), whole(bias)]
    in_specs += [anywhere] * len(mixer_p)
    aliases = {}
    if kept is not None:
        aliases = {len(operands) + i: i for i in range(5)}
        operands += list(kept)
        in_specs += [anywhere] * 5
    cols = mixer_p[0].shape[-1] // 2
    return pl.pallas_call(
        lambda *refs: attend_kernel(len(mixer_p) // 2, call, *refs),
        grid_spec=pltpu.PrefetchScalarGridSpec(
            num_scalar_prefetch=2,
            grid=(2,),
            in_specs=in_specs,
            out_specs=[col(384), col(384), col(128), col(128)]
            + [pl.BlockSpec((None, tokens, 8), lambda j, o, g: (g[j], 0, 0))],
            scratch_shapes=[pltpu.VMEM((2, width, cols), low), pltpu.SemaphoreType.DMA((2,))],
        ),
        out_shape=[shape(1536), shape(1536), shape(512), shape(512)]
        + [pltpu.HBM((4, tokens, 8), jnp.float32)],
        input_output_aliases=aliases,
        compiler_params=pltpu.CompilerParams(vmem_limit_bytes=40 * 2**20),
        cost_estimate=pl.CostEstimate(flops=48 * 10**9, bytes_accessed=8 * 10**6, transcendentals=0),
        name="attend",
    )(*operands)


def projector_copies(count, pieces, order_ref, target, sem):
    rows = pieces[0].shape[1]
    slots = order_ref.shape[0] - 1
    core = order_ref[slots]
    copies = piece_copies(pieces[:count], order_ref, target, sem, 0, 0, core * rows, 2 * rows)
    return copies + piece_copies(
        pieces[count:], order_ref, target, sem, 0, 0, (1 - core) * rows, 2 * rows
    )


def row_to_column(row, lane):
    low = jnp.bfloat16
    pick = (lax.broadcasted_iota(jnp.int32, (8, 128), 1) == lane) & (
        lax.broadcasted_iota(jnp.int32, (8, 128), 0) == 0
    )
    pick = pick.astype(jnp.float32).astype(low)
    rows = jnp.broadcast_to(row, (8, row.shape[1]))
    high = rows.astype(low)
    rest = (rows - high.astype(jnp.float32)).astype(low)
    return (dot(high, pick, TN) + dot(rest, pick, TN)).astype(low)


def attend_back_kernel(mine, counts, call, group_ref, order_ref, branch_ref, hidden_ref, q_ref, k_ref, v_ref, lse_ref, cos_ref, sin_ref, bias_ref, *rest):
    first, second = counts
    pieces, mixer_p = rest[:first], rest[first : first + second]
    rest = rest[first + second :]
    if call:
        part_ref, x_ref, resid_ref, gain_ref = rest[:4]
        rest = rest[4:]
    wide_refs, input_ref = rest[:2], rest[2]
    proj_ref, weight_ref, mixed_ref, grad_ref, dk_ref, dv_ref, total_ref, sems = rest[3:]
    step = pl.program_id(0)
    load = projector_copies(mine, pieces, order_ref, proj_ref, sems.at[0])
    half = second // 2
    more = [
        piece_copies(mixer_p[c * half : (c + 1) * half], order_ref, weight_ref.at[c], sems.at[1 + c], 0, 0, window=call)
        for c in range(2)
    ]

    @pl.when(step == 0)
    def _():
        for copy in load + more[0] + more[1]:
            copy.start()
        for copy in load:
            copy.wait()

    group = group_ref[step]
    low = jnp.bfloat16
    rows = pl.ds(pl.multiple_of(group * 384, 128), 384)
    grad_ref[...] = dot(branch_ref[...], proj_ref[rows, :], NT).astype(low)
    cosine, sine = cos_ref[...], sin_ref[...]
    scaling = HEAD_DIM ** (-0.5)
    tokens = branch_ref.shape[0]
    for seg in reversed(range(tokens // SEG)):
        rows = pl.ds(seg * SEG, SEG)
        span = (seg + 1) * SEG
        bias = bias_ref[rows, :span]
        part = lambda ref, r, h: ref[r, HEAD_DIM * h : HEAD_DIM * (h + 1)]
        keys = [part(k_ref, pl.ds(0, span), kv) for kv in range(2)]
        vals = [part(v_ref, pl.ds(0, span), kv) for kv in range(2)]
        queries = [part(q_ref, rows, h) for h in range(6)]
        grads = [part(grad_ref, rows, h) for h in range(6)]
        scores = [dot(queries[h], keys[h // 3], NT) + bias for h in range(6)]
        gprobs = [dot(grads[h], vals[h // 3], NT) for h in range(6)]
        probs = [jnp.exp(v - lse_ref[rows, h : h + 1]) for h, v in enumerate(scores)]
        centres = [jnp.sum(p * g, axis=1, keepdims=True) for p, g in zip(probs, gprobs)]
        gscore = [(p * (g - c)).astype(low) for p, g, c in zip(probs, gprobs, centres)]
        probs = [p.astype(low) for p in probs]
        gqs = [dot(v, keys[h // 3], NN) * scaling for h, v in enumerate(gscore)]
        three = lambda values, kv: jnp.concatenate(values[3 * kv : 3 * kv + 3], 0)
        gks = [dot(three(gscore, kv), three(queries, kv), TN) for kv in range(2)]
        gvs = [dot(three(probs, kv), three(grads, kv), TN) for kv in range(2)]
        gq = jnp.concatenate(gqs, axis=1)
        cos_rows, sin_rows = cosine[seg * SEG : span], sine[seg * SEG : span]
        for p in range(3):
            part = gq[:, 128 * p : 128 * p + 128]
            mixed_ref[rows, 128 * p : 128 * p + 128] = (
                part * cos_rows - turned(part * sin_rows)
            ).astype(low)
        gk = jnp.concatenate(gks, axis=1)
        gv = jnp.concatenate(gvs, axis=1)
        if span == tokens:
            dk_ref[...] = gk
            dv_ref[...] = gv
        else:
            dk_ref[:span, :] += gk
            dv_ref[:span, :] += gv
    gk = dk_ref[...]
    mixed_ref[:, 384:512] = (gk * cosine - turned(gk * sine)).astype(low)
    mixed_ref[:, 512:640] = dv_ref[...].astype(low)
    for c in range(2):

        @pl.when(step == c)
        def _():
            for copy in more[c]:
                copy.wait()

    wide = dot(hidden_ref[...], mixed_ref[...], TN).astype(low)
    part = dot(mixed_ref[...], weight_ref[step], NT)
    for c in range(2):

        @pl.when(step == c)
        def _():
            wide_refs[c][:, :640] = wide

    if not call:

        @pl.when(step == 0)
        def _():
            input_ref[...] = part

        @pl.when(step > 0)
        def _():
            input_ref[...] += part

        return

    @pl.when(step == 0)
    def _():
        total_ref[...] = part + part_ref[...]

    @pl.when(step > 0)
    def _():
        value = x_ref[...].astype(jnp.float32)
        scale = lax.rsqrt(jnp.mean(value * value, axis=1, keepdims=True) + EPSILON)
        normed = value * scale
        grad = total_ref[...] + part
        product = grad * normed
        gains = row_to_column(jnp.sum(product, axis=0, keepdims=True), 0)
        for ref in wide_refs:
            ref[:, 640:] = gains
        grad = grad * gain_ref[...]
        mean = jnp.mean(grad * normed, axis=1, keepdims=True)
        input_ref[...] = (resid_ref[...] + scale * (grad - normed * mean)).astype(low)


def attend_back(call, branch, hidden, proj, mixer_p, order, groups, q, k, v, lse, cosine, sine, bias, *more):
    tokens, width = branch.shape
    low = jnp.bfloat16
    whole = lambda a: pl.BlockSpec(a.shape, lambda j, g, o: (0, 0))
    col = lambda w: pl.BlockSpec((tokens, w), lambda j, g, o: (0, g[j]))
    cols = mixer_p[0].shape[-1] // 2
    mine = len(mixer_p) // 2
    wide = jax.ShapeDtypeStruct((width, cols + 128 * call), low)
    given = jax.ShapeDtypeStruct((tokens, width), low if call else jnp.float32)
    return pl.pallas_call(
        lambda *refs: attend_back_kernel(mine, (len(proj), len(mixer_p)), call, *refs),
        grid_spec=pltpu.PrefetchScalarGridSpec(
            num_scalar_prefetch=2,
            grid=(2,),
            in_specs=[whole(branch), whole(hidden), col(384), col(128), col(128)]
            + [pl.BlockSpec((None, tokens, 8), lambda j, g, o: (g[j], 0, 0))]
            + [whole(cosine), whole(sine), whole(bias)]
            + [pl.BlockSpec(memory_space=pltpu.HBM)] * (len(proj) + len(mixer_p))
            + [whole(value) for value in more],
            out_specs=[whole(wide), whole(wide), whole(given)],
            scratch_shapes=[
                pltpu.VMEM((width, width), low),
                pltpu.VMEM((2, width, cols), low),
                pltpu.VMEM((tokens, cols), low),
                pltpu.VMEM((tokens, 384), low),
                pltpu.VMEM((tokens, 128), jnp.float32),
                pltpu.VMEM((tokens, 128), jnp.float32),
                pltpu.VMEM((tokens, width) if call else (8, 128), jnp.float32),
                pltpu.SemaphoreType.DMA((3,)),
            ],
        ),
        out_shape=[wide, wide, given],
        compiler_params=pltpu.CompilerParams(vmem_limit_bytes=58 * 2**20),
        cost_estimate=pl.CostEstimate(flops=60 * 10**9, bytes_accessed=8 * 10**6, transcendentals=0),
        name="attend_back",
    )(groups, order, branch, hidden, q, k, v, lse, cosine, sine, bias, *proj, *mixer_p, *more)


TILE = 256


def extra_rows(expert_count):
    return 8 if expert_count <= 24 else 16


def table_picks(expert_count):
    extra = extra_rows(expert_count)
    row = lax.broadcasted_iota(jnp.int32, (extra, 128), 0)
    lane = lax.broadcasted_iota(jnp.int32, (extra, 128), 1)
    return [
        (lane == row + block * extra).astype(jnp.float32).astype(jnp.bfloat16)
        for block in range(expert_count // extra)
    ]


def table_rows(values, picks, width):
    low = jnp.bfloat16
    high = values.astype(low)
    parts = (high, (values - high.astype(jnp.float32)).astype(low))
    rows = [dot(pick, value, NT).astype(low) for pick in picks for value in parts]
    left = width - TILE * len(rows)
    if left:
        rows.append(jnp.zeros((picks[0].shape[0], left), low))
    return jnp.concatenate(rows, axis=1)


def table_values(rows, picks):
    total = None
    for block, pick in enumerate(picks):
        for part in range(2):
            at = (2 * block + part) * TILE
            value = dot(rows[:, at : at + TILE], pick, TN)
            total = value if total is None else total + value
    return total


def project_kernel(mine, count, expert_count, order_ref, left_ref, x_ref, routes_ref, gain_ref, router_ref, *rest):
    pieces = rest[:count]
    resid_ref, gates_ref, rows_ref, weight_ref, sem = rest[count:]
    copies = projector_copies(mine, pieces, order_ref, weight_ref, sem)

    @pl.when(pl.program_id(0) == 0)
    def _():
        for copy in copies:
            copy.start()
        for copy in copies:
            copy.wait()

    low = jnp.bfloat16
    resid = x_ref[...].astype(jnp.float32) + dot(left_ref[...], weight_ref[...], NN)
    resid_ref[...] = resid
    scale = lax.rsqrt(jnp.mean(resid * resid, axis=1, keepdims=True) + EPSILON)
    hidden = (resid * scale * gain_ref[...]).astype(low)
    rows_ref[:TILE, :] = hidden
    logits = dot(hidden, router_ref[...], NT)
    lane = lax.broadcasted_iota(jnp.int32, logits.shape, 1)
    routed = lane == routes_ref[:, 0:1]
    for k in range(1, routes_ref.shape[1]):
        routed = routed | (lane == routes_ref[:, k : k + 1])
    logits = jnp.where(routed, logits, NEGATIVE)
    powers = jnp.exp(logits - jnp.max(logits, axis=1, keepdims=True))
    gates = powers / jnp.sum(powers, axis=1, keepdims=True)
    gates_ref[...] = gates
    rows_ref[TILE:, :] = table_rows(gates, table_picks(expert_count), hidden.shape[1])


def project(left, x, routes, gain, router, expert_count, proj, mine, order):
    tokens, width = left.shape
    tall = TILE + extra_rows(expert_count)
    tile = lambda w, h=TILE: pl.BlockSpec((h, w), lambda i, o: (i, 0))
    whole = lambda a: pl.BlockSpec(a.shape, lambda i, o: (0, 0))
    return pl.pallas_call(
        lambda *refs: project_kernel(mine, len(proj), expert_count, *refs),
        grid_spec=pltpu.PrefetchScalarGridSpec(
            num_scalar_prefetch=1,
            grid=(tokens // TILE,),
            in_specs=[tile(width), tile(width), tile(routes.shape[1]), whole(gain), whole(router)]
            + [pl.BlockSpec(memory_space=pltpu.HBM)] * len(proj),
            out_specs=[tile(width), tile(128), tile(width, tall)],
            scratch_shapes=[pltpu.VMEM((width, width), jnp.bfloat16), pltpu.SemaphoreType.DMA],
        ),
        out_shape=[
            jax.ShapeDtypeStruct((tokens, width), jnp.float32),
            jax.ShapeDtypeStruct((tokens, 128), jnp.float32),
            jax.ShapeDtypeStruct((tokens // TILE * tall, width), jnp.bfloat16),
        ],
        compiler_params=pltpu.CompilerParams(vmem_limit_bytes=40 * 2**20),
        cost_estimate=pl.CostEstimate(flops=30 * 10**9, bytes_accessed=8 * 10**6, transcendentals=0),
        name="project",
    )(order, left, x, routes, gain, router, *proj)


def turn_kernel(expert_count, order_ref, a_ref, b_ref, c_ref, rows_ref, gates_ref, resid_ref, cot_ref, left_ref, gain_ref, router_ref,
                branch_ref, grad_ref, mine_ref, other_ref, low_ref, small_ref, gains_ref):
    low = jnp.bfloat16
    step = pl.program_id(0)
    total = a_ref[...].astype(jnp.float32) + b_ref[...].astype(jnp.float32) + c_ref[...].astype(jnp.float32)
    gates = gates_ref[...]
    grad_gates = table_values(total[TILE:, :].astype(low), table_picks(expert_count))
    mean = jnp.sum(gates * grad_gates, axis=1, keepdims=True)
    grad_logits = gates * (grad_gates - mean)
    high = grad_logits.astype(low)
    rest = (grad_logits - high.astype(jnp.float32)).astype(low)
    grad = total[:TILE, :] + dot(high, router_ref[...], NN) + dot(rest, router_ref[...], NN)
    resid = resid_ref[...]
    scale = lax.rsqrt(jnp.mean(resid * resid, axis=1, keepdims=True) + EPSILON)
    normed = resid * scale
    hidden = rows_ref[:TILE, :]
    small = dot(hidden, jnp.concatenate([high, rest], axis=1), TN)
    small = small[:, :128] + small[:, 128:]
    gains = jnp.sum(grad * normed, axis=0, keepdims=True)
    grad = grad * gain_ref[...]
    mean = jnp.mean(grad * normed, axis=1, keepdims=True)
    grad = cot_ref[...].astype(jnp.float32) + scale * (grad - normed * mean)
    grad_ref[...] = grad
    branch = grad.astype(low)
    branch_ref[...] = branch
    low_ref[pl.ds(pl.multiple_of(step * TILE, TILE), TILE), :] = branch

    @pl.when(step == 0)
    def _():
        small_ref[...] = small
        gains_ref[...] = gains

    @pl.when(step > 0)
    def _():
        small_ref[...] += small
        gains_ref[...] += gains

    @pl.when(step == pl.num_programs(0) - 1)
    def _():
        core = order_ref[order_ref.shape[0] - 1]
        half = low_ref.shape[1] // 2
        left = left_ref[...]
        small = small_ref[...].astype(low) + row_to_column(gains_ref[...], expert_count)
        for ref, which in ((mine_ref, core), (other_ref, 1 - core)):
            part = low_ref[:, pl.ds(pl.multiple_of(which * half, 128), half)]
            ref[:, :half] = dot(left, part, TN).astype(low)
            ref[:, half:] = small


def turn(expert_count, order, a, b, c, rows, gates, resid, cots, left, gain, router):
    tokens, width = left.shape
    tall = TILE + extra_rows(expert_count)
    tile = lambda w, h=TILE: pl.BlockSpec((h, w), lambda i, o: (i, 0))
    whole = lambda a: pl.BlockSpec(a.shape, lambda i, o: (0, 0))
    half = jax.ShapeDtypeStruct((width, width // 2 + 128), jnp.bfloat16)
    return pl.pallas_call(
        lambda *refs: turn_kernel(expert_count, *refs),
        grid_spec=pltpu.PrefetchScalarGridSpec(
            num_scalar_prefetch=1,
            grid=(tokens // TILE,),
            in_specs=[tile(width, tall)] * 4 + [tile(128), tile(width), tile(width), whole(left)]
            + [whole(gain), whole(router)],
            out_specs=[tile(width), tile(width), whole(half), whole(half)],
            scratch_shapes=[
                pltpu.VMEM((tokens, width), jnp.bfloat16),
                pltpu.VMEM((width, 128), jnp.float32),
                pltpu.VMEM((1, width), jnp.float32),
            ],
        ),
        out_shape=[
            jax.ShapeDtypeStruct((tokens, width), jnp.bfloat16),
            jax.ShapeDtypeStruct((tokens, width), jnp.float32),
            half,
            half,
        ],
        compiler_params=pltpu.CompilerParams(vmem_limit_bytes=58 * 2**20),
        cost_estimate=pl.CostEstimate(flops=30 * 10**9, bytes_accessed=8 * 10**6, transcendentals=0),
        name="turn",
    )(order, a, b, c, rows, gates, resid, cots, left, gain, router)


def fold_kernel(pairs, table_ref, *refs):
    x_ref, y_ref, own_ref, beside_ref, above_ref = refs[2 * pairs :]
    places = ((x_ref, 0, 2), (y_ref, 2, 4), (own_ref, 4, 6), (beside_ref, 6, 7), (above_ref, 7, 8))
    step = pl.program_id(0)
    at = 0
    for i in range(pairs):
        left, right = refs[2 * i][...], refs[2 * i + 1][...]
        value = (left.astype(jnp.float32) + right.astype(jnp.float32)).astype(jnp.bfloat16)
        columns = slice(at, at + value.shape[1])
        at += value.shape[1]
        for ref, low, high in places:

            @pl.when((step >= low) & (step < high))
            def _():
                ref[:, columns] = value


def fold(*operands):
    if lax.axis_size("shard") != 4:
        parts = [add_low(operands[i], operands[i + 1]) for i in range(0, len(operands), 2)]
        blocks = jnp.concatenate(parts, axis=1)
        return reduce_first(blocks.reshape(lax.axis_size("shard"), -1, blocks.shape[1]))
    me = lax.axis_index("shard")
    rows = operands[0].shape[0] // 8
    where = [(3, 0), (1, 0), (3, 1), (2, 1), (0, 0), (0, 1), (1, 1), (2, 0)]
    table = jnp.stack([(me ^ r) * 2 + half for r, half in where]).astype(jnp.int32)
    columns = sum(v.shape[1] for v in operands[::2])
    given = lambda n: jax.ShapeDtypeStruct((n * rows, columns), jnp.bfloat16)
    place = lambda low, count: pl.BlockSpec((rows, columns), lambda i, t: (jnp.clip(i - low, 0, count - 1), 0))
    x, y, own, beside, above = pl.pallas_call(
        lambda *refs: fold_kernel(len(operands) // 2, *refs),
        grid_spec=pltpu.PrefetchScalarGridSpec(
            num_scalar_prefetch=1,
            grid=(8,),
            in_specs=[pl.BlockSpec((rows, v.shape[1]), lambda i, t: (t[i], 0)) for v in operands],
            out_specs=[place(0, 2), place(2, 2), place(4, 2), place(6, 1), place(7, 1)],
        ),
        out_shape=[given(2), given(2), given(2), given(1), given(1)],
        cost_estimate=pl.CostEstimate(flops=10**9, bytes_accessed=4 * 10**6, transcendentals=0),
        name="fold",
    )(table, *operands)
    return own, beside, above, across(x, 1), across(y, 2)


def finish_kernel(order_ref, one_mine, one_other, two_mine, two_other, mixer_ref, proj_ref, router_ref, second_ref, first_ref):
    lower = order_ref[order_ref.shape[0] - 1] == 0
    wide = jnp.float32
    half = proj_ref.shape[1] // 2
    groups = []
    for mine, other in ((one_mine, one_other), (two_mine, two_other)):
        a, b = mine[:, :640].astype(wide), other[:, :640].astype(wide)
        groups += [jnp.where(lower, a, b), jnp.where(lower, b, a)]
    for g, value in enumerate(groups):
        mixer_ref[:, 384 * g : 384 * (g + 1)] = value[:, :384]
        mixer_ref[:, 1536 + 128 * g : 1536 + 128 * (g + 1)] = value[:, 384:512]
        mixer_ref[:, 2048 + 128 * g : 2048 + 128 * (g + 1)] = value[:, 512:]
    a, b = one_mine[:, 640 : 640 + half].astype(wide), one_other[:, 640 : 640 + half].astype(wide)
    proj_ref[:, :half] = jnp.where(lower, a, b)
    proj_ref[:, half:] = jnp.where(lower, b, a)
    experts = router_ref.shape[0]
    size = (experts + 8, 128)
    pick = lax.broadcasted_iota(jnp.int32, size, 0) == lax.broadcasted_iota(jnp.int32, size, 1)
    pick = pick.astype(wide).astype(jnp.bfloat16)
    rows = dot(pick, one_mine[:, 640 + half :], NT)
    router_ref[...] = rows[:experts, :]
    second_ref[...] = rows[experts : experts + 1, :]
    first_ref[...] = dot(pick, two_mine[:, 640:], NT)[:1, :]


def finish(expert_count, order, one, two):
    rows = one[0].shape[0]
    block = 128 if rows % 128 == 0 else rows
    tall = [jax.ShapeDtypeStruct((rows, w), jnp.float32) for w in (2560, 1536)]
    flat = [jax.ShapeDtypeStruct((h, rows), jnp.float32) for h in (expert_count, 1, 1)]
    spec = lambda a: pl.BlockSpec((block, a.shape[1]), lambda i, o: (i, 0))
    flat_spec = lambda a: pl.BlockSpec((a.shape[0], block), lambda i, o: (0, i))
    operands = [*one, *two]
    return pl.pallas_call(
        finish_kernel,
        grid_spec=pltpu.PrefetchScalarGridSpec(
            num_scalar_prefetch=1,
            grid=(rows // block,),
            in_specs=[spec(v) for v in operands],
            out_specs=[spec(v) for v in tall] + [flat_spec(v) for v in flat],
        ),
        out_shape=tall + flat,
        cost_estimate=pl.CostEstimate(flops=10**9, bytes_accessed=4 * 10**6, transcendentals=0),
        name="finish",
    )(order, *operands)


def expert_kernel(counts, expert_count, order_ref, place_ref, xa_ref, xb_ref, u_ref, *rest):
    pieces, more = counts
    gates_p, ups_p, downs_p = (rest[i * pieces : (i + 1) * pieces] for i in range(3))
    rest = rest[3 * pieces + more :]
    (gta_ref, gtb_ref, out_ref, x_ref, mid_ref, sides_ref, wg_ref, wu_ref, wd_ref, sems) = rest
    low = jnp.bfloat16
    extra = extra_rows(expert_count)
    step = pl.program_id(0)
    half = pl.num_programs(0) // 2
    load = piece_copies(gates_p, order_ref, wg_ref, sems.at[0], 1, 0)
    load += piece_copies(ups_p, order_ref, wu_ref, sems.at[0], 1, 0)
    load_down = piece_copies(downs_p, order_ref, wd_ref, sems.at[1], 2, 0)

    @pl.when(step == 0)
    def _():
        for copy in load + load_down:
            copy.start()

    first = step < half
    table = jnp.where(first, xa_ref[TILE:, :], xb_ref[TILE:, :])

    @pl.when(first)
    def _():
        x_ref[...] = xa_ref[:TILE, :]

    @pl.when(jnp.logical_not(first))
    def _():
        x_ref[...] = xb_ref[:TILE, :]

    @pl.when(step == 0)
    def _():
        for copy in load + load_down:
            copy.wait()

    rows, cots = x_ref[...], u_ref[...]
    row = lax.broadcasted_iota(jnp.int32, (extra, 128), 0)
    lane = lax.broadcasted_iota(jnp.int32, (extra, 128), 1)
    expert = place_ref[2] * 2 + lane
    picks = []
    for block in range(expert_count // extra):
        hit = (lane < 2) & (row == expert - block * extra)
        picks.append(jnp.where(hit, 1.0, 0.0).astype(low))
    gates_wide = None
    for block, pick in enumerate(picks):
        for part in range(2):
            at = (2 * block + part) * TILE
            value = dot(table[:, at : at + TILE], pick, TN)
            gates_wide = value if gates_wide is None else gates_wide + value
    out = None
    taken = None
    sums = []
    for l in range(2):
        gates = gates_wide[:, l : l + 1]
        gate_in = dot(rows, wg_ref[l], NN)
        up_in = dot(rows, wu_ref[l], NN)
        back = dot(cots, wd_ref[l], NT)
        sigma = 1.0 / (1.0 + jnp.exp(-gate_in))
        active = gate_in * sigma
        mid = active * up_in
        sums.append(jnp.sum(mid * back, axis=1, keepdims=True))
        mid_low = (mid * gates).astype(low)
        mid_ref[l] = mid_low
        part = dot(mid_low, wd_ref[l], NN)
        out = part if out is None else out + part
        back = back * gates
        grad_gate = (back * up_in * sigma * (1.0 + gate_in * (1.0 - sigma))).astype(low)
        grad_up = (back * active).astype(low)
        sides_ref[2 * l] = grad_gate
        sides_ref[2 * l + 1] = grad_up
        part = dot(grad_gate, wg_ref[l], NT) + dot(grad_up, wu_ref[l], NT)
        taken = part if taken is None else taken + part
    out_ref[...] = out.astype(low)
    taken_low = taken.astype(low)
    wide = lax.broadcasted_iota(jnp.int32, (TILE, 128), 1)
    sums = jnp.where(wide == 0, sums[0], jnp.where(wide == 1, sums[1], 0.0))
    high = sums.astype(low)
    parts = (high, (sums - high.astype(jnp.float32)).astype(low))
    columns = [dot(pick, value, NT).astype(low) for pick in picks for value in parts]
    left = rows.shape[1] - TILE * len(columns)
    if left:
        columns.append(jnp.zeros((extra, left), low))
    columns = jnp.concatenate(columns, axis=1)

    @pl.when(first)
    def _():
        gta_ref[:TILE, :] = taken_low
        gta_ref[TILE:, :] = columns

    @pl.when(jnp.logical_not(first))
    def _():
        gtb_ref[:TILE, :] = taken_low
        gtb_ref[TILE:, :] = columns


def expert_chunk(order, place, xa, xb, cots, gates, ups, downs, expert_count, kept):
    total, width = cots.shape
    devices = lax.axis_size("expert")
    tokens = total // devices
    hidden = gates[0].shape[-1]
    half = tokens // TILE
    steps = 2 * half
    low = jnp.bfloat16
    tall = TILE + extra_rows(expert_count)
    first = pl.BlockSpec((tall, width), lambda i, o, p: (jnp.minimum(i, half - 1), 0))
    second = pl.BlockSpec((tall, width), lambda i, o, p: (jnp.maximum(i - half, 0), 0))
    where = lambda i, p: jnp.where(i < half, p[0] * half + i, p[1] * half + i - half)
    anywhere = pl.BlockSpec(memory_space=pltpu.HBM)
    big_row = pl.BlockSpec((TILE, width), lambda i, o, p: (where(i, p), 0))
    big = lambda n: pl.BlockSpec((n, TILE, hidden), lambda i, o, p: (0, where(i, p), 0))
    single = jax.ShapeDtypeStruct((half * tall, width), low)
    shapes = [jax.ShapeDtypeStruct((total, width), low)] * 2
    shapes += [jax.ShapeDtypeStruct((n, total, hidden), low) for n in (2, 4)]
    operands = [order, place, xa, xb, cots, *gates, *ups, *downs]
    in_specs = [first, second, big_row] + [anywhere] * (3 * len(gates))
    aliases = {}
    more = 0
    if kept is not None:
        more = len(shapes)
        aliases = {len(operands) + i: 2 + i for i in range(more)}
        operands += list(kept)
        in_specs += [anywhere] * more
    res = pl.pallas_call(
        lambda *refs: expert_kernel((len(gates), more), expert_count, *refs),
        grid_spec=pltpu.PrefetchScalarGridSpec(
            num_scalar_prefetch=2,
            grid=(steps,),
            in_specs=in_specs,
            out_specs=[first, second, big_row, big_row, big(2), big(4)],
            scratch_shapes=[
                pltpu.VMEM((2, width, hidden), low),
                pltpu.VMEM((2, width, hidden), low),
                pltpu.VMEM((2, hidden, width), low),
                pltpu.SemaphoreType.DMA((2,)),
            ],
        ),
        out_shape=[single] * 2 + shapes,
        input_output_aliases=aliases,
        compiler_params=pltpu.CompilerParams(vmem_limit_bytes=58 * 2**20),
        cost_estimate=pl.CostEstimate(flops=81 * 10**9, bytes_accessed=8 * 10**6, transcendentals=0),
        name="expert_chunk",
    )(*operands)
    return res[:2], res[2:]


def wide_grad_kernel(on_rows, left_ref, right_ref, out_ref, acc_ref):
    step = pl.program_id(1)
    value = dot(left_ref[...], right_ref[...], TN)

    @pl.when(step == 0)
    def _():
        acc_ref[...] = value

    @pl.when(step > 0)
    def _():
        acc_ref[...] += value

    @pl.when(step == pl.num_programs(1) - 1)
    def _():
        rows, cols = out_ref.shape[-2:]
        for j in range(out_ref.shape[0]):
            if on_rows:
                part = acc_ref[j * rows : (j + 1) * rows, :]
            else:
                part = acc_ref[:, j * cols : (j + 1) * cols]
            out_ref[j] = part.astype(out_ref.dtype)


def weight_grad(left, right, parts, on_rows):
    count = left.shape[0] if left.ndim == 3 else right.shape[0]
    total, size_m = left.shape[-2:]
    size_n = right.shape[-1]
    block = 1024
    spec = lambda a: (
        pl.BlockSpec((None, block, a.shape[-1]), lambda l, k: (l, k, 0))
        if a.ndim == 3
        else pl.BlockSpec((block, a.shape[-1]), lambda l, k: (k, 0))
    )
    shape = (size_m // parts, size_n) if on_rows else (size_m, size_n // parts)
    return pl.pallas_call(
        lambda *refs: wide_grad_kernel(on_rows, *refs),
        grid=(count, total // block),
        in_specs=[spec(left), spec(right)],
        out_specs=pl.BlockSpec((parts, None) + shape, lambda l, k: (0, l, 0, 0)),
        out_shape=jax.ShapeDtypeStruct((parts, count) + shape, jnp.bfloat16),
        scratch_shapes=[pltpu.VMEM((size_m, size_n), jnp.float32)],
        compiler_params=pltpu.CompilerParams(vmem_limit_bytes=48 * 2**20),
        cost_estimate=pl.CostEstimate(flops=60 * 10**9, bytes_accessed=8 * 10**6, transcendentals=0),
        name="weight_grad",
    )(left, right)


def sorted_grad_kernel(on_rows, half, order_ref, left_ref, right_ref, own_ref, beside_ref, above_ref, x_ref, y_ref, acc_ref):
    index, step = pl.program_id(0), pl.program_id(1)
    value = dot(left_ref[...], right_ref[...], TN)

    @pl.when(step == 0)
    def _():
        acc_ref[...] = value

    @pl.when(step > 0)
    def _():
        acc_ref[...] += value

    def block(r):
        rows, cols = own_ref.shape
        size = rows if on_rows else cols
        place = pl.ds(pl.multiple_of(order_ref[r] * size, 128), size)
        part = acc_ref[place, :] if on_rows else acc_ref[:, place]
        return part.astype(own_ref.dtype)

    last = step == pl.num_programs(1) - 1

    @pl.when(last)
    def _():
        own_ref[...] = block(0)

    @pl.when(last & (index < half))
    def _():
        x_ref[0] = block(3)
        x_ref[1] = block(1)
        above_ref[...] = block(2)

    @pl.when(last & (index >= half))
    def _():
        y_ref[0] = block(3)
        y_ref[1] = block(2)
        beside_ref[...] = block(1)


def grad_exchange(left, right, order, on_rows, pick=0, stride=1):
    shards = lax.axis_size("shard")
    if shards != 4:
        return reduce_first(weight_grad(left, right[pick::stride] if right.ndim == 3 else right, shards, on_rows))
    count = left.shape[0] if left.ndim == 3 else right.shape[0] // stride
    half = count // 2
    total, size_m = left.shape[-2:]
    size_n = right.shape[-1]
    block = 1024
    spec = lambda a: (
        pl.BlockSpec((None, block, a.shape[-1]), lambda l, k, o: (l * stride + pick, k, 0))
        if a.ndim == 3
        else pl.BlockSpec((block, a.shape[-1]), lambda l, k, o: (k, 0))
    )
    shape = (size_m // 4, size_n) if on_rows else (size_m, size_n // 4)
    early = lambda l: jnp.minimum(l, half - 1)
    late = lambda l: jnp.maximum(l - half, 0)
    one = lambda f: pl.BlockSpec((None,) + shape, lambda l, k, o: (f(l), 0, 0))
    two = lambda f: pl.BlockSpec((2, None) + shape, lambda l, k, o: (0, f(l), 0, 0))
    low = lambda *lead: jax.ShapeDtypeStruct(lead + shape, jnp.bfloat16)
    own, beside, above, x, y = pl.pallas_call(
        lambda *refs: sorted_grad_kernel(on_rows, half, *refs),
        grid_spec=pltpu.PrefetchScalarGridSpec(
            num_scalar_prefetch=1,
            grid=(count, total // block),
            in_specs=[spec(left), spec(right)],
            out_specs=[one(lambda l: l), one(late), one(early), two(early), two(late)],
            scratch_shapes=[pltpu.VMEM((size_m, size_n), jnp.float32)],
        ),
        out_shape=[low(count), low(half), low(half), low(2, half), low(2, half)],
        compiler_params=pltpu.CompilerParams(vmem_limit_bytes=48 * 2**20),
        cost_estimate=pl.CostEstimate(flops=60 * 10**9, bytes_accessed=8 * 10**6, transcendentals=0),
        name="weight_grad",
    )(order, left, right)
    merged = lambda v: v.reshape((2 * half,) + shape)
    return own, beside, above, across(merged(x), 1), across(merged(y), 2)


def per_device(
    layer_input,
    out_cotangent,
    parents,
    routes,
    norm1_gain,
    qkv_weight,
    out_weight,
    norm2_gain,
    router_weight,
    gate_weight,
    up_weight,
    down_weight,
):
    low = jnp.bfloat16
    shards = lax.axis_size("shard")
    tokens, width = layer_input.shape
    expert_count = router_weight.shape[1]
    local_count = gate_weight.shape[0]
    chips = lax.axis_size("expert") // 2
    me = lax.axis_index("expert")
    core = me % 2
    order = shard_order()
    queries = HEADS * HEAD_DIM

    by_group = [
        jnp.concatenate(
            [
                qkv_weight[:, 384 * g : 384 * (g + 1)],
                qkv_weight[:, queries + 128 * g : queries + 128 * (g + 1)],
                qkv_weight[:, queries + 512 + 128 * g : queries + 512 + 128 * (g + 1)],
            ],
            axis=1,
        )
        for g in range(4)
    ]
    half_columns = lambda g, h: jnp.concatenate([by_group[g], by_group[h]], axis=1)
    block = jnp.where(core == 0, half_columns(0, 2), half_columns(1, 3))
    small = jnp.concatenate([router_weight, norm1_gain[:, None], norm2_gain[:, None]], axis=1).T
    small = gather_small(small)
    mixer_first = gather_first(block)
    router = jnp.pad(small[:expert_count], ((0, 128 - expert_count), (0, 0)))
    gain_one = small[expert_count].astype(jnp.float32)[None, :]
    gain_two = small[expert_count + 1].astype(jnp.float32)[None, :]
    activity = layer_input.astype(jnp.float32)
    hidden_one = (activity * inverse_rms(activity) * gain_one).astype(low)
    bias, cosine, sine = tree_tables(parents)
    mixer_first, hidden_one, bias, cosine, sine = lax.optimization_barrier(
        (mixer_first, hidden_one, bias, cosine, sine)
    )
    mine = gather_second(mixer_first, 0)
    mixer_p = mine + [swap_core(p) for p in mine]
    block = lax.dynamic_slice_in_dim(out_weight, core * (out_weight.shape[0] // 2), out_weight.shape[0] // 2, 0)
    project_first = gather_first(after(block, *mine))

    cots = lax.all_gather(out_cotangent, "expert", axis=0, tiled=True)

    saved = None
    groups = []
    for call in range(2):
        groups.append(jnp.stack([2 * call + core, 2 * call + 1 - core]).astype(jnp.int32))
        saved = attend(hidden_one, mixer_p, call, order, groups[call], cosine, sine, bias, saved)
        if call == 0:
            project_first, saved = lax.optimization_barrier((project_first, saved))
            proj = gather_second(project_first, 0)
            near = swap_core(jnp.concatenate(proj[:3], axis=0))
            gates_first = gather_first(after(gate_weight, project_first))
    proj, near, gates_first, saved = lax.optimization_barrier((proj, near, gates_first, saved))
    far = [swap_core(p) for p in proj[3:]]
    ups_first = gather_first(after(up_weight, proj))
    proj = proj + [near] + far
    attended, query, keys, values, log_total = saved
    resid, gates, sent_rows = project(
        attended, layer_input, routes, gain_two, router, expert_count, proj, len(mixer_p) // 2, order
    )
    ups_first, sent_rows = lax.optimization_barrier((ups_first, sent_rows))
    gates_p = gather_second(gates_first, 0)
    ups_first, down_block = lax.optimization_barrier((ups_first, after(down_weight, *gates_p)))
    downs_first = gather_first(down_block, True)
    ups_p = gather_second(ups_first, 0)
    downs_p = gather_second(downs_first, 0)
    rows = [sent_rows]
    rows.append(next_chip(rows[0]))
    beside = swap_core(rows[0])
    rows[0], rows[1], beside = lax.optimization_barrier((rows[0], rows[1], beside))
    kept = total = None
    for step in range(chips):
        ahead = next_chip(rows[step + 1]) if step + 2 < chips else None
        beside_next = swap_core(rows[step + 1]) if step + 1 < chips else None
        here = rows[step]
        if step > 1:
            here, total = lax.optimization_barrier((here, total))
        sent = next_chip(total) if step > 1 else None
        place = jnp.stack([(me - 2 * step) % (2 * chips), (me - 2 * step) % (2 * chips) ^ 1, me])
        parts, kept = expert_chunk(
            order, place.astype(jnp.int32), here, beside, cots, gates_p, ups_p, downs_p, expert_count, kept
        )
        parts, kept, ahead, beside, sent = lax.optimization_barrier((parts, kept, ahead, beside_next, sent))
        if ahead is not None:
            rows.append(ahead)
        pair = (parts[0], swap_core(parts[1]))
        if step == 0:
            last = pair
        else:
            total = add_low(*pair, *(() if sent is None else (sent,)))
    out_all, all_rows, all_mid, all_sides = kept
    all_rows, total = lax.optimization_barrier((all_rows, total))
    sent = next_chip(total)
    gate_state = grad_exchange(all_rows, all_sides, order, True, 0, 2)
    gate_done, all_rows = lax.optimization_barrier((gate_state[0], all_rows))
    gate_state = (gate_done,) + gate_state[1:]
    up_state = grad_exchange(all_rows, all_sides, order, True, 1, 2)
    sent, up_done, gate_state = lax.optimization_barrier((sent, up_state[0], gate_state))
    up_state = (up_done,) + up_state[1:]
    branch_out = lax.psum_scatter(after(out_all, sent), "expert", scatter_dimension=0, tiled=True)
    grad_branch, grad_resid, out_mine, out_other = turn(
        expert_count, order, *last, sent, sent_rows, gates, resid, out_cotangent, attended, gain_two, router
    )
    grad_branch, up_state, out_other = lax.optimization_barrier((grad_branch, up_state, out_other))
    gate_state, up_state = reduce_second(gate_state), reduce_second(up_state)
    out_sent = swap_core(out_other)
    backward = lambda call, branch, *more: attend_back(
        call, branch, hidden_one, proj, mixer_p, order, groups[call],
        query, keys, values, log_total, cosine, sine, bias, *more,
    )
    wide, other, part = backward(0, grad_branch)
    grad_branch, wide, other, part, out_mine, out_sent, gate_state, up_state = lax.optimization_barrier(
        (grad_branch, wide, other, part, out_mine, out_sent, gate_state, up_state)
    )
    state_one = fold(wide, swap_core(other), out_mine, out_sent)
    grad_branch, folded = lax.optimization_barrier((grad_branch, state_one[0]))
    state_one = (folded,) + state_one[1:]
    wide, other, grad_input = backward(1, grad_branch, part, layer_input, grad_resid, gain_one)
    wide, other, grad_input, state_one, all_mid = lax.optimization_barrier(
        (wide, other, grad_input, state_one, all_mid)
    )
    state_one = reduce_second(state_one)
    sent = swap_core(other)
    down_state = grad_exchange(all_mid, cots, order, False)
    kernel_done, state_one, sent, gate_state, up_state = lax.optimization_barrier(
        (down_state[0], state_one, sent, gate_state, up_state)
    )
    down_state = (kernel_done,) + down_state[1:]
    one = reduce_last(state_one)
    wide, one = lax.optimization_barrier((wide, one))
    state_two = fold(wide, sent)
    state_two = reduce_second(state_two)
    two = reduce_last(state_two)
    two, down_state = lax.optimization_barrier((two, down_state))
    down_state = reduce_second(down_state)
    one = reduce_chips(one)
    two = reduce_chips(two)
    grad_gate = reduce_last(gate_state, jnp.float32)
    grad_up = reduce_last(up_state, jnp.float32)
    grad_down = reduce_last(down_state, jnp.float32)
    output = (resid + branch_out.astype(jnp.float32)).astype(low)
    two, output, grad_gate, grad_up = lax.optimization_barrier((two, output, grad_gate, grad_up))
    grad_mixer, grad_projector, grad_router, grad_gain_two, grad_gain_one = finish(
        expert_count, order, (one, swap_core(one)), (two, swap_core(two))
    )
    return (
        output,
        grad_input,
        grad_gain_one[0],
        grad_mixer,
        grad_projector,
        grad_gain_two[0],
        grad_router.T,
        grad_gate,
        grad_up,
        grad_down,
    )


def solution(mesh):
    return jax.shard_map(
        per_device,
        mesh=mesh,
        in_specs=(
            P(("expert", "shard"), None),
            P(("expert", "shard"), None),
            P(("expert", "shard")),
            P(("expert", "shard"), None),
            P("shard"),
            P("shard", None),
            P("shard", None),
            P("shard"),
            P("shard", None),
            P("expert", "shard", None),
            P("expert", "shard", None),
            P("expert", None, "shard"),
        ),
        out_specs=(
            P(("expert", "shard"), None),
            P(("expert", "shard"), None),
            P("shard"),
            P("shard", None),
            P("shard", None),
            P("shard"),
            P("shard", None),
            P("expert", "shard", None),
            P("expert", "shard", None),
            P("expert", None, "shard"),
        ),
        check_vma=False,
    )
```

```python
import jax
import jax.numpy as jnp
from jax import lax
from jax.experimental import pallas as pl
from jax.experimental.pallas import tpu as pltpu
from jax.sharding import PartitionSpec as P

HEADS = 24
KV_HEADS = 8
HEAD_DIM = 64
SEG = 128

EPSILON = 1e-06
THETA = 10000.0
NEGATIVE = -1e30

NT = (((1,), (1,)), ((), ()))
NN = (((1,), (0,)), ((), ()))
TN = (((0,), (0,)), ((), ()))
def dot(left, right, dims):
    return lax.dot_general(left, right, dims, preferred_element_type=jnp.float32)

def turned(values):
    lane = lax.broadcasted_iota(jnp.int32, values.shape, 1)
    first = lane % HEAD_DIM < HEAD_DIM // 2
    ahead = pltpu.roll(values, 128 - HEAD_DIM // 2, 1)
    behind = pltpu.roll(values, HEAD_DIM // 2, 1)
    return jnp.where(first, -ahead, behind)


def tree_tables(parents):
    segs = parents.shape[0]
    ids = jnp.arange(segs, dtype=jnp.int32)
    pointer = ids
    ancestry = jnp.zeros((segs, segs), jnp.bool_)
    for _ in range(segs):
        landed = pointer[:, None] == ids[None, :]
        ancestry = ancestry | landed
        pointer = jnp.sum(jnp.where(landed, parents[None, :], 0), axis=1)
    depth = jnp.sum(ancestry.astype(jnp.float32), axis=1) - 1.0
    token_ids = jnp.arange(segs * SEG, dtype=jnp.int32)
    positions = jnp.repeat(depth, SEG) * SEG + (token_ids % SEG).astype(jnp.float32)
    reach = jnp.repeat(jnp.repeat(ancestry.astype(jnp.float32), SEG, axis=0), SEG, axis=1)
    allowed = (reach > 0.5) & (token_ids[None, :] <= token_ids[:, None])
    half = HEAD_DIM // 2
    frequency = THETA ** (-(jnp.arange(half, dtype=jnp.float32) * 2.0) / HEAD_DIM)
    angles = positions[:, None] * frequency[None, :]
    cosine, sine = jnp.cos(angles), jnp.sin(angles)
    return (
        jnp.where(allowed, 0.0, NEGATIVE),
        jnp.concatenate([cosine] * 4, axis=1),
        jnp.concatenate([sine] * 4, axis=1),
    )


def inverse_rms(values):
    return lax.rsqrt(jnp.mean(values * values, axis=1, keepdims=True) + EPSILON)


def swap_core(value):
    count = lax.axis_size("expert")
    return lax.ppermute(value, "expert", [(i, i ^ 1) for i in range(count)])


def next_chip(value):
    count = lax.axis_size("expert")
    return lax.ppermute(value, "expert", [(i, (i + 2) % count) for i in range(count)])


def across(value, mask):
    return lax.ppermute(value, "shard", [(i, i ^ mask) for i in range(4)])


def after(value, *earlier):
    return lax.optimization_barrier((value,) + earlier)[0]


def gather_first(block, on_lanes=False):
    if lax.axis_size("shard") != 4:
        if on_lanes:
            return [lax.all_gather(block, "shard", axis=block.ndim - 1, tiled=True)[None]]
        return [lax.all_gather(block, "shard", axis=0, tiled=False)]
    return [block[None], across(block, 1)[None], across(block, 2)[None]]


def gather_second(pieces, split):
    if len(pieces) == 1:
        return pieces
    axis = split + 1
    half = pieces[1].shape[axis] // 2
    first = lax.slice_in_dim(pieces[2], 0, half, axis=axis)
    last = lax.slice_in_dim(pieces[1], half, 2 * half, axis=axis)
    return pieces + [across(first, 1), across(last, 2)]


def gather_small(value):
    if lax.axis_size("shard") != 4:
        return lax.all_gather(value, "shard", axis=1, tiled=True)
    me = lax.axis_index("shard")
    rows = value.shape[0]
    near = jnp.concatenate([value, across(value, 1)])
    far = across(near, 2)
    parts = [near[:rows], near[rows:], far[:rows], far[rows:]]
    odd = me % 2 == 1
    parts = [jnp.where(odd, parts[i ^ 1], parts[i]) for i in range(4)]
    high = me >= 2
    parts = [jnp.where(high, parts[i ^ 2], parts[i]) for i in range(4)]
    return jnp.concatenate(parts, axis=1)


def own_groups_kernel(order_ref, query_ref, key_ref, value_ref, out_ref):
    out_ref[:, :384] = query_ref[...]
    out_ref[:, 384:512] = key_ref[...]
    out_ref[:, 512:] = value_ref[...]


def own_groups(weight, order):
    rows = weight.shape[0]
    last = order.shape[0] - 1
    spec = lambda w, at: pl.BlockSpec((rows, w), lambda j, o: (0, at + 2 * j + o[last]))
    return pl.pallas_call(
        own_groups_kernel,
        grid_spec=pltpu.PrefetchScalarGridSpec(
            num_scalar_prefetch=1,
            grid=(2,),
            in_specs=[spec(384, 0), spec(128, 12), spec(128, 16)],
            out_specs=pl.BlockSpec((rows, 640), lambda j, o: (0, j)),
        ),
        out_shape=pltpu.HBM((rows, 1280), weight.dtype),
        cost_estimate=pl.CostEstimate(flops=10**8, bytes_accessed=10**6, transcendentals=0),
        name="own_groups",
    )(order, weight, weight, weight)


def shard_order():
    shards = lax.axis_size("shard")
    me = lax.axis_index("shard")
    core = lax.axis_index("expert") % 2
    if shards != 4:
        return jnp.concatenate([jnp.arange(shards, dtype=jnp.int32), core[None].astype(jnp.int32)])
    return jnp.stack([me, me ^ 1, me ^ 2, me ^ 3, me ^ 3, core]).astype(jnp.int32)


def add_low(*terms):
    total = terms[0].astype(jnp.float32)
    for term in terms[1:]:
        total = total + term.astype(jnp.float32)
    return total.astype(jnp.bfloat16)


def reduce_first(blocks):
    if lax.axis_size("shard") != 4:
        return (lax.psum_scatter(blocks, "shard", scatter_dimension=0, tiled=False),)
    me = lax.axis_index("shard")
    own, beside, above, far = (
        lax.dynamic_index_in_dim(blocks, me ^ r, 0, keepdims=False) for r in range(4)
    )
    half = own.shape[0] // 2
    from_x = across(jnp.concatenate([far[:half], beside[:half]]), 1)
    from_y = across(jnp.concatenate([far[half:], above[half:]]), 2)
    return own, beside[half:], above[:half], from_x, from_y


def reduce_second(state):
    if len(state) == 1:
        return state
    own, beside, above, from_x, from_y = state
    half = own.shape[0] // 2
    last_x = across(add_low(beside, from_y[:half]), 1)
    last_y = across(add_low(above, from_x[:half]), 2)
    return own, from_x, from_y, last_x, last_y


def reduce_last(state, dtype=jnp.bfloat16):
    if len(state) == 1:
        return state[0].astype(dtype)
    own, from_x, from_y, last_x, last_y = (v.astype(jnp.float32) for v in state)
    half = own.shape[0] // 2
    low_half, high_half = own[:half] + from_x[half:] + last_y, own[half:] + last_x + from_y[half:]
    return jnp.concatenate([low_half, high_half]).astype(dtype)


def chip_ahead(value, distance):
    count = lax.axis_size("expert")
    return lax.ppermute(value, "expert", [(i, (i + 2 * distance) % count) for i in range(count)])


def chips_send(value):
    chips = lax.axis_size("expert") // 2
    z = lax.axis_index("expert") // 2
    size = value.shape[0] // chips
    part = lambda d: lax.dynamic_slice_in_dim(value, (z + d) % chips * size, size, 0)
    return [part(0)] + [chip_ahead(part(d), d) for d in range(1, chips)]


def chips_gather(parts):
    mine = add_low(*parts)
    return [mine] + [chip_ahead(mine, d) for d in range(1, len(parts))]


def chips_order(parts):
    chips = len(parts)
    z = lax.axis_index("expert") // 2
    size = parts[0].shape[0]
    onward = [parts[-j % chips] for j in range(chips)]
    return lax.dynamic_slice_in_dim(
        jnp.concatenate(onward + onward[:-1]), (chips - z) % chips * size, chips * size, 0
    )


def piece_copies(pieces, order_ref, target, sem, axis, split, base=0, stride=None, window=None):
    copies = []
    slot = 0
    block = pieces[0].shape[1:]
    stride = block[axis] if stride is None else stride
    align = 128 if axis == len(block) - 1 else 16
    for piece in pieces:
        for c in range(piece.shape[0]):
            shape = piece.shape[1:]
            start = [0] * len(shape)
            if slot == 4 and shape[split] < block[split]:
                start[split] = block[split] - shape[split]
            start[axis] = pl.multiple_of(order_ref[slot] * stride + base + start[axis], align)
            index = tuple(pl.ds(first, size) for first, size in zip(start, shape))
            source = piece.at[c]
            if window is not None:
                cols = shape[-1] // 2
                source = source.at[:, window * cols : (window + 1) * cols]
                index = index[:-1] + (slice(None),)
            copies.append(pltpu.make_async_copy(source, target.at[index], sem))
            slot += 1
    return copies


def attend_kernel(count, call, order_ref, group_ref, hidden_ref, cos_ref, sin_ref, bias_ref, *rest):
    mine, other = rest[:count], rest[count : 2 * count]
    att_ref, q_ref, k_ref, v_ref, lse_ref, weight_ref, sems = rest[-7:]
    step = pl.program_id(0)
    first = piece_copies(mine, order_ref, weight_ref.at[0], sems.at[0], 0, 0, window=call)
    second = piece_copies(other, order_ref, weight_ref.at[1], sems.at[1], 0, 0, window=call)

    @pl.when(step == 0)
    def _():
        for copy in first + second:
            copy.start()
        for copy in first:
            copy.wait()

    @pl.when(step == 1)
    def _():
        for copy in second:
            copy.wait()

    hidden = hidden_ref[...]
    cosine, sine = cos_ref[...], sin_ref[...]
    mixed = dot(hidden, weight_ref[step], NN)
    low = jnp.bfloat16
    scaling = HEAD_DIM ** (-0.5)
    for p in range(3):
        part = mixed[:, 128 * p : 128 * p + 128]
        turned_part = (part * cosine + turned(part) * sine).astype(low)
        q_ref[:, 128 * p : 128 * p + 128] = turned_part * scaling
    part = mixed[:, 384:512]
    k_ref[...] = (part * cosine + turned(part) * sine).astype(low)
    v_ref[...] = mixed[:, 512:640].astype(low)
    tokens = hidden.shape[0]
    for seg in range(tokens // SEG):
        rows = pl.ds(seg * SEG, SEG)
        span = (seg + 1) * SEG
        bias = bias_ref[rows, :span]
        keys = [k_ref[:span, HEAD_DIM * kv : HEAD_DIM * (kv + 1)] for kv in range(2)]
        vals = [v_ref[:span, HEAD_DIM * kv : HEAD_DIM * (kv + 1)] for kv in range(2)]
        queries = [q_ref[rows, HEAD_DIM * h : HEAD_DIM * (h + 1)] for h in range(6)]
        scores = [dot(queries[h], keys[h // 3], NT) + bias for h in range(6)]
        highest = [jnp.max(v, axis=1, keepdims=True) for v in scores]
        powers = [jnp.exp(v - m) for v, m in zip(scores, highest)]
        totals = [jnp.sum(v, axis=1, keepdims=True) for v in powers]
        probs = [(v * (1.0 / t)).astype(low) for v, t in zip(powers, totals)]
        outs = [dot(v, vals[h // 3], NN) for h, v in enumerate(probs)]
        logs = [m + jnp.log(t) for m, t in zip(highest, totals)]
        att_ref[rows, :] = jnp.concatenate(outs, axis=1).astype(low)
        lse_ref[rows, :] = jnp.concatenate(logs + [logs[-1]] * 2, axis=1)


def attend(hidden, mixer_p, call, order, groups, cosine, sine, bias, kept):
    tokens, width = hidden.shape
    low = jnp.bfloat16
    whole = lambda a: pl.BlockSpec(a.shape, lambda j, o, g: (0, 0))
    anywhere = pl.BlockSpec(memory_space=pltpu.HBM)
    col = lambda w: pl.BlockSpec((tokens, w), lambda j, o, g: (0, g[j]))
    shape = lambda w: pltpu.HBM((tokens, w), low)
    operands = [order, groups, hidden, cosine, sine, bias, *mixer_p]
    in_specs = [whole(hidden), whole(cosine), whole(sine), whole(bias)]
    in_specs += [anywhere] * len(mixer_p)
    aliases = {}
    if kept is not None:
        aliases = {len(operands) + i: i for i in range(5)}
        operands += list(kept)
        in_specs += [anywhere] * 5
    cols = mixer_p[0].shape[-1] // 2
    return pl.pallas_call(
        lambda *refs: attend_kernel(len(mixer_p) // 2, call, *refs),
        grid_spec=pltpu.PrefetchScalarGridSpec(
            num_scalar_prefetch=2,
            grid=(2,),
            in_specs=in_specs,
            out_specs=[col(384), col(384), col(128), col(128)]
            + [pl.BlockSpec((None, tokens, 8), lambda j, o, g: (g[j], 0, 0))],
            scratch_shapes=[pltpu.VMEM((2, width, cols), low), pltpu.SemaphoreType.DMA((2,))],
        ),
        out_shape=[shape(1536), shape(1536), shape(512), shape(512)]
        + [pltpu.HBM((4, tokens, 8), jnp.float32)],
        input_output_aliases=aliases,
        compiler_params=pltpu.CompilerParams(vmem_limit_bytes=40 * 2**20),
        cost_estimate=pl.CostEstimate(flops=48 * 10**9, bytes_accessed=8 * 10**6, transcendentals=0),
        name="attend",
    )(*operands)


def projector_copies(count, pieces, order_ref, target, sem):
    rows = pieces[0].shape[1]
    slots = order_ref.shape[0] - 1
    core = order_ref[slots]
    copies = piece_copies(pieces[:count], order_ref, target, sem, 0, 0, core * rows, 2 * rows)
    return copies + piece_copies(
        pieces[count:], order_ref, target, sem, 0, 0, (1 - core) * rows, 2 * rows
    )


def row_to_column(row, lane):
    low = jnp.bfloat16
    pick = (lax.broadcasted_iota(jnp.int32, (8, 128), 1) == lane) & (
        lax.broadcasted_iota(jnp.int32, (8, 128), 0) == 0
    )
    pick = pick.astype(jnp.float32).astype(low)
    rows = jnp.broadcast_to(row, (8, row.shape[1]))
    high = rows.astype(low)
    rest = (rows - high.astype(jnp.float32)).astype(low)
    return (dot(high, pick, TN) + dot(rest, pick, TN)).astype(low)


def attend_back_kernel(mine, counts, call, group_ref, order_ref, branch_ref, hidden_ref, q_ref, k_ref, v_ref, lse_ref, cos_ref, sin_ref, bias_ref, *rest):
    first, second = counts
    pieces, mixer_p = rest[:first], rest[first : first + second]
    rest = rest[first + second :]
    if call:
        part_ref, x_ref, resid_ref, gain_ref = rest[:4]
        rest = rest[4:]
    wide_refs, input_ref = rest[:2], rest[2]
    proj_ref, weight_ref, mixed_ref, grad_ref, dk_ref, dv_ref, total_ref, sems = rest[3:]
    step = pl.program_id(0)
    load = projector_copies(mine, pieces, order_ref, proj_ref, sems.at[0])
    half = second // 2
    more = [
        piece_copies(mixer_p[c * half : (c + 1) * half], order_ref, weight_ref.at[c], sems.at[1 + c], 0, 0, window=call)
        for c in range(2)
    ]

    @pl.when(step == 0)
    def _():
        for copy in load + more[0] + more[1]:
            copy.start()
        for copy in load:
            copy.wait()

    group = group_ref[step]
    low = jnp.bfloat16
    rows = pl.ds(pl.multiple_of(group * 384, 128), 384)
    grad_ref[...] = dot(branch_ref[...], proj_ref[rows, :], NT).astype(low)
    cosine, sine = cos_ref[...], sin_ref[...]
    scaling = HEAD_DIM ** (-0.5)
    tokens = branch_ref.shape[0]
    for seg in reversed(range(tokens // SEG)):
        rows = pl.ds(seg * SEG, SEG)
        span = (seg + 1) * SEG
        bias = bias_ref[rows, :span]
        part = lambda ref, r, h: ref[r, HEAD_DIM * h : HEAD_DIM * (h + 1)]
        keys = [part(k_ref, pl.ds(0, span), kv) for kv in range(2)]
        vals = [part(v_ref, pl.ds(0, span), kv) for kv in range(2)]
        queries = [part(q_ref, rows, h) for h in range(6)]
        grads = [part(grad_ref, rows, h) for h in range(6)]
        scores = [dot(queries[h], keys[h // 3], NT) + bias for h in range(6)]
        gprobs = [dot(grads[h], vals[h // 3], NT) for h in range(6)]
        probs = [jnp.exp(v - lse_ref[rows, h : h + 1]) for h, v in enumerate(scores)]
        centres = [jnp.sum(p * g, axis=1, keepdims=True) for p, g in zip(probs, gprobs)]
        gscore = [(p * (g - c)).astype(low) for p, g, c in zip(probs, gprobs, centres)]
        probs = [p.astype(low) for p in probs]
        gqs = [dot(v, keys[h // 3], NN) * scaling for h, v in enumerate(gscore)]
        three = lambda values, kv: jnp.concatenate(values[3 * kv : 3 * kv + 3], 0)
        gks = [dot(three(gscore, kv), three(queries, kv), TN) for kv in range(2)]
        gvs = [dot(three(probs, kv), three(grads, kv), TN) for kv in range(2)]
        gq = jnp.concatenate(gqs, axis=1)
        cos_rows, sin_rows = cosine[seg * SEG : span], sine[seg * SEG : span]
        for p in range(3):
            part = gq[:, 128 * p : 128 * p + 128]
            mixed_ref[rows, 128 * p : 128 * p + 128] = (
                part * cos_rows - turned(part * sin_rows)
            ).astype(low)
        gk = jnp.concatenate(gks, axis=1)
        gv = jnp.concatenate(gvs, axis=1)
        if span == tokens:
            dk_ref[...] = gk
            dv_ref[...] = gv
        else:
            dk_ref[:span, :] += gk
            dv_ref[:span, :] += gv
    gk = dk_ref[...]
    mixed_ref[:, 384:512] = (gk * cosine - turned(gk * sine)).astype(low)
    mixed_ref[:, 512:640] = dv_ref[...].astype(low)
    for c in range(2):

        @pl.when(step == c)
        def _():
            for copy in more[c]:
                copy.wait()

    wide = dot(hidden_ref[...], mixed_ref[...], TN).astype(low)
    part = dot(mixed_ref[...], weight_ref[step], NT)
    for c in range(2):

        @pl.when(step == c)
        def _():
            wide_refs[c][:, :640] = wide

    if not call:

        @pl.when(step == 0)
        def _():
            input_ref[...] = part

        @pl.when(step > 0)
        def _():
            input_ref[...] += part

        return

    @pl.when(step == 0)
    def _():
        total_ref[...] = part + part_ref[...]

    @pl.when(step > 0)
    def _():
        value = x_ref[...].astype(jnp.float32)
        scale = lax.rsqrt(jnp.mean(value * value, axis=1, keepdims=True) + EPSILON)
        normed = value * scale
        grad = total_ref[...] + part
        product = grad * normed
        gains = row_to_column(jnp.sum(product, axis=0, keepdims=True), 0)
        for ref in wide_refs:
            ref[:, 640:] = gains
        grad = grad * gain_ref[...]
        mean = jnp.mean(grad * normed, axis=1, keepdims=True)
        input_ref[...] = (resid_ref[...] + scale * (grad - normed * mean)).astype(low)


def attend_back(call, branch, hidden, proj, mixer_p, order, groups, q, k, v, lse, cosine, sine, bias, *more):
    tokens, width = branch.shape
    low = jnp.bfloat16
    whole = lambda a: pl.BlockSpec(a.shape, lambda j, g, o: (0, 0))
    col = lambda w: pl.BlockSpec((tokens, w), lambda j, g, o: (0, g[j]))
    cols = mixer_p[0].shape[-1] // 2
    mine = len(mixer_p) // 2
    wide = jax.ShapeDtypeStruct((width, cols + 128 * call), low)
    given = jax.ShapeDtypeStruct((tokens, width), low if call else jnp.float32)
    return pl.pallas_call(
        lambda *refs: attend_back_kernel(mine, (len(proj), len(mixer_p)), call, *refs),
        grid_spec=pltpu.PrefetchScalarGridSpec(
            num_scalar_prefetch=2,
            grid=(2,),
            in_specs=[whole(branch), whole(hidden), col(384), col(128), col(128)]
            + [pl.BlockSpec((None, tokens, 8), lambda j, g, o: (g[j], 0, 0))]
            + [whole(cosine), whole(sine), whole(bias)]
            + [pl.BlockSpec(memory_space=pltpu.HBM)] * (len(proj) + len(mixer_p))
            + [whole(value) for value in more],
            out_specs=[whole(wide), whole(wide), whole(given)],
            scratch_shapes=[
                pltpu.VMEM((width, width), low),
                pltpu.VMEM((2, width, cols), low),
                pltpu.VMEM((tokens, cols), low),
                pltpu.VMEM((tokens, 384), low),
                pltpu.VMEM((tokens, 128), jnp.float32),
                pltpu.VMEM((tokens, 128), jnp.float32),
                pltpu.VMEM((tokens, width) if call else (8, 128), jnp.float32),
                pltpu.SemaphoreType.DMA((3,)),
            ],
        ),
        out_shape=[wide, wide, given],
        compiler_params=pltpu.CompilerParams(vmem_limit_bytes=58 * 2**20),
        cost_estimate=pl.CostEstimate(flops=60 * 10**9, bytes_accessed=8 * 10**6, transcendentals=0),
        name="attend_back",
    )(groups, order, branch, hidden, q, k, v, lse, cosine, sine, bias, *proj, *mixer_p, *more)


TILE = 256


def extra_rows(expert_count):
    return 8 if expert_count <= 24 else 16


def table_picks(expert_count):
    extra = extra_rows(expert_count)
    row = lax.broadcasted_iota(jnp.int32, (extra, 128), 0)
    lane = lax.broadcasted_iota(jnp.int32, (extra, 128), 1)
    return [
        (lane == row + block * extra).astype(jnp.float32).astype(jnp.bfloat16)
        for block in range(expert_count // extra)
    ]


def table_rows(values, picks, width):
    low = jnp.bfloat16
    high = values.astype(low)
    parts = (high, (values - high.astype(jnp.float32)).astype(low))
    rows = [dot(pick, value, NT).astype(low) for pick in picks for value in parts]
    left = width - TILE * len(rows)
    if left:
        rows.append(jnp.zeros((picks[0].shape[0], left), low))
    return jnp.concatenate(rows, axis=1)


def table_values(rows, picks):
    total = None
    for block, pick in enumerate(picks):
        for part in range(2):
            at = (2 * block + part) * TILE
            value = dot(rows[:, at : at + TILE], pick, TN)
            total = value if total is None else total + value
    return total


def project_kernel(mine, count, expert_count, order_ref, left_ref, x_ref, routes_ref, gain_ref, router_ref, *rest):
    pieces = rest[:count]
    resid_ref, gates_ref, rows_ref, weight_ref, sem = rest[count:]
    copies = projector_copies(mine, pieces, order_ref, weight_ref, sem)

    @pl.when(pl.program_id(0) == 0)
    def _():
        for copy in copies:
            copy.start()
        for copy in copies:
            copy.wait()

    low = jnp.bfloat16
    resid = x_ref[...].astype(jnp.float32) + dot(left_ref[...], weight_ref[...], NN)
    resid_ref[...] = resid
    scale = lax.rsqrt(jnp.mean(resid * resid, axis=1, keepdims=True) + EPSILON)
    hidden = (resid * scale * gain_ref[...]).astype(low)
    rows_ref[:TILE, :] = hidden
    logits = dot(hidden, router_ref[...], NT)
    lane = lax.broadcasted_iota(jnp.int32, logits.shape, 1)
    routed = lane == routes_ref[:, 0:1]
    for k in range(1, routes_ref.shape[1]):
        routed = routed | (lane == routes_ref[:, k : k + 1])
    logits = jnp.where(routed, logits, NEGATIVE)
    powers = jnp.exp(logits - jnp.max(logits, axis=1, keepdims=True))
    gates = powers / jnp.sum(powers, axis=1, keepdims=True)
    gates_ref[...] = gates
    rows_ref[TILE:, :] = table_rows(gates, table_picks(expert_count), hidden.shape[1])


def project(left, x, routes, gain, router, expert_count, proj, mine, order):
    tokens, width = left.shape
    tall = TILE + extra_rows(expert_count)
    tile = lambda w, h=TILE: pl.BlockSpec((h, w), lambda i, o: (i, 0))
    whole = lambda a: pl.BlockSpec(a.shape, lambda i, o: (0, 0))
    return pl.pallas_call(
        lambda *refs: project_kernel(mine, len(proj), expert_count, *refs),
        grid_spec=pltpu.PrefetchScalarGridSpec(
            num_scalar_prefetch=1,
            grid=(tokens // TILE,),
            in_specs=[tile(width), tile(width), tile(routes.shape[1]), whole(gain), whole(router)]
            + [pl.BlockSpec(memory_space=pltpu.HBM)] * len(proj),
            out_specs=[tile(width), tile(128), tile(width, tall)],
            scratch_shapes=[pltpu.VMEM((width, width), jnp.bfloat16), pltpu.SemaphoreType.DMA],
        ),
        out_shape=[
            jax.ShapeDtypeStruct((tokens, width), jnp.float32),
            jax.ShapeDtypeStruct((tokens, 128), jnp.float32),
            jax.ShapeDtypeStruct((tokens // TILE * tall, width), jnp.bfloat16),
        ],
        compiler_params=pltpu.CompilerParams(vmem_limit_bytes=40 * 2**20),
        cost_estimate=pl.CostEstimate(flops=30 * 10**9, bytes_accessed=8 * 10**6, transcendentals=0),
        name="project",
    )(order, left, x, routes, gain, router, *proj)


def turn_kernel(expert_count, order_ref, a_ref, b_ref, c_ref, rows_ref, gates_ref, resid_ref, cot_ref, left_ref, gain_ref, router_ref,
                branch_ref, grad_ref, mine_ref, other_ref, low_ref, small_ref, gains_ref):
    low = jnp.bfloat16
    step = pl.program_id(0)
    total = a_ref[...].astype(jnp.float32) + b_ref[...].astype(jnp.float32) + c_ref[...].astype(jnp.float32)
    gates = gates_ref[...]
    grad_gates = table_values(total[TILE:, :].astype(low), table_picks(expert_count))
    mean = jnp.sum(gates * grad_gates, axis=1, keepdims=True)
    grad_logits = gates * (grad_gates - mean)
    high = grad_logits.astype(low)
    rest = (grad_logits - high.astype(jnp.float32)).astype(low)
    grad = total[:TILE, :] + dot(high, router_ref[...], NN) + dot(rest, router_ref[...], NN)
    resid = resid_ref[...]
    scale = lax.rsqrt(jnp.mean(resid * resid, axis=1, keepdims=True) + EPSILON)
    normed = resid * scale
    hidden = rows_ref[:TILE, :]
    small = dot(hidden, jnp.concatenate([high, rest], axis=1), TN)
    small = small[:, :128] + small[:, 128:]
    gains = jnp.sum(grad * normed, axis=0, keepdims=True)
    grad = grad * gain_ref[...]
    mean = jnp.mean(grad * normed, axis=1, keepdims=True)
    grad = cot_ref[...].astype(jnp.float32) + scale * (grad - normed * mean)
    grad_ref[...] = grad
    branch = grad.astype(low)
    branch_ref[...] = branch
    low_ref[pl.ds(pl.multiple_of(step * TILE, TILE), TILE), :] = branch

    @pl.when(step == 0)
    def _():
        small_ref[...] = small
        gains_ref[...] = gains

    @pl.when(step > 0)
    def _():
        small_ref[...] += small
        gains_ref[...] += gains

    @pl.when(step == pl.num_programs(0) - 1)
    def _():
        core = order_ref[order_ref.shape[0] - 1]
        half = low_ref.shape[1] // 2
        left = left_ref[...]
        small = small_ref[...].astype(low) + row_to_column(gains_ref[...], expert_count)
        for ref, which in ((mine_ref, core), (other_ref, 1 - core)):
            part = low_ref[:, pl.ds(pl.multiple_of(which * half, 128), half)]
            ref[:, :half] = dot(left, part, TN).astype(low)
            ref[:, half:] = small


def turn(expert_count, order, a, b, c, rows, gates, resid, cots, left, gain, router):
    tokens, width = left.shape
    tall = TILE + extra_rows(expert_count)
    tile = lambda w, h=TILE: pl.BlockSpec((h, w), lambda i, o: (i, 0))
    whole = lambda a: pl.BlockSpec(a.shape, lambda i, o: (0, 0))
    half = jax.ShapeDtypeStruct((width, width // 2 + 128), jnp.bfloat16)
    return pl.pallas_call(
        lambda *refs: turn_kernel(expert_count, *refs),
        grid_spec=pltpu.PrefetchScalarGridSpec(
            num_scalar_prefetch=1,
            grid=(tokens // TILE,),
            in_specs=[tile(width, tall)] * 4 + [tile(128), tile(width), tile(width), whole(left)]
            + [whole(gain), whole(router)],
            out_specs=[tile(width), tile(width), whole(half), whole(half)],
            scratch_shapes=[
                pltpu.VMEM((tokens, width), jnp.bfloat16),
                pltpu.VMEM((width, 128), jnp.float32),
                pltpu.VMEM((1, width), jnp.float32),
            ],
        ),
        out_shape=[
            jax.ShapeDtypeStruct((tokens, width), jnp.bfloat16),
            jax.ShapeDtypeStruct((tokens, width), jnp.float32),
            half,
            half,
        ],
        compiler_params=pltpu.CompilerParams(vmem_limit_bytes=58 * 2**20),
        cost_estimate=pl.CostEstimate(flops=30 * 10**9, bytes_accessed=8 * 10**6, transcendentals=0),
        name="turn",
    )(order, a, b, c, rows, gates, resid, cots, left, gain, router)


def fold_kernel(pairs, order_ref, *refs):
    x_ref, y_ref, own_ref, beside_ref, above_ref = refs[2 * pairs :]
    step = pl.program_id(0)
    half = x_ref.shape[0] // 2
    low, high = slice(0, half), slice(half, 2 * half)
    places = (
        ((own_ref, low), (own_ref, high)),
        ((x_ref, high), (beside_ref, low)),
        ((above_ref, low), (y_ref, high)),
        ((x_ref, low), (y_ref, low)),
    )
    at = 0
    for i in range(pairs):
        value = refs[2 * i][...] + refs[2 * i + 1][...]
        columns = slice(at, at + value.shape[1])
        at += value.shape[1]
        for r, ((first, first_rows), (second, second_rows)) in enumerate(places):

            @pl.when(step == r)
            def _():
                first[first_rows, columns] = value[low]
                second[second_rows, columns] = value[high]


def fold(order, *operands):
    if lax.axis_size("shard") != 4:
        parts = [add_low(operands[i], operands[i + 1]) for i in range(0, len(operands), 2)]
        blocks = jnp.concatenate(parts, axis=1)
        return reduce_first(blocks.reshape(lax.axis_size("shard"), -1, blocks.shape[1]))
    rows = operands[0].shape[0] // 4
    columns = sum(v.shape[1] for v in operands[::2])
    given = [jax.ShapeDtypeStruct((n * rows // 2, columns), jnp.bfloat16) for n in (2, 2, 2, 1, 1)]
    x, y, own, beside, above = pl.pallas_call(
        lambda *refs: fold_kernel(len(operands) // 2, *refs),
        grid_spec=pltpu.PrefetchScalarGridSpec(
            num_scalar_prefetch=1,
            grid=(4,),
            in_specs=[pl.BlockSpec((rows, v.shape[1]), lambda i, o: (o[i], 0)) for v in operands],
            out_specs=[pl.BlockSpec(v.shape, lambda i, o: (0, 0)) for v in given],
        ),
        out_shape=given,
        compiler_params=pltpu.CompilerParams(vmem_limit_bytes=40 * 2**20),
        cost_estimate=pl.CostEstimate(flops=3 * 10**9, bytes_accessed=4 * 10**6, transcendentals=0),
        name="fold",
    )(order, *operands)
    return own, beside, above, across(x, 1), across(y, 2)


def finish_kernel(order_ref, one_mine, one_other, two_mine, two_other, mixer_ref, proj_ref, router_ref, second_ref, first_ref):
    lower = order_ref[order_ref.shape[0] - 1] == 0
    wide = jnp.float32
    half = proj_ref.shape[1] // 2
    groups = []
    for mine, other in ((one_mine, one_other), (two_mine, two_other)):
        a, b = mine[:, :640].astype(wide), other[:, :640].astype(wide)
        groups += [jnp.where(lower, a, b), jnp.where(lower, b, a)]
    for g, value in enumerate(groups):
        mixer_ref[:, 384 * g : 384 * (g + 1)] = value[:, :384]
        mixer_ref[:, 1536 + 128 * g : 1536 + 128 * (g + 1)] = value[:, 384:512]
        mixer_ref[:, 2048 + 128 * g : 2048 + 128 * (g + 1)] = value[:, 512:]
    a, b = one_mine[:, 640 : 640 + half].astype(wide), one_other[:, 640 : 640 + half].astype(wide)
    proj_ref[:, :half] = jnp.where(lower, a, b)
    proj_ref[:, half:] = jnp.where(lower, b, a)
    experts = router_ref.shape[0]
    size = (experts + 8, 128)
    pick = lax.broadcasted_iota(jnp.int32, size, 0) == lax.broadcasted_iota(jnp.int32, size, 1)
    pick = pick.astype(wide).astype(jnp.bfloat16)
    rows = dot(pick, one_mine[:, 640 + half :], NT)
    router_ref[...] = rows[:experts, :]
    second_ref[...] = rows[experts : experts + 1, :]
    first_ref[...] = dot(pick, two_mine[:, 640:], NT)[:1, :]


def finish(expert_count, order, one, two):
    rows = one[0].shape[0]
    block = 128 if rows % 128 == 0 else rows
    tall = [jax.ShapeDtypeStruct((rows, w), jnp.float32) for w in (2560, 1536)]
    flat = [jax.ShapeDtypeStruct((h, rows), jnp.float32) for h in (expert_count, 1, 1)]
    spec = lambda a: pl.BlockSpec((block, a.shape[1]), lambda i, o: (i, 0))
    flat_spec = lambda a: pl.BlockSpec((a.shape[0], block), lambda i, o: (0, i))
    operands = [*one, *two]
    return pl.pallas_call(
        finish_kernel,
        grid_spec=pltpu.PrefetchScalarGridSpec(
            num_scalar_prefetch=1,
            grid=(rows // block,),
            in_specs=[spec(v) for v in operands],
            out_specs=[spec(v) for v in tall] + [flat_spec(v) for v in flat],
        ),
        out_shape=tall + flat,
        cost_estimate=pl.CostEstimate(flops=10**9, bytes_accessed=4 * 10**6, transcendentals=0),
        name="finish",
    )(order, *operands)


def expert_kernel(counts, expert_count, order_ref, place_ref, xa_ref, xb_ref, u_ref, *rest):
    pieces, more = counts
    gates_p, ups_p, downs_p = (rest[i * pieces : (i + 1) * pieces] for i in range(3))
    rest = rest[3 * pieces + more :]
    (gta_ref, gtb_ref, out_ref, x_ref, mid_ref, sides_ref, wg_ref, wu_ref, wd_ref, sems) = rest
    low = jnp.bfloat16
    extra = extra_rows(expert_count)
    step = pl.program_id(0)
    half = pl.num_programs(0) // 2
    load = piece_copies(gates_p, order_ref, wg_ref, sems.at[0], 1, 0)
    load += piece_copies(ups_p, order_ref, wu_ref, sems.at[0], 1, 0)
    load_down = piece_copies(downs_p, order_ref, wd_ref, sems.at[1], 2, 0)

    @pl.when(step == 0)
    def _():
        for copy in load + load_down:
            copy.start()

    first = step < half
    table = jnp.where(first, xa_ref[TILE:, :], xb_ref[TILE:, :])

    @pl.when(first)
    def _():
        x_ref[...] = xa_ref[:TILE, :]

    @pl.when(jnp.logical_not(first))
    def _():
        x_ref[...] = xb_ref[:TILE, :]

    @pl.when(step == 0)
    def _():
        for copy in load + load_down:
            copy.wait()

    rows, cots = x_ref[...], u_ref[...]
    row = lax.broadcasted_iota(jnp.int32, (extra, 128), 0)
    lane = lax.broadcasted_iota(jnp.int32, (extra, 128), 1)
    expert = place_ref[2] * 2 + lane
    picks = []
    for block in range(expert_count // extra):
        hit = (lane < 2) & (row == expert - block * extra)
        picks.append(jnp.where(hit, 1.0, 0.0).astype(low))
    gates_wide = None
    for block, pick in enumerate(picks):
        for part in range(2):
            at = (2 * block + part) * TILE
            value = dot(table[:, at : at + TILE], pick, TN)
            gates_wide = value if gates_wide is None else gates_wide + value
    out = None
    taken = None
    sums = []
    for l in range(2):
        gates = gates_wide[:, l : l + 1]
        gate_in = dot(rows, wg_ref[l], NN)
        up_in = dot(rows, wu_ref[l], NN)
        back = dot(cots, wd_ref[l], NT)
        sigma = 1.0 / (1.0 + jnp.exp(-gate_in))
        active = gate_in * sigma
        mid = active * up_in
        sums.append(jnp.sum(mid * back, axis=1, keepdims=True))
        mid_low = (mid * gates).astype(low)
        mid_ref[l] = mid_low
        part = dot(mid_low, wd_ref[l], NN)
        out = part if out is None else out + part
        back = back * gates
        grad_gate = (back * up_in * sigma * (1.0 + gate_in * (1.0 - sigma))).astype(low)
        grad_up = (back * active).astype(low)
        sides_ref[2 * l] = grad_gate
        sides_ref[2 * l + 1] = grad_up
        part = dot(grad_gate, wg_ref[l], NT) + dot(grad_up, wu_ref[l], NT)
        taken = part if taken is None else taken + part
    out_ref[...] = out.astype(low)
    taken_low = taken.astype(low)
    wide = lax.broadcasted_iota(jnp.int32, (TILE, 128), 1)
    sums = jnp.where(wide == 0, sums[0], jnp.where(wide == 1, sums[1], 0.0))
    high = sums.astype(low)
    parts = (high, (sums - high.astype(jnp.float32)).astype(low))
    columns = [dot(pick, value, NT).astype(low) for pick in picks for value in parts]
    left = rows.shape[1] - TILE * len(columns)
    if left:
        columns.append(jnp.zeros((extra, left), low))
    columns = jnp.concatenate(columns, axis=1)

    @pl.when(first)
    def _():
        gta_ref[:TILE, :] = taken_low
        gta_ref[TILE:, :] = columns

    @pl.when(jnp.logical_not(first))
    def _():
        gtb_ref[:TILE, :] = taken_low
        gtb_ref[TILE:, :] = columns


def expert_chunk(order, place, xa, xb, cots, gates, ups, downs, expert_count, kept):
    total, width = cots.shape
    devices = lax.axis_size("expert")
    tokens = total // devices
    hidden = gates[0].shape[-1]
    half = tokens // TILE
    steps = 2 * half
    low = jnp.bfloat16
    tall = TILE + extra_rows(expert_count)
    first = pl.BlockSpec((tall, width), lambda i, o, p: (jnp.minimum(i, half - 1), 0))
    second = pl.BlockSpec((tall, width), lambda i, o, p: (jnp.maximum(i - half, 0), 0))
    where = lambda i, p: jnp.where(i < half, p[0] * half + i, p[1] * half + i - half)
    anywhere = pl.BlockSpec(memory_space=pltpu.HBM)
    big_row = pl.BlockSpec((TILE, width), lambda i, o, p: (where(i, p), 0))
    big = lambda n: pl.BlockSpec((n, TILE, hidden), lambda i, o, p: (0, where(i, p), 0))
    single = jax.ShapeDtypeStruct((half * tall, width), low)
    shapes = [jax.ShapeDtypeStruct((total, width), low)] * 2
    shapes += [jax.ShapeDtypeStruct((n, total, hidden), low) for n in (2, 4)]
    operands = [order, place, xa, xb, cots, *gates, *ups, *downs]
    in_specs = [first, second, big_row] + [anywhere] * (3 * len(gates))
    aliases = {}
    more = 0
    if kept is not None:
        more = len(shapes)
        aliases = {len(operands) + i: 2 + i for i in range(more)}
        operands += list(kept)
        in_specs += [anywhere] * more
    res = pl.pallas_call(
        lambda *refs: expert_kernel((len(gates), more), expert_count, *refs),
        grid_spec=pltpu.PrefetchScalarGridSpec(
            num_scalar_prefetch=2,
            grid=(steps,),
            in_specs=in_specs,
            out_specs=[first, second, big_row, big_row, big(2), big(4)],
            scratch_shapes=[
                pltpu.VMEM((2, width, hidden), low),
                pltpu.VMEM((2, width, hidden), low),
                pltpu.VMEM((2, hidden, width), low),
                pltpu.SemaphoreType.DMA((2,)),
            ],
        ),
        out_shape=[single] * 2 + shapes,
        input_output_aliases=aliases,
        compiler_params=pltpu.CompilerParams(vmem_limit_bytes=58 * 2**20),
        cost_estimate=pl.CostEstimate(flops=81 * 10**9, bytes_accessed=8 * 10**6, transcendentals=0),
        name="expert_chunk",
    )(*operands)
    return res[:2], res[2:]


def wide_grad_kernel(on_rows, left_ref, right_ref, out_ref, acc_ref):
    step = pl.program_id(1)
    value = dot(left_ref[...], right_ref[...], TN)

    @pl.when(step == 0)
    def _():
        acc_ref[...] = value

    @pl.when(step > 0)
    def _():
        acc_ref[...] += value

    @pl.when(step == pl.num_programs(1) - 1)
    def _():
        rows, cols = out_ref.shape[-2:]
        for j in range(out_ref.shape[0]):
            if on_rows:
                part = acc_ref[j * rows : (j + 1) * rows, :]
            else:
                part = acc_ref[:, j * cols : (j + 1) * cols]
            out_ref[j] = part.astype(out_ref.dtype)


def weight_grad(left, right, parts, on_rows):
    count = left.shape[0] if left.ndim == 3 else right.shape[0]
    total, size_m = left.shape[-2:]
    size_n = right.shape[-1]
    block = 1024
    spec = lambda a: (
        pl.BlockSpec((None, block, a.shape[-1]), lambda l, k: (l, k, 0))
        if a.ndim == 3
        else pl.BlockSpec((block, a.shape[-1]), lambda l, k: (k, 0))
    )
    shape = (size_m // parts, size_n) if on_rows else (size_m, size_n // parts)
    return pl.pallas_call(
        lambda *refs: wide_grad_kernel(on_rows, *refs),
        grid=(count, total // block),
        in_specs=[spec(left), spec(right)],
        out_specs=pl.BlockSpec((parts, None) + shape, lambda l, k: (0, l, 0, 0)),
        out_shape=jax.ShapeDtypeStruct((parts, count) + shape, jnp.bfloat16),
        scratch_shapes=[pltpu.VMEM((size_m, size_n), jnp.float32)],
        compiler_params=pltpu.CompilerParams(vmem_limit_bytes=48 * 2**20),
        cost_estimate=pl.CostEstimate(flops=60 * 10**9, bytes_accessed=8 * 10**6, transcendentals=0),
        name="weight_grad",
    )(left, right)


def sorted_grad_kernel(on_rows, half, order_ref, left_ref, right_ref, own_ref, beside_ref, above_ref, x_ref, y_ref, acc_ref):
    index, step = pl.program_id(0), pl.program_id(1)
    value = dot(left_ref[...], right_ref[...], TN)

    @pl.when(step == 0)
    def _():
        acc_ref[...] = value

    @pl.when(step > 0)
    def _():
        acc_ref[...] += value

    def block(r):
        rows, cols = own_ref.shape
        size = rows if on_rows else cols
        place = pl.ds(pl.multiple_of(order_ref[r] * size, 128), size)
        part = acc_ref[place, :] if on_rows else acc_ref[:, place]
        return part.astype(own_ref.dtype)

    last = step == pl.num_programs(1) - 1

    @pl.when(last)
    def _():
        own_ref[...] = block(0)

    @pl.when(last & (index < half))
    def _():
        x_ref[0] = block(3)
        x_ref[1] = block(1)
        above_ref[...] = block(2)

    @pl.when(last & (index >= half))
    def _():
        y_ref[0] = block(3)
        y_ref[1] = block(2)
        beside_ref[...] = block(1)


def exchange_first(state):
    if len(state) == 1:
        return reduce_first(state[0])
    own, beside, above, x, y = state
    return own, beside, above, across(x, 1), across(y, 2)


def grad_exchange(left, right, order, on_rows, pick=0, stride=1):
    shards = lax.axis_size("shard")
    if shards != 4:
        return (weight_grad(left, right[pick::stride] if right.ndim == 3 else right, shards, on_rows),)
    count = left.shape[0] if left.ndim == 3 else right.shape[0] // stride
    half = count // 2
    total, size_m = left.shape[-2:]
    size_n = right.shape[-1]
    block = 1024
    spec = lambda a: (
        pl.BlockSpec((None, block, a.shape[-1]), lambda l, k, o: (l * stride + pick, k, 0))
        if a.ndim == 3
        else pl.BlockSpec((block, a.shape[-1]), lambda l, k, o: (k, 0))
    )
    shape = (size_m // 4, size_n) if on_rows else (size_m, size_n // 4)
    early = lambda l: jnp.minimum(l, half - 1)
    late = lambda l: jnp.maximum(l - half, 0)
    one = lambda f: pl.BlockSpec((None,) + shape, lambda l, k, o: (f(l), 0, 0))
    two = lambda f: pl.BlockSpec((2, None) + shape, lambda l, k, o: (0, f(l), 0, 0))
    low = lambda *lead: jax.ShapeDtypeStruct(lead + shape, jnp.bfloat16)
    own, beside, above, x, y = pl.pallas_call(
        lambda *refs: sorted_grad_kernel(on_rows, half, *refs),
        grid_spec=pltpu.PrefetchScalarGridSpec(
            num_scalar_prefetch=1,
            grid=(count, total // block),
            in_specs=[spec(left), spec(right)],
            out_specs=[one(lambda l: l), one(late), one(early), two(early), two(late)],
            scratch_shapes=[pltpu.VMEM((size_m, size_n), jnp.float32)],
        ),
        out_shape=[low(count), low(half), low(half), low(2, half), low(2, half)],
        compiler_params=pltpu.CompilerParams(vmem_limit_bytes=48 * 2**20),
        cost_estimate=pl.CostEstimate(flops=60 * 10**9, bytes_accessed=8 * 10**6, transcendentals=0),
        name="weight_grad",
    )(order, left, right)
    merged = lambda v: v.reshape((2 * half,) + shape)
    return own, beside, above, merged(x), merged(y)


def per_device(
    layer_input,
    out_cotangent,
    parents,
    routes,
    norm1_gain,
    qkv_weight,
    out_weight,
    norm2_gain,
    router_weight,
    gate_weight,
    up_weight,
    down_weight,
):
    low = jnp.bfloat16
    shards = lax.axis_size("shard")
    tokens, width = layer_input.shape
    expert_count = router_weight.shape[1]
    local_count = gate_weight.shape[0]
    chips = lax.axis_size("expert") // 2
    me = lax.axis_index("expert")
    core = me % 2
    order = shard_order()
    queries = HEADS * HEAD_DIM

    block = own_groups(qkv_weight, order)
    small = jnp.concatenate([router_weight, norm1_gain[:, None], norm2_gain[:, None]], axis=1).T
    small = gather_small(small)
    mixer_first = gather_first(block)
    router = jnp.pad(small[:expert_count], ((0, 128 - expert_count), (0, 0)))
    gain_one = small[expert_count].astype(jnp.float32)[None, :]
    gain_two = small[expert_count + 1].astype(jnp.float32)[None, :]
    activity = layer_input.astype(jnp.float32)
    hidden_one = (activity * inverse_rms(activity) * gain_one).astype(low)
    bias, cosine, sine = tree_tables(parents)
    mine = gather_second(mixer_first, 0)
    last_pieces, hidden_one, bias, cosine, sine = lax.optimization_barrier(
        (mine[3:], hidden_one, bias, cosine, sine)
    )
    mine = mine[:3] + last_pieces
    mixer_p = mine + [swap_core(p) for p in mine]
    block = lax.dynamic_slice_in_dim(out_weight, core * (out_weight.shape[0] // 2), out_weight.shape[0] // 2, 0)
    project_first = gather_first(after(block, *mine))

    cots = lax.all_gather(out_cotangent, "expert", axis=0, tiled=True)

    saved = None
    groups = []
    for call in range(2):
        groups.append(jnp.stack([2 * call + core, 2 * call + 1 - core]).astype(jnp.int32))
        saved = attend(hidden_one, mixer_p, call, order, groups[call], cosine, sine, bias, saved)
        if call == 0:
            project_first, saved = lax.optimization_barrier((project_first, saved))
            proj = gather_second(project_first, 0)
            near = swap_core(jnp.concatenate(proj[:3], axis=0))
            gates_first = gather_first(after(gate_weight, project_first))
    proj, near, gates_first, saved = lax.optimization_barrier((proj, near, gates_first, saved))
    far = [swap_core(p) for p in proj[3:]]
    ups_first = gather_first(after(up_weight, proj))
    proj = proj + [near] + far
    attended, query, keys, values, log_total = saved
    resid, gates, sent_rows = project(
        attended, layer_input, routes, gain_two, router, expert_count, proj, len(mixer_p) // 2, order
    )
    onward = next_chip(sent_rows)
    ups_first, sent_rows = lax.optimization_barrier((ups_first, sent_rows))
    gates_p = gather_second(gates_first, 0)
    ups_first, down_block = lax.optimization_barrier((ups_first, after(down_weight, *gates_p)))
    downs_first = gather_first(down_block, True)
    ups_p = gather_second(ups_first, 0)
    downs_p = gather_second(downs_first, 0)
    rows = [sent_rows]
    rows.append(onward)
    beside = swap_core(rows[0])
    rows[0], rows[1], beside = lax.optimization_barrier((rows[0], rows[1], beside))
    kept = total = None
    for step in range(chips):
        ahead = next_chip(rows[step + 1]) if step + 2 < chips else None
        beside_next = swap_core(rows[step + 1]) if step + 1 < chips else None
        here = rows[step]
        if step > 1:
            here, total = lax.optimization_barrier((here, total))
        sent = next_chip(total) if step > 1 else None
        place = jnp.stack([(me - 2 * step) % (2 * chips), (me - 2 * step) % (2 * chips) ^ 1, me])
        parts, kept = expert_chunk(
            order, place.astype(jnp.int32), here, beside, cots, gates_p, ups_p, downs_p, expert_count, kept
        )
        parts, kept, ahead, beside, sent = lax.optimization_barrier((parts, kept, ahead, beside_next, sent))
        if ahead is not None:
            rows.append(ahead)
        pair = (parts[0], swap_core(parts[1]))
        if step == 0:
            last = pair
        else:
            total = add_low(*pair, *(() if sent is None else (sent,)))
    out_all, all_rows, all_mid, all_sides = kept
    all_rows, total = lax.optimization_barrier((all_rows, total))
    sent = next_chip(total)
    gate_state = grad_exchange(all_rows, all_sides, order, True, 0, 2)
    gate_done, all_rows = lax.optimization_barrier((gate_state[0], all_rows))
    gate_state = exchange_first((gate_done,) + gate_state[1:])
    up_state = grad_exchange(all_rows, all_sides, order, True, 1, 2)
    sent, up_done, gate_state = lax.optimization_barrier((sent, up_state[0], gate_state))
    up_state = exchange_first((up_done,) + up_state[1:])
    branch_out = lax.psum_scatter(after(out_all, sent), "expert", scatter_dimension=0, tiled=True)
    grad_branch, grad_resid, out_mine, out_other = turn(
        expert_count, order, *last, sent, sent_rows, gates, resid, out_cotangent, attended, gain_two, router
    )
    grad_branch, up_state, out_other = lax.optimization_barrier((grad_branch, up_state, out_other))
    gate_state, up_state = reduce_second(gate_state), reduce_second(up_state)
    out_sent = swap_core(out_other)
    backward = lambda call, branch, *more: attend_back(
        call, branch, hidden_one, proj, mixer_p, order, groups[call],
        query, keys, values, log_total, cosine, sine, bias, *more,
    )
    wide, other, part = backward(0, grad_branch)
    grad_branch, wide, other, part, out_mine, out_sent, gate_state, up_state = lax.optimization_barrier(
        (grad_branch, wide, other, part, out_mine, out_sent, gate_state, up_state)
    )
    state_one = fold(order, wide, swap_core(other), out_mine, out_sent)
    grad_branch, folded = lax.optimization_barrier((grad_branch, state_one[0]))
    state_one = (folded,) + state_one[1:]
    wide, other, grad_input = backward(1, grad_branch, part, layer_input, grad_resid, gain_one)
    wide, other, grad_input, state_one, all_mid = lax.optimization_barrier(
        (wide, other, grad_input, state_one, all_mid)
    )
    state_one = reduce_second(state_one)
    state_two = fold(order, wide, swap_core(other))
    folded, state_one = lax.optimization_barrier((state_two[0], state_one))
    state_two = (folded,) + state_two[1:]
    one = reduce_last(state_one)
    all_mid, one, folded = lax.optimization_barrier((all_mid, one, state_two[0]))
    state_two = (folded,) + state_two[1:]
    one = chips_send(one)
    down_state = grad_exchange(all_mid, cots, order, False)
    kernel_done, state_two, one, gate_state, up_state = lax.optimization_barrier(
        (down_state[0], state_two, one, gate_state, up_state)
    )
    down_state = (kernel_done,) + down_state[1:]
    state_two = reduce_second(state_two)
    one = chips_gather(one)
    state_two, one, down_state = lax.optimization_barrier((state_two, one, down_state))
    two = chips_send(reduce_last(state_two))
    down_state = exchange_first(down_state)
    one = chips_order(one)
    two, down_state, one = lax.optimization_barrier((two, down_state, one))
    two = chips_gather(two)
    down_state = reduce_second(down_state)
    two, down_state, one = lax.optimization_barrier((two, down_state, one))
    two = chips_order(two)
    one = (one, swap_core(one))
    two = (two, swap_core(two))
    grad_gate = reduce_last(gate_state, jnp.float32)
    grad_up = reduce_last(up_state, jnp.float32)
    grad_down = reduce_last(down_state, jnp.float32)
    output = (resid + branch_out.astype(jnp.float32)).astype(low)
    grad_mixer, grad_projector, grad_router, grad_gain_two, grad_gain_one = finish(
        expert_count, order, one, two
    )
    return (
        output,
        grad_input,
        grad_gain_one[0],
        grad_mixer,
        grad_projector,
        grad_gain_two[0],
        grad_router.T,
        grad_gate,
        grad_up,
        grad_down,
    )


def solution(mesh):
    return jax.shard_map(
        per_device,
        mesh=mesh,
        in_specs=(
            P(("expert", "shard"), None),
            P(("expert", "shard"), None),
            P(("expert", "shard")),
            P(("expert", "shard"), None),
            P("shard"),
            P("shard", None),
            P("shard", None),
            P("shard"),
            P("shard", None),
            P("expert", "shard", None),
            P("expert", "shard", None),
            P("expert", None, "shard"),
        ),
        out_specs=(
            P(("expert", "shard"), None),
            P(("expert", "shard"), None),
            P("shard"),
            P("shard", None),
            P("shard", None),
            P("shard"),
            P("shard", None),
            P("expert", "shard", None),
            P("expert", "shard", None),
            P("expert", None, "shard"),
        ),
        check_vma=False,
    )
```

```python
import jax
import jax.numpy as jnp
from jax import lax
from jax.experimental import pallas as pl
from jax.experimental.pallas import tpu as pltpu
from jax.sharding import PartitionSpec as P

HEADS = 24
KV_HEADS = 8
HEAD_DIM = 64
SEG = 128

EPSILON = 1e-06
THETA = 10000.0
NEGATIVE = -1e30

NT = (((1,), (1,)), ((), ()))
NN = (((1,), (0,)), ((), ()))
TN = (((0,), (0,)), ((), ()))
def dot(left, right, dims):
    return lax.dot_general(left, right, dims, preferred_element_type=jnp.float32)

def turned(values):
    lane = lax.broadcasted_iota(jnp.int32, values.shape, 1)
    first = lane % HEAD_DIM < HEAD_DIM // 2
    ahead = pltpu.roll(values, 128 - HEAD_DIM // 2, 1)
    behind = pltpu.roll(values, HEAD_DIM // 2, 1)
    return jnp.where(first, -ahead, behind)


def tree_tables(parents):
    segs = parents.shape[0]
    ids = jnp.arange(segs, dtype=jnp.int32)
    pointer = ids
    ancestry = jnp.zeros((segs, segs), jnp.bool_)
    for _ in range(segs):
        landed = pointer[:, None] == ids[None, :]
        ancestry = ancestry | landed
        pointer = jnp.sum(jnp.where(landed, parents[None, :], 0), axis=1)
    depth = jnp.sum(ancestry.astype(jnp.float32), axis=1) - 1.0
    token_ids = jnp.arange(segs * SEG, dtype=jnp.int32)
    positions = jnp.repeat(depth, SEG) * SEG + (token_ids % SEG).astype(jnp.float32)
    reach = jnp.repeat(jnp.repeat(ancestry.astype(jnp.float32), SEG, axis=0), SEG, axis=1)
    allowed = (reach > 0.5) & (token_ids[None, :] <= token_ids[:, None])
    half = HEAD_DIM // 2
    frequency = THETA ** (-(jnp.arange(half, dtype=jnp.float32) * 2.0) / HEAD_DIM)
    angles = positions[:, None] * frequency[None, :]
    cosine, sine = jnp.cos(angles), jnp.sin(angles)
    return (
        jnp.where(allowed, 0.0, NEGATIVE),
        jnp.concatenate([cosine] * 4, axis=1),
        jnp.concatenate([sine] * 4, axis=1),
    )


def inverse_rms(values):
    return lax.rsqrt(jnp.mean(values * values, axis=1, keepdims=True) + EPSILON)


def swap_core(value):
    count = lax.axis_size("expert")
    return lax.ppermute(value, "expert", [(i, i ^ 1) for i in range(count)])


def next_chip(value):
    count = lax.axis_size("expert")
    return lax.ppermute(value, "expert", [(i, (i + 2) % count) for i in range(count)])


def across(value, mask):
    return lax.ppermute(value, "shard", [(i, i ^ mask) for i in range(4)])


def after(value, *earlier):
    return lax.optimization_barrier((value,) + earlier)[0]


def gather_first(block, on_lanes=False):
    if lax.axis_size("shard") != 4:
        if on_lanes:
            return [lax.all_gather(block, "shard", axis=block.ndim - 1, tiled=True)[None]]
        return [lax.all_gather(block, "shard", axis=0, tiled=False)]
    return [block[None], across(block, 1)[None], across(block, 2)[None]]


def gather_second(pieces, split):
    if len(pieces) == 1:
        return pieces
    axis = split + 1
    half = pieces[1].shape[axis] // 2
    first = lax.slice_in_dim(pieces[2], 0, half, axis=axis)
    last = lax.slice_in_dim(pieces[1], half, 2 * half, axis=axis)
    return pieces + [across(first, 1), across(last, 2)]


def gather_small(value):
    if lax.axis_size("shard") != 4:
        return lax.all_gather(value, "shard", axis=1, tiled=True)
    me = lax.axis_index("shard")
    rows = value.shape[0]
    near = jnp.concatenate([value, across(value, 1)])
    far = across(near, 2)
    parts = [near[:rows], near[rows:], far[:rows], far[rows:]]
    odd = me % 2 == 1
    parts = [jnp.where(odd, parts[i ^ 1], parts[i]) for i in range(4)]
    high = me >= 2
    parts = [jnp.where(high, parts[i ^ 2], parts[i]) for i in range(4)]
    return jnp.concatenate(parts, axis=1)


def own_groups_kernel(order_ref, query_ref, key_ref, value_ref, out_ref):
    out_ref[:, :384] = query_ref[...]
    out_ref[:, 384:512] = key_ref[...]
    out_ref[:, 512:] = value_ref[...]


def own_groups(weight, order):
    rows = weight.shape[0]
    last = order.shape[0] - 1
    spec = lambda w, at: pl.BlockSpec((rows, w), lambda j, o: (0, at + 2 * j + o[last]))
    return pl.pallas_call(
        own_groups_kernel,
        grid_spec=pltpu.PrefetchScalarGridSpec(
            num_scalar_prefetch=1,
            grid=(2,),
            in_specs=[spec(384, 0), spec(128, 12), spec(128, 16)],
            out_specs=pl.BlockSpec((rows, 640), lambda j, o: (0, j)),
        ),
        out_shape=pltpu.HBM((rows, 1280), weight.dtype),
        cost_estimate=pl.CostEstimate(flops=10**8, bytes_accessed=10**6, transcendentals=0),
        name="own_groups",
    )(order, weight, weight, weight)


def shard_order():
    shards = lax.axis_size("shard")
    me = lax.axis_index("shard")
    core = lax.axis_index("expert") % 2
    if shards != 4:
        return jnp.concatenate([jnp.arange(shards, dtype=jnp.int32), core[None].astype(jnp.int32)])
    return jnp.stack([me, me ^ 1, me ^ 2, me ^ 3, me ^ 3, core]).astype(jnp.int32)


def add_low(*terms):
    total = terms[0].astype(jnp.float32)
    for term in terms[1:]:
        total = total + term.astype(jnp.float32)
    return total.astype(jnp.bfloat16)


def reduce_first(blocks):
    if lax.axis_size("shard") != 4:
        return (lax.psum_scatter(blocks, "shard", scatter_dimension=0, tiled=False),)
    me = lax.axis_index("shard")
    own, beside, above, far = (
        lax.dynamic_index_in_dim(blocks, me ^ r, 0, keepdims=False) for r in range(4)
    )
    half = own.shape[0] // 2
    from_x = across(jnp.concatenate([far[:half], beside[:half]]), 1)
    from_y = across(jnp.concatenate([far[half:], above[half:]]), 2)
    return own, beside[half:], above[:half], from_x, from_y


def reduce_second(state):
    if len(state) == 1:
        return state
    own, beside, above, from_x, from_y = state
    half = own.shape[0] // 2
    last_x = across(add_low(beside, from_y[:half]), 1)
    last_y = across(add_low(above, from_x[:half]), 2)
    return own, from_x, from_y, last_x, last_y


def reduce_last(state, dtype=jnp.bfloat16):
    if len(state) == 1:
        return state[0].astype(dtype)
    own, from_x, from_y, last_x, last_y = (v.astype(jnp.float32) for v in state)
    half = own.shape[0] // 2
    low_half, high_half = own[:half] + from_x[half:] + last_y, own[half:] + last_x + from_y[half:]
    return jnp.concatenate([low_half, high_half]).astype(dtype)


def chip_ahead(value, distance):
    count = lax.axis_size("expert")
    return lax.ppermute(value, "expert", [(i, (i + 2 * distance) % count) for i in range(count)])


def chips_send(value):
    chips = lax.axis_size("expert") // 2
    z = lax.axis_index("expert") // 2
    size = value.shape[0] // chips
    part = lambda d: lax.dynamic_slice_in_dim(value, (z + d) % chips * size, size, 0)
    return [part(0)] + [chip_ahead(part(d), d) for d in range(1, chips)]


def chips_gather(parts):
    mine = add_low(*parts)
    return [mine] + [chip_ahead(mine, d) for d in range(1, len(parts))]


def chips_order(parts):
    chips = len(parts)
    z = lax.axis_index("expert") // 2
    size = parts[0].shape[0]
    onward = [parts[-j % chips] for j in range(chips)]
    return lax.dynamic_slice_in_dim(
        jnp.concatenate(onward + onward[:-1]), (chips - z) % chips * size, chips * size, 0
    )


def piece_copies(pieces, order_ref, target, sem, axis, split, base=0, stride=None, window=None):
    copies = []
    slot = 0
    block = pieces[0].shape[1:]
    stride = block[axis] if stride is None else stride
    align = 128 if axis == len(block) - 1 else 16
    for piece in pieces:
        for c in range(piece.shape[0]):
            shape = piece.shape[1:]
            start = [0] * len(shape)
            if slot == 4 and shape[split] < block[split]:
                start[split] = block[split] - shape[split]
            start[axis] = pl.multiple_of(order_ref[slot] * stride + base + start[axis], align)
            index = tuple(pl.ds(first, size) for first, size in zip(start, shape))
            source = piece.at[c]
            if window is not None:
                cols = shape[-1] // 2
                source = source.at[:, window * cols : (window + 1) * cols]
                index = index[:-1] + (slice(None),)
            copies.append(pltpu.make_async_copy(source, target.at[index], sem))
            slot += 1
    return copies


def attend_kernel(count, call, order_ref, group_ref, hidden_ref, cos_ref, sin_ref, bias_ref, *rest):
    mine, other = rest[:count], rest[count : 2 * count]
    att_ref, q_ref, k_ref, v_ref, lse_ref, weight_ref, sems = rest[-7:]
    step = pl.program_id(0)
    first = piece_copies(mine, order_ref, weight_ref.at[0], sems.at[0], 0, 0, window=call)
    second = piece_copies(other, order_ref, weight_ref.at[1], sems.at[1], 0, 0, window=call)

    @pl.when(step == 0)
    def _():
        for copy in first + second:
            copy.start()
        for copy in first:
            copy.wait()

    @pl.when(step == 1)
    def _():
        for copy in second:
            copy.wait()

    hidden = hidden_ref[...]
    cosine, sine = cos_ref[...], sin_ref[...]
    mixed = dot(hidden, weight_ref[step], NN)
    low = jnp.bfloat16
    scaling = HEAD_DIM ** (-0.5)
    for p in range(3):
        part = mixed[:, 128 * p : 128 * p + 128]
        turned_part = (part * cosine + turned(part) * sine).astype(low)
        q_ref[:, 128 * p : 128 * p + 128] = turned_part * scaling
    part = mixed[:, 384:512]
    k_ref[...] = (part * cosine + turned(part) * sine).astype(low)
    v_ref[...] = mixed[:, 512:640].astype(low)
    tokens = hidden.shape[0]
    for seg in range(tokens // SEG):
        rows = pl.ds(seg * SEG, SEG)
        span = (seg + 1) * SEG
        bias = bias_ref[rows, :span]
        keys = [k_ref[:span, HEAD_DIM * kv : HEAD_DIM * (kv + 1)] for kv in range(2)]
        vals = [v_ref[:span, HEAD_DIM * kv : HEAD_DIM * (kv + 1)] for kv in range(2)]
        queries = [q_ref[rows, HEAD_DIM * h : HEAD_DIM * (h + 1)] for h in range(6)]
        scores = [dot(queries[h], keys[h // 3], NT) + bias for h in range(6)]
        highest = [jnp.max(v, axis=1, keepdims=True) for v in scores]
        powers = [jnp.exp(v - m) for v, m in zip(scores, highest)]
        totals = [jnp.sum(v, axis=1, keepdims=True) for v in powers]
        probs = [(v * (1.0 / t)).astype(low) for v, t in zip(powers, totals)]
        outs = [dot(v, vals[h // 3], NN) for h, v in enumerate(probs)]
        logs = [m + jnp.log(t) for m, t in zip(highest, totals)]
        att_ref[rows, :] = jnp.concatenate(outs, axis=1).astype(low)
        lse_ref[rows, :] = jnp.concatenate(logs + [logs[-1]] * 2, axis=1)


def attend(hidden, mixer_p, call, order, groups, cosine, sine, bias, kept):
    tokens, width = hidden.shape
    low = jnp.bfloat16
    whole = lambda a: pl.BlockSpec(a.shape, lambda j, o, g: (0, 0))
    anywhere = pl.BlockSpec(memory_space=pltpu.HBM)
    col = lambda w: pl.BlockSpec((tokens, w), lambda j, o, g: (0, g[j]))
    shape = lambda w: pltpu.HBM((tokens, w), low)
    operands = [order, groups, hidden, cosine, sine, bias, *mixer_p]
    in_specs = [whole(hidden), whole(cosine), whole(sine), whole(bias)]
    in_specs += [anywhere] * len(mixer_p)
    aliases = {}
    if kept is not None:
        aliases = {len(operands) + i: i for i in range(5)}
        operands += list(kept)
        in_specs += [anywhere] * 5
    cols = mixer_p[0].shape[-1] // 2
    return pl.pallas_call(
        lambda *refs: attend_kernel(len(mixer_p) // 2, call, *refs),
        grid_spec=pltpu.PrefetchScalarGridSpec(
            num_scalar_prefetch=2,
            grid=(2,),
            in_specs=in_specs,
            out_specs=[col(384), col(384), col(128), col(128)]
            + [pl.BlockSpec((None, tokens, 8), lambda j, o, g: (g[j], 0, 0))],
            scratch_shapes=[pltpu.VMEM((2, width, cols), low), pltpu.SemaphoreType.DMA((2,))],
        ),
        out_shape=[shape(1536), shape(1536), shape(512), shape(512)]
        + [pltpu.HBM((4, tokens, 8), jnp.float32)],
        input_output_aliases=aliases,
        compiler_params=pltpu.CompilerParams(vmem_limit_bytes=40 * 2**20),
        cost_estimate=pl.CostEstimate(flops=48 * 10**9, bytes_accessed=8 * 10**6, transcendentals=0),
        name="attend",
    )(*operands)


def projector_copies(count, pieces, order_ref, target, sem):
    rows = pieces[0].shape[1]
    slots = order_ref.shape[0] - 1
    core = order_ref[slots]
    copies = piece_copies(pieces[:count], order_ref, target, sem, 0, 0, core * rows, 2 * rows)
    return copies + piece_copies(
        pieces[count:], order_ref, target, sem, 0, 0, (1 - core) * rows, 2 * rows
    )


def row_to_column(row, lane):
    low = jnp.bfloat16
    pick = (lax.broadcasted_iota(jnp.int32, (8, 128), 1) == lane) & (
        lax.broadcasted_iota(jnp.int32, (8, 128), 0) == 0
    )
    pick = pick.astype(jnp.float32).astype(low)
    rows = jnp.broadcast_to(row, (8, row.shape[1]))
    high = rows.astype(low)
    rest = (rows - high.astype(jnp.float32)).astype(low)
    return (dot(high, pick, TN) + dot(rest, pick, TN)).astype(low)


def attend_back_kernel(mine, counts, call, group_ref, order_ref, branch_ref, hidden_ref, q_ref, k_ref, v_ref, lse_ref, cos_ref, sin_ref, bias_ref, *rest):
    first, second = counts
    pieces, mixer_p = rest[:first], rest[first : first + second]
    rest = rest[first + second :]
    if call:
        part_ref, x_ref, resid_ref, gain_ref = rest[:4]
        rest = rest[4:]
    wide_refs, input_ref = rest[:2], rest[2]
    proj_ref, weight_ref, mixed_ref, grad_ref, dk_ref, dv_ref, total_ref, sems = rest[3:]
    step = pl.program_id(0)
    load = projector_copies(mine, pieces, order_ref, proj_ref, sems.at[0])
    half = second // 2
    more = [
        piece_copies(mixer_p[c * half : (c + 1) * half], order_ref, weight_ref.at[c], sems.at[1 + c], 0, 0, window=call)
        for c in range(2)
    ]

    @pl.when(step == 0)
    def _():
        for copy in load + more[0] + more[1]:
            copy.start()
        for copy in load:
            copy.wait()

    group = group_ref[step]
    low = jnp.bfloat16
    rows = pl.ds(pl.multiple_of(group * 384, 128), 384)
    grad_ref[...] = dot(branch_ref[...], proj_ref[rows, :], NT).astype(low)
    cosine, sine = cos_ref[...], sin_ref[...]
    scaling = HEAD_DIM ** (-0.5)
    tokens = branch_ref.shape[0]
    for seg in reversed(range(tokens // SEG)):
        rows = pl.ds(seg * SEG, SEG)
        span = (seg + 1) * SEG
        bias = bias_ref[rows, :span]
        part = lambda ref, r, h: ref[r, HEAD_DIM * h : HEAD_DIM * (h + 1)]
        keys = [part(k_ref, pl.ds(0, span), kv) for kv in range(2)]
        vals = [part(v_ref, pl.ds(0, span), kv) for kv in range(2)]
        queries = [part(q_ref, rows, h) for h in range(6)]
        grads = [part(grad_ref, rows, h) for h in range(6)]
        scores = [dot(queries[h], keys[h // 3], NT) + bias for h in range(6)]
        gprobs = [dot(grads[h], vals[h // 3], NT) for h in range(6)]
        probs = [jnp.exp(v - lse_ref[rows, h : h + 1]) for h, v in enumerate(scores)]
        centres = [jnp.sum(p * g, axis=1, keepdims=True) for p, g in zip(probs, gprobs)]
        gscore = [(p * (g - c)).astype(low) for p, g, c in zip(probs, gprobs, centres)]
        probs = [p.astype(low) for p in probs]
        gqs = [dot(v, keys[h // 3], NN) * scaling for h, v in enumerate(gscore)]
        three = lambda values, kv: jnp.concatenate(values[3 * kv : 3 * kv + 3], 0)
        gks = [dot(three(gscore, kv), three(queries, kv), TN) for kv in range(2)]
        gvs = [dot(three(probs, kv), three(grads, kv), TN) for kv in range(2)]
        gq = jnp.concatenate(gqs, axis=1)
        cos_rows, sin_rows = cosine[seg * SEG : span], sine[seg * SEG : span]
        for p in range(3):
            part = gq[:, 128 * p : 128 * p + 128]
            mixed_ref[rows, 128 * p : 128 * p + 128] = (
                part * cos_rows - turned(part * sin_rows)
            ).astype(low)
        gk = jnp.concatenate(gks, axis=1)
        gv = jnp.concatenate(gvs, axis=1)
        if span == tokens:
            dk_ref[...] = gk
            dv_ref[...] = gv
        else:
            dk_ref[:span, :] += gk
            dv_ref[:span, :] += gv
    gk = dk_ref[...]
    mixed_ref[:, 384:512] = (gk * cosine - turned(gk * sine)).astype(low)
    mixed_ref[:, 512:640] = dv_ref[...].astype(low)
    for c in range(2):

        @pl.when(step == c)
        def _():
            for copy in more[c]:
                copy.wait()

    wide = dot(hidden_ref[...], mixed_ref[...], TN).astype(low)
    part = dot(mixed_ref[...], weight_ref[step], NT)
    for c in range(2):

        @pl.when(step == c)
        def _():
            wide_refs[c][:, :640] = wide

    if not call:

        @pl.when(step == 0)
        def _():
            input_ref[...] = part

        @pl.when(step > 0)
        def _():
            input_ref[...] += part

        return

    @pl.when(step == 0)
    def _():
        total_ref[...] = part + part_ref[...]

    @pl.when(step > 0)
    def _():
        value = x_ref[...].astype(jnp.float32)
        scale = lax.rsqrt(jnp.mean(value * value, axis=1, keepdims=True) + EPSILON)
        normed = value * scale
        grad = total_ref[...] + part
        product = grad * normed
        gains = row_to_column(jnp.sum(product, axis=0, keepdims=True), 0)
        for ref in wide_refs:
            ref[:, 640:] = gains
        grad = grad * gain_ref[...]
        mean = jnp.mean(grad * normed, axis=1, keepdims=True)
        input_ref[...] = (resid_ref[...] + scale * (grad - normed * mean)).astype(low)


def attend_back(call, branch, hidden, proj, mixer_p, order, groups, q, k, v, lse, cosine, sine, bias, *more):
    tokens, width = branch.shape
    low = jnp.bfloat16
    whole = lambda a: pl.BlockSpec(a.shape, lambda j, g, o: (0, 0))
    col = lambda w: pl.BlockSpec((tokens, w), lambda j, g, o: (0, g[j]))
    cols = mixer_p[0].shape[-1] // 2
    mine = len(mixer_p) // 2
    wide = jax.ShapeDtypeStruct((width, cols + 128 * call), low)
    given = jax.ShapeDtypeStruct((tokens, width), low if call else jnp.float32)
    return pl.pallas_call(
        lambda *refs: attend_back_kernel(mine, (len(proj), len(mixer_p)), call, *refs),
        grid_spec=pltpu.PrefetchScalarGridSpec(
            num_scalar_prefetch=2,
            grid=(2,),
            in_specs=[whole(branch), whole(hidden), col(384), col(128), col(128)]
            + [pl.BlockSpec((None, tokens, 8), lambda j, g, o: (g[j], 0, 0))]
            + [whole(cosine), whole(sine), whole(bias)]
            + [pl.BlockSpec(memory_space=pltpu.HBM)] * (len(proj) + len(mixer_p))
            + [whole(value) for value in more],
            out_specs=[whole(wide), whole(wide), whole(given)],
            scratch_shapes=[
                pltpu.VMEM((width, width), low),
                pltpu.VMEM((2, width, cols), low),
                pltpu.VMEM((tokens, cols), low),
                pltpu.VMEM((tokens, 384), low),
                pltpu.VMEM((tokens, 128), jnp.float32),
                pltpu.VMEM((tokens, 128), jnp.float32),
                pltpu.VMEM((tokens, width) if call else (8, 128), jnp.float32),
                pltpu.SemaphoreType.DMA((3,)),
            ],
        ),
        out_shape=[wide, wide, given],
        compiler_params=pltpu.CompilerParams(vmem_limit_bytes=58 * 2**20),
        cost_estimate=pl.CostEstimate(flops=60 * 10**9, bytes_accessed=8 * 10**6, transcendentals=0),
        name="attend_back",
    )(groups, order, branch, hidden, q, k, v, lse, cosine, sine, bias, *proj, *mixer_p, *more)


TILE = 256


def extra_rows(expert_count):
    return 8 if expert_count <= 24 else 16


def table_picks(expert_count):
    extra = extra_rows(expert_count)
    row = lax.broadcasted_iota(jnp.int32, (extra, 128), 0)
    lane = lax.broadcasted_iota(jnp.int32, (extra, 128), 1)
    return [
        (lane == row + block * extra).astype(jnp.float32).astype(jnp.bfloat16)
        for block in range(expert_count // extra)
    ]


def table_rows(values, picks, width):
    low = jnp.bfloat16
    high = values.astype(low)
    parts = (high, (values - high.astype(jnp.float32)).astype(low))
    rows = [dot(pick, value, NT).astype(low) for pick in picks for value in parts]
    left = width - TILE * len(rows)
    if left:
        rows.append(jnp.zeros((picks[0].shape[0], left), low))
    return jnp.concatenate(rows, axis=1)


def table_values(rows, picks):
    total = None
    for block, pick in enumerate(picks):
        for part in range(2):
            at = (2 * block + part) * TILE
            value = dot(rows[:, at : at + TILE], pick, TN)
            total = value if total is None else total + value
    return total


def project_kernel(mine, count, expert_count, order_ref, left_ref, x_ref, routes_ref, gain_ref, router_ref, *rest):
    pieces = rest[:count]
    resid_ref, gates_ref, rows_ref, weight_ref, sem = rest[count:]
    copies = projector_copies(mine, pieces, order_ref, weight_ref, sem)

    @pl.when(pl.program_id(0) == 0)
    def _():
        for copy in copies:
            copy.start()
        for copy in copies:
            copy.wait()

    low = jnp.bfloat16
    resid = x_ref[...].astype(jnp.float32) + dot(left_ref[...], weight_ref[...], NN)
    resid_ref[...] = resid
    scale = lax.rsqrt(jnp.mean(resid * resid, axis=1, keepdims=True) + EPSILON)
    hidden = (resid * scale * gain_ref[...]).astype(low)
    rows_ref[:TILE, :] = hidden
    logits = dot(hidden, router_ref[...], NT)
    lane = lax.broadcasted_iota(jnp.int32, logits.shape, 1)
    routed = lane == routes_ref[:, 0:1]
    for k in range(1, routes_ref.shape[1]):
        routed = routed | (lane == routes_ref[:, k : k + 1])
    logits = jnp.where(routed, logits, NEGATIVE)
    powers = jnp.exp(logits - jnp.max(logits, axis=1, keepdims=True))
    gates = powers / jnp.sum(powers, axis=1, keepdims=True)
    gates_ref[...] = gates
    rows_ref[TILE:, :] = table_rows(gates, table_picks(expert_count), hidden.shape[1])


def project(left, x, routes, gain, router, expert_count, proj, mine, order):
    tokens, width = left.shape
    tall = TILE + extra_rows(expert_count)
    tile = lambda w, h=TILE: pl.BlockSpec((h, w), lambda i, o: (i, 0))
    whole = lambda a: pl.BlockSpec(a.shape, lambda i, o: (0, 0))
    return pl.pallas_call(
        lambda *refs: project_kernel(mine, len(proj), expert_count, *refs),
        grid_spec=pltpu.PrefetchScalarGridSpec(
            num_scalar_prefetch=1,
            grid=(tokens // TILE,),
            in_specs=[tile(width), tile(width), tile(routes.shape[1]), whole(gain), whole(router)]
            + [pl.BlockSpec(memory_space=pltpu.HBM)] * len(proj),
            out_specs=[tile(width), tile(128), tile(width, tall)],
            scratch_shapes=[pltpu.VMEM((width, width), jnp.bfloat16), pltpu.SemaphoreType.DMA],
        ),
        out_shape=[
            jax.ShapeDtypeStruct((tokens, width), jnp.float32),
            jax.ShapeDtypeStruct((tokens, 128), jnp.float32),
            jax.ShapeDtypeStruct((tokens // TILE * tall, width), jnp.bfloat16),
        ],
        compiler_params=pltpu.CompilerParams(vmem_limit_bytes=40 * 2**20),
        cost_estimate=pl.CostEstimate(flops=30 * 10**9, bytes_accessed=8 * 10**6, transcendentals=0),
        name="project",
    )(order, left, x, routes, gain, router, *proj)


def turn_kernel(expert_count, order_ref, a_ref, b_ref, c_ref, rows_ref, gates_ref, resid_ref, cot_ref, left_ref, gain_ref, router_ref,
                branch_ref, grad_ref, mine_ref, other_ref, low_ref, small_ref, gains_ref):
    low = jnp.bfloat16
    step = pl.program_id(0)
    total = a_ref[...].astype(jnp.float32) + b_ref[...].astype(jnp.float32) + c_ref[...].astype(jnp.float32)
    gates = gates_ref[...]
    grad_gates = table_values(total[TILE:, :].astype(low), table_picks(expert_count))
    mean = jnp.sum(gates * grad_gates, axis=1, keepdims=True)
    grad_logits = gates * (grad_gates - mean)
    high = grad_logits.astype(low)
    rest = (grad_logits - high.astype(jnp.float32)).astype(low)
    grad = total[:TILE, :] + dot(high, router_ref[...], NN) + dot(rest, router_ref[...], NN)
    resid = resid_ref[...]
    scale = lax.rsqrt(jnp.mean(resid * resid, axis=1, keepdims=True) + EPSILON)
    normed = resid * scale
    hidden = rows_ref[:TILE, :]
    small = dot(hidden, jnp.concatenate([high, rest], axis=1), TN)
    small = small[:, :128] + small[:, 128:]
    gains = jnp.sum(grad * normed, axis=0, keepdims=True)
    grad = grad * gain_ref[...]
    mean = jnp.mean(grad * normed, axis=1, keepdims=True)
    grad = cot_ref[...].astype(jnp.float32) + scale * (grad - normed * mean)
    grad_ref[...] = grad
    branch = grad.astype(low)
    branch_ref[...] = branch
    low_ref[pl.ds(pl.multiple_of(step * TILE, TILE), TILE), :] = branch

    @pl.when(step == 0)
    def _():
        small_ref[...] = small
        gains_ref[...] = gains

    @pl.when(step > 0)
    def _():
        small_ref[...] += small
        gains_ref[...] += gains

    @pl.when(step == pl.num_programs(0) - 1)
    def _():
        core = order_ref[order_ref.shape[0] - 1]
        half = low_ref.shape[1] // 2
        left = left_ref[...]
        small = small_ref[...].astype(low) + row_to_column(gains_ref[...], expert_count)
        for ref, which in ((mine_ref, core), (other_ref, 1 - core)):
            part = low_ref[:, pl.ds(pl.multiple_of(which * half, 128), half)]
            ref[:, :half] = dot(left, part, TN).astype(low)
            ref[:, half:] = small


def turn(expert_count, order, a, b, c, rows, gates, resid, cots, left, gain, router):
    tokens, width = left.shape
    tall = TILE + extra_rows(expert_count)
    tile = lambda w, h=TILE: pl.BlockSpec((h, w), lambda i, o: (i, 0))
    whole = lambda a: pl.BlockSpec(a.shape, lambda i, o: (0, 0))
    half = jax.ShapeDtypeStruct((width, width // 2 + 128), jnp.bfloat16)
    return pl.pallas_call(
        lambda *refs: turn_kernel(expert_count, *refs),
        grid_spec=pltpu.PrefetchScalarGridSpec(
            num_scalar_prefetch=1,
            grid=(tokens // TILE,),
            in_specs=[tile(width, tall)] * 4 + [tile(128), tile(width), tile(width), whole(left)]
            + [whole(gain), whole(router)],
            out_specs=[tile(width), tile(width), whole(half), whole(half)],
            scratch_shapes=[
                pltpu.VMEM((tokens, width), jnp.bfloat16),
                pltpu.VMEM((width, 128), jnp.float32),
                pltpu.VMEM((1, width), jnp.float32),
            ],
        ),
        out_shape=[
            jax.ShapeDtypeStruct((tokens, width), jnp.bfloat16),
            jax.ShapeDtypeStruct((tokens, width), jnp.float32),
            half,
            half,
        ],
        compiler_params=pltpu.CompilerParams(vmem_limit_bytes=58 * 2**20),
        cost_estimate=pl.CostEstimate(flops=30 * 10**9, bytes_accessed=8 * 10**6, transcendentals=0),
        name="turn",
    )(order, a, b, c, rows, gates, resid, cots, left, gain, router)


def fold_kernel(pairs, order_ref, *refs):
    x_ref, y_ref, own_ref, beside_ref, above_ref = refs[2 * pairs :]
    step = pl.program_id(0)
    half = x_ref.shape[0] // 2
    low, high = slice(0, half), slice(half, 2 * half)
    places = (
        ((own_ref, low), (own_ref, high)),
        ((x_ref, high), (beside_ref, low)),
        ((above_ref, low), (y_ref, high)),
        ((x_ref, low), (y_ref, low)),
    )
    at = 0
    for i in range(pairs):
        value = refs[2 * i][...] + refs[2 * i + 1][...]
        columns = slice(at, at + value.shape[1])
        at += value.shape[1]
        for r, ((first, first_rows), (second, second_rows)) in enumerate(places):

            @pl.when(step == r)
            def _():
                first[first_rows, columns] = value[low]
                second[second_rows, columns] = value[high]


def fold(order, *operands):
    if lax.axis_size("shard") != 4:
        parts = [add_low(operands[i], operands[i + 1]) for i in range(0, len(operands), 2)]
        blocks = jnp.concatenate(parts, axis=1)
        return reduce_first(blocks.reshape(lax.axis_size("shard"), -1, blocks.shape[1]))
    rows = operands[0].shape[0] // 4
    columns = sum(v.shape[1] for v in operands[::2])
    given = [jax.ShapeDtypeStruct((n * rows // 2, columns), jnp.bfloat16) for n in (2, 2, 2, 1, 1)]
    x, y, own, beside, above = pl.pallas_call(
        lambda *refs: fold_kernel(len(operands) // 2, *refs),
        grid_spec=pltpu.PrefetchScalarGridSpec(
            num_scalar_prefetch=1,
            grid=(4,),
            in_specs=[pl.BlockSpec((rows, v.shape[1]), lambda i, o: (o[i], 0)) for v in operands],
            out_specs=[pl.BlockSpec(v.shape, lambda i, o: (0, 0)) for v in given],
        ),
        out_shape=given,
        compiler_params=pltpu.CompilerParams(vmem_limit_bytes=40 * 2**20),
        cost_estimate=pl.CostEstimate(flops=3 * 10**9, bytes_accessed=4 * 10**6, transcendentals=0),
        name="fold",
    )(order, *operands)
    return own, beside, above, across(x, 1), across(y, 2)


def finish_kernel(order_ref, one_mine, one_other, two_mine, two_other, mixer_ref, proj_ref, router_ref, second_ref, first_ref):
    lower = order_ref[order_ref.shape[0] - 1] == 0
    wide = jnp.float32
    half = proj_ref.shape[1] // 2
    groups = []
    for mine, other in ((one_mine, one_other), (two_mine, two_other)):
        a, b = mine[:, :640].astype(wide), other[:, :640].astype(wide)
        groups += [jnp.where(lower, a, b), jnp.where(lower, b, a)]
    for g, value in enumerate(groups):
        mixer_ref[:, 384 * g : 384 * (g + 1)] = value[:, :384]
        mixer_ref[:, 1536 + 128 * g : 1536 + 128 * (g + 1)] = value[:, 384:512]
        mixer_ref[:, 2048 + 128 * g : 2048 + 128 * (g + 1)] = value[:, 512:]
    a, b = one_mine[:, 640 : 640 + half].astype(wide), one_other[:, 640 : 640 + half].astype(wide)
    proj_ref[:, :half] = jnp.where(lower, a, b)
    proj_ref[:, half:] = jnp.where(lower, b, a)
    experts = router_ref.shape[0]
    size = (experts + 8, 128)
    pick = lax.broadcasted_iota(jnp.int32, size, 0) == lax.broadcasted_iota(jnp.int32, size, 1)
    pick = pick.astype(wide).astype(jnp.bfloat16)
    rows = dot(pick, one_mine[:, 640 + half :], NT)
    router_ref[...] = rows[:experts, :]
    second_ref[...] = rows[experts : experts + 1, :]
    first_ref[...] = dot(pick, two_mine[:, 640:], NT)[:1, :]


def finish(expert_count, order, one, two):
    rows = one[0].shape[0]
    block = 128 if rows % 128 == 0 else rows
    tall = [jax.ShapeDtypeStruct((rows, w), jnp.float32) for w in (2560, 1536)]
    flat = [jax.ShapeDtypeStruct((h, rows), jnp.float32) for h in (expert_count, 1, 1)]
    spec = lambda a: pl.BlockSpec((block, a.shape[1]), lambda i, o: (i, 0))
    flat_spec = lambda a: pl.BlockSpec((a.shape[0], block), lambda i, o: (0, i))
    operands = [*one, *two]
    return pl.pallas_call(
        finish_kernel,
        grid_spec=pltpu.PrefetchScalarGridSpec(
            num_scalar_prefetch=1,
            grid=(rows // block,),
            in_specs=[spec(v) for v in operands],
            out_specs=[spec(v) for v in tall] + [flat_spec(v) for v in flat],
        ),
        out_shape=tall + flat,
        cost_estimate=pl.CostEstimate(flops=10**9, bytes_accessed=4 * 10**6, transcendentals=0),
        name="finish",
    )(order, *operands)


def expert_kernel(counts, expert_count, order_ref, place_ref, xa_ref, u_ref, *rest):
    pieces, more = counts
    gates_p, ups_p, downs_p = (rest[i * pieces : (i + 1) * pieces] for i in range(3))
    rest = rest[3 * pieces + more :]
    (gt_ref, out_ref, x_ref, mid_ref, sides_ref, wg_ref, wu_ref, wd_ref, sems) = rest
    low = jnp.bfloat16
    extra = extra_rows(expert_count)
    step = pl.program_id(0)
    loads = [
        piece_copies(gates_p, order_ref, wg_ref, sems.at[0], 1, 0),
        piece_copies(ups_p, order_ref, wu_ref, sems.at[1], 1, 0),
        piece_copies(downs_p, order_ref, wd_ref, sems.at[2], 2, 0),
    ]

    @pl.when(step == 0)
    def _():
        for load in loads:
            for copy in load:
                copy.start()

    def arrive(number):
        @pl.when(step == 0)
        def _():
            for copy in loads[number]:
                copy.wait()

    rows, table, cots = xa_ref[:TILE, :], xa_ref[TILE:, :], u_ref[...]
    x_ref[...] = rows
    row = lax.broadcasted_iota(jnp.int32, (extra, 128), 0)
    lane = lax.broadcasted_iota(jnp.int32, (extra, 128), 1)
    expert = place_ref[1] * 2 + lane
    picks = []
    for block in range(expert_count // extra):
        hit = (lane < 2) & (row == expert - block * extra)
        picks.append(jnp.where(hit, 1.0, 0.0).astype(low))
    gates_wide = table_values(table, picks)
    arrive(0)
    gate_ins = [dot(rows, wg_ref[l], NN) for l in range(2)]
    arrive(1)
    up_ins = [dot(rows, wu_ref[l], NN) for l in range(2)]
    arrive(2)
    out = None
    taken = None
    sums = []
    for l in range(2):
        gates = gates_wide[:, l : l + 1]
        gate_in, up_in = gate_ins[l], up_ins[l]
        back = dot(cots, wd_ref[l], NT)
        sigma = 1.0 / (1.0 + jnp.exp(-gate_in))
        active = gate_in * sigma
        mid = active * up_in
        sums.append(jnp.sum(mid * back, axis=1, keepdims=True))
        mid_low = (mid * gates).astype(low)
        mid_ref[l] = mid_low
        part = dot(mid_low, wd_ref[l], NN)
        out = part if out is None else out + part
        back = back * gates
        grad_gate = (back * up_in * sigma * (1.0 + gate_in * (1.0 - sigma))).astype(low)
        grad_up = (back * active).astype(low)
        sides_ref[2 * l] = grad_gate
        sides_ref[2 * l + 1] = grad_up
        part = dot(grad_gate, wg_ref[l], NT) + dot(grad_up, wu_ref[l], NT)
        taken = part if taken is None else taken + part
    out_ref[...] = out.astype(low)
    gt_ref[:TILE, :] = taken.astype(low)
    wide = lax.broadcasted_iota(jnp.int32, (TILE, 128), 1)
    sums = jnp.where(wide == 0, sums[0], jnp.where(wide == 1, sums[1], 0.0))
    gt_ref[TILE:, :] = table_rows(sums, picks, rows.shape[1])


def expert_chunk(order, place, xa, cots, gates, ups, downs, expert_count, kept):
    total, width = cots.shape
    devices = lax.axis_size("expert")
    tokens = total // devices
    hidden = gates[0].shape[-1]
    steps = tokens // TILE
    low = jnp.bfloat16
    tall = TILE + extra_rows(expert_count)
    own = pl.BlockSpec((tall, width), lambda i, o, p: (i, 0))
    anywhere = pl.BlockSpec(memory_space=pltpu.HBM)
    big_row = pl.BlockSpec((TILE, width), lambda i, o, p: (p[0] * steps + i, 0))
    big = lambda n: pl.BlockSpec((n, TILE, hidden), lambda i, o, p: (0, p[0] * steps + i, 0))
    single = jax.ShapeDtypeStruct((steps * tall, width), low)
    shapes = [jax.ShapeDtypeStruct((total, width), low)] * 2
    shapes += [jax.ShapeDtypeStruct((n, total, hidden), low) for n in (2, 4)]
    operands = [order, place, xa, cots, *gates, *ups, *downs]
    in_specs = [own, big_row] + [anywhere] * (3 * len(gates))
    aliases = {}
    more = 0
    if kept is not None:
        more = len(shapes)
        aliases = {len(operands) + i: 1 + i for i in range(more)}
        operands += list(kept)
        in_specs += [anywhere] * more
    res = pl.pallas_call(
        lambda *refs: expert_kernel((len(gates), more), expert_count, *refs),
        grid_spec=pltpu.PrefetchScalarGridSpec(
            num_scalar_prefetch=2,
            grid=(steps,),
            in_specs=in_specs,
            out_specs=[own, big_row, big_row, big(2), big(4)],
            scratch_shapes=[
                pltpu.VMEM((2, width, hidden), low),
                pltpu.VMEM((2, width, hidden), low),
                pltpu.VMEM((2, hidden, width), low),
                pltpu.SemaphoreType.DMA((3,)),
            ],
        ),
        out_shape=[single] + shapes,
        input_output_aliases=aliases,
        compiler_params=pltpu.CompilerParams(vmem_limit_bytes=58 * 2**20),
        cost_estimate=pl.CostEstimate(flops=50 * 10**9, bytes_accessed=4 * 10**6, transcendentals=0),
        name="expert_chunk",
    )(*operands)
    return res[0], res[1:]


def wide_grad_kernel(on_rows, left_ref, right_ref, out_ref, acc_ref):
    step = pl.program_id(1)
    value = dot(left_ref[...], right_ref[...], TN)

    @pl.when(step == 0)
    def _():
        acc_ref[...] = value

    @pl.when(step > 0)
    def _():
        acc_ref[...] += value

    @pl.when(step == pl.num_programs(1) - 1)
    def _():
        rows, cols = out_ref.shape[-2:]
        for j in range(out_ref.shape[0]):
            if on_rows:
                part = acc_ref[j * rows : (j + 1) * rows, :]
            else:
                part = acc_ref[:, j * cols : (j + 1) * cols]
            out_ref[j] = part.astype(out_ref.dtype)


def weight_grad(left, right, parts, on_rows):
    count = left.shape[0] if left.ndim == 3 else right.shape[0]
    total, size_m = left.shape[-2:]
    size_n = right.shape[-1]
    block = 1024
    spec = lambda a: (
        pl.BlockSpec((None, block, a.shape[-1]), lambda l, k: (l, k, 0))
        if a.ndim == 3
        else pl.BlockSpec((block, a.shape[-1]), lambda l, k: (k, 0))
    )
    shape = (size_m // parts, size_n) if on_rows else (size_m, size_n // parts)
    return pl.pallas_call(
        lambda *refs: wide_grad_kernel(on_rows, *refs),
        grid=(count, total // block),
        in_specs=[spec(left), spec(right)],
        out_specs=pl.BlockSpec((parts, None) + shape, lambda l, k: (0, l, 0, 0)),
        out_shape=jax.ShapeDtypeStruct((parts, count) + shape, jnp.bfloat16),
        scratch_shapes=[pltpu.VMEM((size_m, size_n), jnp.float32)],
        compiler_params=pltpu.CompilerParams(vmem_limit_bytes=48 * 2**20),
        cost_estimate=pl.CostEstimate(flops=60 * 10**9, bytes_accessed=8 * 10**6, transcendentals=0),
        name="weight_grad",
    )(left, right)


def sorted_grad_kernel(on_rows, half, order_ref, left_ref, right_ref, own_ref, beside_ref, above_ref, x_ref, y_ref, acc_ref):
    index, step = pl.program_id(0), pl.program_id(1)
    value = dot(left_ref[...], right_ref[...], TN)

    @pl.when(step == 0)
    def _():
        acc_ref[...] = value

    @pl.when(step > 0)
    def _():
        acc_ref[...] += value

    def block(r):
        rows, cols = own_ref.shape
        size = rows if on_rows else cols
        place = pl.ds(pl.multiple_of(order_ref[r] * size, 128), size)
        part = acc_ref[place, :] if on_rows else acc_ref[:, place]
        return part.astype(own_ref.dtype)

    last = step == pl.num_programs(1) - 1

    @pl.when(last)
    def _():
        own_ref[...] = block(0)

    @pl.when(last & (index < half))
    def _():
        x_ref[0] = block(3)
        x_ref[1] = block(1)
        above_ref[...] = block(2)

    @pl.when(last & (index >= half))
    def _():
        y_ref[0] = block(3)
        y_ref[1] = block(2)
        beside_ref[...] = block(1)


def exchange_first(state):
    if len(state) == 1:
        return reduce_first(state[0])
    own, beside, above, x, y = state
    return own, beside, above, across(x, 1), across(y, 2)


def grad_exchange(left, right, order, on_rows, pick=0, stride=1):
    shards = lax.axis_size("shard")
    if shards != 4:
        return (weight_grad(left, right[pick::stride] if right.ndim == 3 else right, shards, on_rows),)
    count = left.shape[0] if left.ndim == 3 else right.shape[0] // stride
    half = count // 2
    total, size_m = left.shape[-2:]
    size_n = right.shape[-1]
    block = 1024
    spec = lambda a: (
        pl.BlockSpec((None, block, a.shape[-1]), lambda l, k, o: (l * stride + pick, k, 0))
        if a.ndim == 3
        else pl.BlockSpec((block, a.shape[-1]), lambda l, k, o: (k, 0))
    )
    shape = (size_m // 4, size_n) if on_rows else (size_m, size_n // 4)
    early = lambda l: jnp.minimum(l, half - 1)
    late = lambda l: jnp.maximum(l - half, 0)
    one = lambda f: pl.BlockSpec((None,) + shape, lambda l, k, o: (f(l), 0, 0))
    two = lambda f: pl.BlockSpec((2, None) + shape, lambda l, k, o: (0, f(l), 0, 0))
    low = lambda *lead: jax.ShapeDtypeStruct(lead + shape, jnp.bfloat16)
    own, beside, above, x, y = pl.pallas_call(
        lambda *refs: sorted_grad_kernel(on_rows, half, *refs),
        grid_spec=pltpu.PrefetchScalarGridSpec(
            num_scalar_prefetch=1,
            grid=(count, total // block),
            in_specs=[spec(left), spec(right)],
            out_specs=[one(lambda l: l), one(late), one(early), two(early), two(late)],
            scratch_shapes=[pltpu.VMEM((size_m, size_n), jnp.float32)],
        ),
        out_shape=[low(count), low(half), low(half), low(2, half), low(2, half)],
        compiler_params=pltpu.CompilerParams(vmem_limit_bytes=48 * 2**20),
        cost_estimate=pl.CostEstimate(flops=60 * 10**9, bytes_accessed=8 * 10**6, transcendentals=0),
        name="weight_grad",
    )(order, left, right)
    merged = lambda v: v.reshape((2 * half,) + shape)
    return own, beside, above, merged(x), merged(y)


def per_device(
    layer_input,
    out_cotangent,
    parents,
    routes,
    norm1_gain,
    qkv_weight,
    out_weight,
    norm2_gain,
    router_weight,
    gate_weight,
    up_weight,
    down_weight,
):
    low = jnp.bfloat16
    shards = lax.axis_size("shard")
    tokens, width = layer_input.shape
    expert_count = router_weight.shape[1]
    local_count = gate_weight.shape[0]
    chips = lax.axis_size("expert") // 2
    me = lax.axis_index("expert")
    core = me % 2
    order = shard_order()
    queries = HEADS * HEAD_DIM

    block = own_groups(qkv_weight, order)
    small = jnp.concatenate([router_weight, norm1_gain[:, None], norm2_gain[:, None]], axis=1).T
    small = gather_small(small)
    mixer_first = gather_first(block)
    router = jnp.pad(small[:expert_count], ((0, 128 - expert_count), (0, 0)))
    gain_one = small[expert_count].astype(jnp.float32)[None, :]
    gain_two = small[expert_count + 1].astype(jnp.float32)[None, :]
    activity = layer_input.astype(jnp.float32)
    hidden_one = (activity * inverse_rms(activity) * gain_one).astype(low)
    bias, cosine, sine = tree_tables(parents)
    mine = gather_second(mixer_first, 0)
    last_pieces, hidden_one, bias, cosine, sine = lax.optimization_barrier(
        (mine[3:], hidden_one, bias, cosine, sine)
    )
    mine = mine[:3] + last_pieces
    mixer_p = mine + [swap_core(p) for p in mine]
    block = lax.dynamic_slice_in_dim(out_weight, core * (out_weight.shape[0] // 2), out_weight.shape[0] // 2, 0)
    project_first = gather_first(after(block, *mine))

    cots = lax.all_gather(out_cotangent, "expert", axis=0, tiled=True)

    saved = None
    groups = []
    for call in range(2):
        groups.append(jnp.stack([2 * call + core, 2 * call + 1 - core]).astype(jnp.int32))
        saved = attend(hidden_one, mixer_p, call, order, groups[call], cosine, sine, bias, saved)
        if call == 0:
            project_first, saved = lax.optimization_barrier((project_first, saved))
            proj = gather_second(project_first, 0)
            near = swap_core(jnp.concatenate(proj[:3], axis=0))
            gates_first = gather_first(after(gate_weight, project_first))
    proj, near, gates_first, saved = lax.optimization_barrier((proj, near, gates_first, saved))
    far = [swap_core(p) for p in proj[3:]]
    ups_first = gather_first(after(up_weight, proj))
    proj = proj + [near] + far
    attended, query, keys, values, log_total = saved
    resid, gates, sent_rows = project(
        attended, layer_input, routes, gain_two, router, expert_count, proj, len(mixer_p) // 2, order
    )
    onward = next_chip(sent_rows)
    ups_first, sent_rows = lax.optimization_barrier((ups_first, sent_rows))
    gates_p = gather_second(gates_first, 0)
    ups_first, down_block = lax.optimization_barrier((ups_first, after(down_weight, *gates_p)))
    downs_first = gather_first(down_block, True)
    ups_p = gather_second(ups_first, 0)
    downs_p = gather_second(downs_first, 0)
    rows = [sent_rows]
    rows.append(onward)
    beside = swap_core(rows[0])
    rows[0], rows[1], beside = lax.optimization_barrier((rows[0], rows[1], beside))
    kept = total = None
    for step in range(chips):
        ahead = next_chip(rows[step + 1]) if step + 2 < chips else None
        beside_next = swap_core(rows[step + 1]) if step + 1 < chips else None
        here = rows[step]
        if step > 1:
            here, beside, total = lax.optimization_barrier((here, beside, total))
        sent = next_chip(total) if step > 1 else None
        source = (me - 2 * step) % (2 * chips)
        place = lambda at: jnp.stack([at, me]).astype(jnp.int32)
        run = lambda at, value, kept: expert_chunk(
            order, place(at), value, cots, gates_p, ups_p, downs_p, expert_count, kept
        )
        other, kept = run(source ^ 1, beside, kept)
        other = swap_core(other)
        mine, kept = run(source, here, kept)
        mine, kept, ahead, beside, sent, other = lax.optimization_barrier(
            (mine, kept, ahead, beside_next, sent, other)
        )
        if ahead is not None:
            rows.append(ahead)
        pair = (mine, other)
        if step == 0:
            last = pair
        else:
            total = add_low(*pair, *(() if sent is None else (sent,)))
    out_all, all_rows, all_mid, all_sides = kept
    all_rows, total = lax.optimization_barrier((all_rows, total))
    sent = next_chip(total)
    gate_state = grad_exchange(all_rows, all_sides, order, True, 0, 2)
    gate_done, all_rows = lax.optimization_barrier((gate_state[0], all_rows))
    gate_state = exchange_first((gate_done,) + gate_state[1:])
    up_state = grad_exchange(all_rows, all_sides, order, True, 1, 2)
    sent, up_done, gate_state = lax.optimization_barrier((sent, up_state[0], gate_state))
    up_state = exchange_first((up_done,) + up_state[1:])
    branch_out = lax.psum_scatter(after(out_all, sent), "expert", scatter_dimension=0, tiled=True)
    grad_branch, grad_resid, out_mine, out_other = turn(
        expert_count, order, *last, sent, sent_rows, gates, resid, out_cotangent, attended, gain_two, router
    )
    grad_branch, up_state, out_other = lax.optimization_barrier((grad_branch, up_state, out_other))
    gate_state, up_state = reduce_second(gate_state), reduce_second(up_state)
    out_sent = swap_core(out_other)
    backward = lambda call, branch, *more: attend_back(
        call, branch, hidden_one, proj, mixer_p, order, groups[call],
        query, keys, values, log_total, cosine, sine, bias, *more,
    )
    wide, other, part = backward(0, grad_branch)
    grad_branch, wide, other, part, out_mine, out_sent, gate_state, up_state = lax.optimization_barrier(
        (grad_branch, wide, other, part, out_mine, out_sent, gate_state, up_state)
    )
    state_one = fold(order, wide, swap_core(other), out_mine, out_sent)
    grad_branch, folded = lax.optimization_barrier((grad_branch, state_one[0]))
    state_one = (folded,) + state_one[1:]
    wide, other, grad_input = backward(1, grad_branch, part, layer_input, grad_resid, gain_one)
    wide, other, grad_input, state_one, all_mid = lax.optimization_barrier(
        (wide, other, grad_input, state_one, all_mid)
    )
    state_one = reduce_second(state_one)
    state_two = fold(order, wide, swap_core(other))
    folded, state_one = lax.optimization_barrier((state_two[0], state_one))
    state_two = (folded,) + state_two[1:]
    one = reduce_last(state_one)
    all_mid, one, folded = lax.optimization_barrier((all_mid, one, state_two[0]))
    state_two = (folded,) + state_two[1:]
    one = chips_send(one)
    down_state = grad_exchange(all_mid, cots, order, False)
    kernel_done, state_two, one, gate_state, up_state = lax.optimization_barrier(
        (down_state[0], state_two, one, gate_state, up_state)
    )
    down_state = (kernel_done,) + down_state[1:]
    state_two = reduce_second(state_two)
    one = chips_gather(one)
    state_two, one, down_state = lax.optimization_barrier((state_two, one, down_state))
    two = chips_send(reduce_last(state_two))
    down_state = exchange_first(down_state)
    one = chips_order(one)
    two, down_state, one = lax.optimization_barrier((two, down_state, one))
    two = chips_gather(two)
    down_state = reduce_second(down_state)
    two, down_state, one = lax.optimization_barrier((two, down_state, one))
    two = chips_order(two)
    one = (one, swap_core(one))
    two = (two, swap_core(two))
    grad_gate = reduce_last(gate_state, jnp.float32)
    grad_up = reduce_last(up_state, jnp.float32)
    grad_down = reduce_last(down_state, jnp.float32)
    output = (resid + branch_out.astype(jnp.float32)).astype(low)
    grad_mixer, grad_projector, grad_router, grad_gain_two, grad_gain_one = finish(
        expert_count, order, one, two
    )
    return (
        output,
        grad_input,
        grad_gain_one[0],
        grad_mixer,
        grad_projector,
        grad_gain_two[0],
        grad_router.T,
        grad_gate,
        grad_up,
        grad_down,
    )


def solution(mesh):
    return jax.shard_map(
        per_device,
        mesh=mesh,
        in_specs=(
            P(("expert", "shard"), None),
            P(("expert", "shard"), None),
            P(("expert", "shard")),
            P(("expert", "shard"), None),
            P("shard"),
            P("shard", None),
            P("shard", None),
            P("shard"),
            P("shard", None),
            P("expert", "shard", None),
            P("expert", "shard", None),
            P("expert", None, "shard"),
        ),
        out_specs=(
            P(("expert", "shard"), None),
            P(("expert", "shard"), None),
            P("shard"),
            P("shard", None),
            P("shard", None),
            P("shard"),
            P("shard", None),
            P("expert", "shard", None),
            P("expert", "shard", None),
            P("expert", None, "shard"),
        ),
        check_vma=False,
    )
```

```python
import jax
import jax.numpy as jnp
from jax import lax
from jax.experimental import pallas as pl
from jax.experimental.pallas import tpu as pltpu
from jax.sharding import PartitionSpec as P

HEADS = 24
KV_HEADS = 8
HEAD_DIM = 64
SEG = 128

EPSILON = 1e-06
THETA = 10000.0
NEGATIVE = -1e30

NT = (((1,), (1,)), ((), ()))
NN = (((1,), (0,)), ((), ()))
TN = (((0,), (0,)), ((), ()))
def dot(left, right, dims):
    return lax.dot_general(left, right, dims, preferred_element_type=jnp.float32)

def turned(values):
    lane = lax.broadcasted_iota(jnp.int32, values.shape, 1)
    first = lane % HEAD_DIM < HEAD_DIM // 2
    ahead = pltpu.roll(values, 128 - HEAD_DIM // 2, 1)
    behind = pltpu.roll(values, HEAD_DIM // 2, 1)
    return jnp.where(first, -ahead, behind)


def tree_tables(parents):
    segs = parents.shape[0]
    ids = jnp.arange(segs, dtype=jnp.int32)
    pointer = ids
    ancestry = jnp.zeros((segs, segs), jnp.bool_)
    for _ in range(segs):
        landed = pointer[:, None] == ids[None, :]
        ancestry = ancestry | landed
        pointer = jnp.sum(jnp.where(landed, parents[None, :], 0), axis=1)
    depth = jnp.sum(ancestry.astype(jnp.float32), axis=1) - 1.0
    token_ids = jnp.arange(segs * SEG, dtype=jnp.int32)
    positions = jnp.repeat(depth, SEG) * SEG + (token_ids % SEG).astype(jnp.float32)
    reach = jnp.repeat(jnp.repeat(ancestry.astype(jnp.float32), SEG, axis=0), SEG, axis=1)
    allowed = (reach > 0.5) & (token_ids[None, :] <= token_ids[:, None])
    half = HEAD_DIM // 2
    frequency = THETA ** (-(jnp.arange(half, dtype=jnp.float32) * 2.0) / HEAD_DIM)
    angles = positions[:, None] * frequency[None, :]
    cosine, sine = jnp.cos(angles), jnp.sin(angles)
    return (
        jnp.where(allowed, 0.0, NEGATIVE),
        jnp.concatenate([cosine] * 4, axis=1),
        jnp.concatenate([sine] * 4, axis=1),
    )


def inverse_rms(values):
    return lax.rsqrt(jnp.mean(values * values, axis=1, keepdims=True) + EPSILON)


def swap_core(value):
    count = lax.axis_size("expert")
    return lax.ppermute(value, "expert", [(i, i ^ 1) for i in range(count)])


def next_chip(value):
    count = lax.axis_size("expert")
    return lax.ppermute(value, "expert", [(i, (i + 2) % count) for i in range(count)])


def across(value, mask):
    return lax.ppermute(value, "shard", [(i, i ^ mask) for i in range(4)])


def after(value, *earlier):
    return lax.optimization_barrier((value,) + earlier)[0]


def gather_first(block, on_lanes=False):
    if lax.axis_size("shard") != 4:
        if on_lanes:
            return [lax.all_gather(block, "shard", axis=block.ndim - 1, tiled=True)[None]]
        return [lax.all_gather(block, "shard", axis=0, tiled=False)]
    return [block[None], across(block, 1)[None], across(block, 2)[None]]


def gather_second(pieces, split):
    if len(pieces) == 1:
        return pieces
    axis = split + 1
    half = pieces[1].shape[axis] // 2
    first = lax.slice_in_dim(pieces[2], 0, half, axis=axis)
    last = lax.slice_in_dim(pieces[1], half, 2 * half, axis=axis)
    return pieces + [across(first, 1), across(last, 2)]


def gather_small(value):
    if lax.axis_size("shard") != 4:
        return lax.all_gather(value, "shard", axis=1, tiled=True)
    me = lax.axis_index("shard")
    rows = value.shape[0]
    near = jnp.concatenate([value, across(value, 1)])
    far = across(near, 2)
    parts = [near[:rows], near[rows:], far[:rows], far[rows:]]
    odd = me % 2 == 1
    parts = [jnp.where(odd, parts[i ^ 1], parts[i]) for i in range(4)]
    high = me >= 2
    parts = [jnp.where(high, parts[i ^ 2], parts[i]) for i in range(4)]
    return jnp.concatenate(parts, axis=1)


def own_groups_kernel(order_ref, query_ref, key_ref, value_ref, out_ref):
    out_ref[:, :384] = query_ref[...]
    out_ref[:, 384:512] = key_ref[...]
    out_ref[:, 512:] = value_ref[...]


def own_groups(weight, order):
    rows = weight.shape[0]
    last = order.shape[0] - 1
    spec = lambda w, at: pl.BlockSpec((rows, w), lambda j, o: (0, at + 2 * j + o[last]))
    return pl.pallas_call(
        own_groups_kernel,
        grid_spec=pltpu.PrefetchScalarGridSpec(
            num_scalar_prefetch=1,
            grid=(2,),
            in_specs=[spec(384, 0), spec(128, 12), spec(128, 16)],
            out_specs=pl.BlockSpec((rows, 640), lambda j, o: (0, j)),
        ),
        out_shape=pltpu.HBM((rows, 1280), weight.dtype),
        cost_estimate=pl.CostEstimate(flops=10**8, bytes_accessed=10**6, transcendentals=0),
        name="own_groups",
    )(order, weight, weight, weight)


def shard_order():
    shards = lax.axis_size("shard")
    me = lax.axis_index("shard")
    core = lax.axis_index("expert") % 2
    if shards != 4:
        return jnp.concatenate([jnp.arange(shards, dtype=jnp.int32), core[None].astype(jnp.int32)])
    return jnp.stack([me, me ^ 1, me ^ 2, me ^ 3, me ^ 3, core]).astype(jnp.int32)


def add_low(*terms):
    total = terms[0].astype(jnp.float32)
    for term in terms[1:]:
        total = total + term.astype(jnp.float32)
    return total.astype(jnp.bfloat16)


def reduce_first(blocks):
    if lax.axis_size("shard") != 4:
        return (lax.psum_scatter(blocks, "shard", scatter_dimension=0, tiled=False),)
    me = lax.axis_index("shard")
    own, beside, above, far = (
        lax.dynamic_index_in_dim(blocks, me ^ r, 0, keepdims=False) for r in range(4)
    )
    half = own.shape[0] // 2
    from_x = across(jnp.concatenate([far[:half], beside[:half]]), 1)
    from_y = across(jnp.concatenate([far[half:], above[half:]]), 2)
    return own, beside[half:], above[:half], from_x, from_y


def reduce_second(state):
    if len(state) == 1:
        return state
    own, beside, above, from_x, from_y = state
    half = own.shape[0] // 2
    last_x = across(add_low(beside, from_y[:half]), 1)
    last_y = across(add_low(above, from_x[:half]), 2)
    return own, from_x, from_y, last_x, last_y


def reduce_last(state, dtype=jnp.bfloat16):
    if len(state) == 1:
        return state[0].astype(dtype)
    own, from_x, from_y, last_x, last_y = (v.astype(jnp.float32) for v in state)
    half = own.shape[0] // 2
    low_half, high_half = own[:half] + from_x[half:] + last_y, own[half:] + last_x + from_y[half:]
    return jnp.concatenate([low_half, high_half]).astype(dtype)


def chip_ahead(value, distance):
    count = lax.axis_size("expert")
    return lax.ppermute(value, "expert", [(i, (i + 2 * distance) % count) for i in range(count)])


def chips_send(value):
    chips = lax.axis_size("expert") // 2
    z = lax.axis_index("expert") // 2
    size = value.shape[0] // chips
    part = lambda d: lax.dynamic_slice_in_dim(value, (z + d) % chips * size, size, 0)
    return [part(0)] + [chip_ahead(part(d), d) for d in range(1, chips)]


def chips_gather(parts):
    mine = add_low(*parts)
    return [mine] + [chip_ahead(mine, d) for d in range(1, len(parts))]


def chips_order(parts):
    chips = len(parts)
    z = lax.axis_index("expert") // 2
    size = parts[0].shape[0]
    onward = [parts[-j % chips] for j in range(chips)]
    return lax.dynamic_slice_in_dim(
        jnp.concatenate(onward + onward[:-1]), (chips - z) % chips * size, chips * size, 0
    )


def piece_copies(pieces, order_ref, target, sem, axis, split, base=0, stride=None, window=None):
    copies = []
    slot = 0
    block = pieces[0].shape[1:]
    stride = block[axis] if stride is None else stride
    align = 128 if axis == len(block) - 1 else 16
    for piece in pieces:
        for c in range(piece.shape[0]):
            shape = piece.shape[1:]
            start = [0] * len(shape)
            if slot == 4 and shape[split] < block[split]:
                start[split] = block[split] - shape[split]
            start[axis] = pl.multiple_of(order_ref[slot] * stride + base + start[axis], align)
            index = tuple(pl.ds(first, size) for first, size in zip(start, shape))
            source = piece.at[c]
            if window is not None:
                cols = shape[-1] // 2
                source = source.at[:, window * cols : (window + 1) * cols]
                index = index[:-1] + (slice(None),)
            copies.append(pltpu.make_async_copy(source, target.at[index], sem))
            slot += 1
    return copies


def attend_kernel(count, call, order_ref, group_ref, hidden_ref, cos_ref, sin_ref, bias_ref, *rest):
    mine, other = rest[:count], rest[count : 2 * count]
    att_ref, q_ref, k_ref, v_ref, lse_ref, weight_ref, sems = rest[-7:]
    step = pl.program_id(0)
    first = piece_copies(mine, order_ref, weight_ref.at[0], sems.at[0], 0, 0, window=call)
    second = piece_copies(other, order_ref, weight_ref.at[1], sems.at[1], 0, 0, window=call)

    @pl.when(step == 0)
    def _():
        for copy in first + second:
            copy.start()
        for copy in first:
            copy.wait()

    @pl.when(step == 1)
    def _():
        for copy in second:
            copy.wait()

    hidden = hidden_ref[...]
    cosine, sine = cos_ref[...], sin_ref[...]
    mixed = dot(hidden, weight_ref[step], NN)
    low = jnp.bfloat16
    scaling = HEAD_DIM ** (-0.5)
    for p in range(3):
        part = mixed[:, 128 * p : 128 * p + 128]
        turned_part = (part * cosine + turned(part) * sine).astype(low)
        q_ref[:, 128 * p : 128 * p + 128] = turned_part * scaling
    part = mixed[:, 384:512]
    k_ref[...] = (part * cosine + turned(part) * sine).astype(low)
    v_ref[...] = mixed[:, 512:640].astype(low)
    tokens = hidden.shape[0]
    for seg in range(tokens // SEG):
        rows = pl.ds(seg * SEG, SEG)
        span = (seg + 1) * SEG
        bias = bias_ref[rows, :span]
        keys = [k_ref[:span, HEAD_DIM * kv : HEAD_DIM * (kv + 1)] for kv in range(2)]
        vals = [v_ref[:span, HEAD_DIM * kv : HEAD_DIM * (kv + 1)] for kv in range(2)]
        queries = [q_ref[rows, HEAD_DIM * h : HEAD_DIM * (h + 1)] for h in range(6)]
        scores = [dot(queries[h], keys[h // 3], NT) + bias for h in range(6)]
        highest = [jnp.max(v, axis=1, keepdims=True) for v in scores]
        powers = [jnp.exp(v - m) for v, m in zip(scores, highest)]
        totals = [jnp.sum(v, axis=1, keepdims=True) for v in powers]
        probs = [(v * (1.0 / t)).astype(low) for v, t in zip(powers, totals)]
        outs = [dot(v, vals[h // 3], NN) for h, v in enumerate(probs)]
        logs = [m + jnp.log(t) for m, t in zip(highest, totals)]
        att_ref[rows, :] = jnp.concatenate(outs, axis=1).astype(low)
        lse_ref[rows, :] = jnp.concatenate(logs + [logs[-1]] * 2, axis=1)


def attend(hidden, mixer_p, call, order, groups, cosine, sine, bias, kept):
    tokens, width = hidden.shape
    low = jnp.bfloat16
    whole = lambda a: pl.BlockSpec(a.shape, lambda j, o, g: (0, 0))
    anywhere = pl.BlockSpec(memory_space=pltpu.HBM)
    col = lambda w: pl.BlockSpec((tokens, w), lambda j, o, g: (0, g[j]))
    shape = lambda w: pltpu.HBM((tokens, w), low)
    operands = [order, groups, hidden, cosine, sine, bias, *mixer_p]
    in_specs = [whole(hidden), whole(cosine), whole(sine), whole(bias)]
    in_specs += [anywhere] * len(mixer_p)
    aliases = {}
    if kept is not None:
        aliases = {len(operands) + i: i for i in range(5)}
        operands += list(kept)
        in_specs += [anywhere] * 5
    cols = mixer_p[0].shape[-1] // 2
    return pl.pallas_call(
        lambda *refs: attend_kernel(len(mixer_p) // 2, call, *refs),
        grid_spec=pltpu.PrefetchScalarGridSpec(
            num_scalar_prefetch=2,
            grid=(2,),
            in_specs=in_specs,
            out_specs=[col(384), col(384), col(128), col(128)]
            + [pl.BlockSpec((None, tokens, 8), lambda j, o, g: (g[j], 0, 0))],
            scratch_shapes=[pltpu.VMEM((2, width, cols), low), pltpu.SemaphoreType.DMA((2,))],
        ),
        out_shape=[shape(1536), shape(1536), shape(512), shape(512)]
        + [pltpu.HBM((4, tokens, 8), jnp.float32)],
        input_output_aliases=aliases,
        compiler_params=pltpu.CompilerParams(vmem_limit_bytes=40 * 2**20),
        cost_estimate=pl.CostEstimate(flops=48 * 10**9, bytes_accessed=8 * 10**6, transcendentals=0),
        name="attend",
    )(*operands)


def projector_copies(count, pieces, order_ref, target, sem):
    rows = pieces[0].shape[1]
    slots = order_ref.shape[0] - 1
    core = order_ref[slots]
    copies = piece_copies(pieces[:count], order_ref, target, sem, 0, 0, core * rows, 2 * rows)
    return copies + piece_copies(
        pieces[count:], order_ref, target, sem, 0, 0, (1 - core) * rows, 2 * rows
    )


def row_to_column(row, lane):
    low = jnp.bfloat16
    pick = (lax.broadcasted_iota(jnp.int32, (8, 128), 1) == lane) & (
        lax.broadcasted_iota(jnp.int32, (8, 128), 0) == 0
    )
    pick = pick.astype(jnp.float32).astype(low)
    rows = jnp.broadcast_to(row, (8, row.shape[1]))
    high = rows.astype(low)
    rest = (rows - high.astype(jnp.float32)).astype(low)
    return (dot(high, pick, TN) + dot(rest, pick, TN)).astype(low)


def attend_back_kernel(mine, counts, call, group_ref, order_ref, branch_ref, hidden_ref, q_ref, k_ref, v_ref, lse_ref, cos_ref, sin_ref, bias_ref, *rest):
    first, second = counts
    pieces, mixer_p = rest[:first], rest[first : first + second]
    rest = rest[first + second :]
    if call:
        part_ref, x_ref, resid_ref, gain_ref = rest[:4]
        rest = rest[4:]
    wide_refs, input_ref = rest[:2], rest[2]
    proj_ref, weight_ref, mixed_ref, grad_ref, dk_ref, dv_ref, total_ref, sems = rest[3:]
    step = pl.program_id(0)
    load = projector_copies(mine, pieces, order_ref, proj_ref, sems.at[0])
    half = second // 2
    more = [
        piece_copies(mixer_p[c * half : (c + 1) * half], order_ref, weight_ref.at[c], sems.at[1 + c], 0, 0, window=call)
        for c in range(2)
    ]

    @pl.when(step == 0)
    def _():
        for copy in load + more[0] + more[1]:
            copy.start()
        for copy in load:
            copy.wait()

    group = group_ref[step]
    low = jnp.bfloat16
    rows = pl.ds(pl.multiple_of(group * 384, 128), 384)
    grad_ref[...] = dot(branch_ref[...], proj_ref[rows, :], NT).astype(low)
    cosine, sine = cos_ref[...], sin_ref[...]
    scaling = HEAD_DIM ** (-0.5)
    tokens = branch_ref.shape[0]
    for seg in reversed(range(tokens // SEG)):
        rows = pl.ds(seg * SEG, SEG)
        span = (seg + 1) * SEG
        bias = bias_ref[rows, :span]
        part = lambda ref, r, h: ref[r, HEAD_DIM * h : HEAD_DIM * (h + 1)]
        keys = [part(k_ref, pl.ds(0, span), kv) for kv in range(2)]
        vals = [part(v_ref, pl.ds(0, span), kv) for kv in range(2)]
        queries = [part(q_ref, rows, h) for h in range(6)]
        grads = [part(grad_ref, rows, h) for h in range(6)]
        scores = [dot(queries[h], keys[h // 3], NT) + bias for h in range(6)]
        gprobs = [dot(grads[h], vals[h // 3], NT) for h in range(6)]
        probs = [jnp.exp(v - lse_ref[rows, h : h + 1]) for h, v in enumerate(scores)]
        centres = [jnp.sum(p * g, axis=1, keepdims=True) for p, g in zip(probs, gprobs)]
        gscore = [(p * (g - c)).astype(low) for p, g, c in zip(probs, gprobs, centres)]
        probs = [p.astype(low) for p in probs]
        gqs = [dot(v, keys[h // 3], NN) * scaling for h, v in enumerate(gscore)]
        three = lambda values, kv: jnp.concatenate(values[3 * kv : 3 * kv + 3], 0)
        gks = [dot(three(gscore, kv), three(queries, kv), TN) for kv in range(2)]
        gvs = [dot(three(probs, kv), three(grads, kv), TN) for kv in range(2)]
        gq = jnp.concatenate(gqs, axis=1)
        cos_rows, sin_rows = cosine[seg * SEG : span], sine[seg * SEG : span]
        for p in range(3):
            part = gq[:, 128 * p : 128 * p + 128]
            mixed_ref[rows, 128 * p : 128 * p + 128] = (
                part * cos_rows - turned(part * sin_rows)
            ).astype(low)
        gk = jnp.concatenate(gks, axis=1)
        gv = jnp.concatenate(gvs, axis=1)
        if span == tokens:
            dk_ref[...] = gk
            dv_ref[...] = gv
        else:
            dk_ref[:span, :] += gk
            dv_ref[:span, :] += gv
    gk = dk_ref[...]
    mixed_ref[:, 384:512] = (gk * cosine - turned(gk * sine)).astype(low)
    mixed_ref[:, 512:640] = dv_ref[...].astype(low)
    for c in range(2):

        @pl.when(step == c)
        def _():
            for copy in more[c]:
                copy.wait()

    wide = dot(hidden_ref[...], mixed_ref[...], TN).astype(low)
    part = dot(mixed_ref[...], weight_ref[step], NT)
    for c in range(2):

        @pl.when(step == c)
        def _():
            wide_refs[c][:, :640] = wide

    if not call:

        @pl.when(step == 0)
        def _():
            input_ref[...] = part

        @pl.when(step > 0)
        def _():
            input_ref[...] += part

        return

    @pl.when(step == 0)
    def _():
        total_ref[...] = part + part_ref[...]

    @pl.when(step > 0)
    def _():
        value = x_ref[...].astype(jnp.float32)
        scale = lax.rsqrt(jnp.mean(value * value, axis=1, keepdims=True) + EPSILON)
        normed = value * scale
        grad = total_ref[...] + part
        product = grad * normed
        gains = row_to_column(jnp.sum(product, axis=0, keepdims=True), 0)
        for ref in wide_refs:
            ref[:, 640:] = gains
        grad = grad * gain_ref[...]
        mean = jnp.mean(grad * normed, axis=1, keepdims=True)
        input_ref[...] = (resid_ref[...] + scale * (grad - normed * mean)).astype(low)


def attend_back(call, branch, hidden, proj, mixer_p, order, groups, q, k, v, lse, cosine, sine, bias, *more):
    tokens, width = branch.shape
    low = jnp.bfloat16
    whole = lambda a: pl.BlockSpec(a.shape, lambda j, g, o: (0, 0))
    col = lambda w: pl.BlockSpec((tokens, w), lambda j, g, o: (0, g[j]))
    cols = mixer_p[0].shape[-1] // 2
    mine = len(mixer_p) // 2
    wide = jax.ShapeDtypeStruct((width, cols + 128 * call), low)
    given = jax.ShapeDtypeStruct((tokens, width), low if call else jnp.float32)
    return pl.pallas_call(
        lambda *refs: attend_back_kernel(mine, (len(proj), len(mixer_p)), call, *refs),
        grid_spec=pltpu.PrefetchScalarGridSpec(
            num_scalar_prefetch=2,
            grid=(2,),
            in_specs=[whole(branch), whole(hidden), col(384), col(128), col(128)]
            + [pl.BlockSpec((None, tokens, 8), lambda j, g, o: (g[j], 0, 0))]
            + [whole(cosine), whole(sine), whole(bias)]
            + [pl.BlockSpec(memory_space=pltpu.HBM)] * (len(proj) + len(mixer_p))
            + [whole(value) for value in more],
            out_specs=[whole(wide), whole(wide), whole(given)],
            scratch_shapes=[
                pltpu.VMEM((width, width), low),
                pltpu.VMEM((2, width, cols), low),
                pltpu.VMEM((tokens, cols), low),
                pltpu.VMEM((tokens, 384), low),
                pltpu.VMEM((tokens, 128), jnp.float32),
                pltpu.VMEM((tokens, 128), jnp.float32),
                pltpu.VMEM((tokens, width) if call else (8, 128), jnp.float32),
                pltpu.SemaphoreType.DMA((3,)),
            ],
        ),
        out_shape=[wide, wide, given],
        compiler_params=pltpu.CompilerParams(vmem_limit_bytes=58 * 2**20),
        cost_estimate=pl.CostEstimate(flops=60 * 10**9, bytes_accessed=8 * 10**6, transcendentals=0),
        name="attend_back",
    )(groups, order, branch, hidden, q, k, v, lse, cosine, sine, bias, *proj, *mixer_p, *more)


TILE = 256


def extra_rows(expert_count):
    return 8 if expert_count <= 24 else 16


def table_picks(expert_count):
    extra = extra_rows(expert_count)
    row = lax.broadcasted_iota(jnp.int32, (extra, 128), 0)
    lane = lax.broadcasted_iota(jnp.int32, (extra, 128), 1)
    return [
        (lane == row + block * extra).astype(jnp.float32).astype(jnp.bfloat16)
        for block in range(expert_count // extra)
    ]


def table_rows(values, picks, width):
    low = jnp.bfloat16
    high = values.astype(low)
    parts = (high, (values - high.astype(jnp.float32)).astype(low))
    rows = [dot(pick, value, NT).astype(low) for pick in picks for value in parts]
    left = width - TILE * len(rows)
    if left:
        rows.append(jnp.zeros((picks[0].shape[0], left), low))
    return jnp.concatenate(rows, axis=1)


def table_values(rows, picks):
    total = None
    for block, pick in enumerate(picks):
        for part in range(2):
            at = (2 * block + part) * TILE
            value = dot(rows[:, at : at + TILE], pick, TN)
            total = value if total is None else total + value
    return total


def project_kernel(mine, count, expert_count, order_ref, left_ref, x_ref, routes_ref, gain_ref, router_ref, *rest):
    pieces = rest[:count]
    resid_ref, gates_ref, rows_ref, weight_ref, sem = rest[count:]
    copies = projector_copies(mine, pieces, order_ref, weight_ref, sem)

    @pl.when(pl.program_id(0) == 0)
    def _():
        for copy in copies:
            copy.start()
        for copy in copies:
            copy.wait()

    low = jnp.bfloat16
    resid = x_ref[...].astype(jnp.float32) + dot(left_ref[...], weight_ref[...], NN)
    resid_ref[...] = resid
    scale = lax.rsqrt(jnp.mean(resid * resid, axis=1, keepdims=True) + EPSILON)
    hidden = (resid * scale * gain_ref[...]).astype(low)
    rows_ref[:TILE, :] = hidden
    logits = dot(hidden, router_ref[...], NT)
    lane = lax.broadcasted_iota(jnp.int32, logits.shape, 1)
    routed = lane == routes_ref[:, 0:1]
    for k in range(1, routes_ref.shape[1]):
        routed = routed | (lane == routes_ref[:, k : k + 1])
    logits = jnp.where(routed, logits, NEGATIVE)
    powers = jnp.exp(logits - jnp.max(logits, axis=1, keepdims=True))
    gates = powers / jnp.sum(powers, axis=1, keepdims=True)
    gates_ref[...] = gates
    rows_ref[TILE:, :] = table_rows(gates, table_picks(expert_count), hidden.shape[1])


def project(left, x, routes, gain, router, expert_count, proj, mine, order):
    tokens, width = left.shape
    tall = TILE + extra_rows(expert_count)
    tile = lambda w, h=TILE: pl.BlockSpec((h, w), lambda i, o: (i, 0))
    whole = lambda a: pl.BlockSpec(a.shape, lambda i, o: (0, 0))
    return pl.pallas_call(
        lambda *refs: project_kernel(mine, len(proj), expert_count, *refs),
        grid_spec=pltpu.PrefetchScalarGridSpec(
            num_scalar_prefetch=1,
            grid=(tokens // TILE,),
            in_specs=[tile(width), tile(width), tile(routes.shape[1]), whole(gain), whole(router)]
            + [pl.BlockSpec(memory_space=pltpu.HBM)] * len(proj),
            out_specs=[tile(width), tile(128), tile(width, tall)],
            scratch_shapes=[pltpu.VMEM((width, width), jnp.bfloat16), pltpu.SemaphoreType.DMA],
        ),
        out_shape=[
            jax.ShapeDtypeStruct((tokens, width), jnp.float32),
            jax.ShapeDtypeStruct((tokens, 128), jnp.float32),
            jax.ShapeDtypeStruct((tokens // TILE * tall, width), jnp.bfloat16),
        ],
        compiler_params=pltpu.CompilerParams(vmem_limit_bytes=40 * 2**20),
        cost_estimate=pl.CostEstimate(flops=30 * 10**9, bytes_accessed=8 * 10**6, transcendentals=0),
        name="project",
    )(order, left, x, routes, gain, router, *proj)


def turn_kernel(expert_count, order_ref, a_ref, b_ref, c_ref, rows_ref, gates_ref, resid_ref, cot_ref, left_ref, gain_ref, router_ref,
                branch_ref, grad_ref, mine_ref, other_ref, low_ref, small_ref, gains_ref):
    low = jnp.bfloat16
    step = pl.program_id(0)
    total = a_ref[...].astype(jnp.float32) + b_ref[...].astype(jnp.float32) + c_ref[...].astype(jnp.float32)
    gates = gates_ref[...]
    grad_gates = table_values(total[TILE:, :].astype(low), table_picks(expert_count))
    mean = jnp.sum(gates * grad_gates, axis=1, keepdims=True)
    grad_logits = gates * (grad_gates - mean)
    high = grad_logits.astype(low)
    rest = (grad_logits - high.astype(jnp.float32)).astype(low)
    grad = total[:TILE, :] + dot(high, router_ref[...], NN) + dot(rest, router_ref[...], NN)
    resid = resid_ref[...]
    scale = lax.rsqrt(jnp.mean(resid * resid, axis=1, keepdims=True) + EPSILON)
    normed = resid * scale
    hidden = rows_ref[:TILE, :]
    small = dot(hidden, jnp.concatenate([high, rest], axis=1), TN)
    small = small[:, :128] + small[:, 128:]
    gains = jnp.sum(grad * normed, axis=0, keepdims=True)
    grad = grad * gain_ref[...]
    mean = jnp.mean(grad * normed, axis=1, keepdims=True)
    grad = cot_ref[...].astype(jnp.float32) + scale * (grad - normed * mean)
    grad_ref[...] = grad
    branch = grad.astype(low)
    branch_ref[...] = branch
    low_ref[pl.ds(pl.multiple_of(step * TILE, TILE), TILE), :] = branch

    @pl.when(step == 0)
    def _():
        small_ref[...] = small
        gains_ref[...] = gains

    @pl.when(step > 0)
    def _():
        small_ref[...] += small
        gains_ref[...] += gains

    @pl.when(step == pl.num_programs(0) - 1)
    def _():
        core = order_ref[order_ref.shape[0] - 1]
        half = low_ref.shape[1] // 2
        left = left_ref[...]
        small = small_ref[...].astype(low) + row_to_column(gains_ref[...], expert_count)
        for ref, which in ((mine_ref, core), (other_ref, 1 - core)):
            part = low_ref[:, pl.ds(pl.multiple_of(which * half, 128), half)]
            ref[:, :half] = dot(left, part, TN).astype(low)
            ref[:, half:] = small


def turn(expert_count, order, a, b, c, rows, gates, resid, cots, left, gain, router):
    tokens, width = left.shape
    tall = TILE + extra_rows(expert_count)
    tile = lambda w, h=TILE: pl.BlockSpec((h, w), lambda i, o: (i, 0))
    whole = lambda a: pl.BlockSpec(a.shape, lambda i, o: (0, 0))
    half = jax.ShapeDtypeStruct((width, width // 2 + 128), jnp.bfloat16)
    return pl.pallas_call(
        lambda *refs: turn_kernel(expert_count, *refs),
        grid_spec=pltpu.PrefetchScalarGridSpec(
            num_scalar_prefetch=1,
            grid=(tokens // TILE,),
            in_specs=[tile(width, tall)] * 4 + [tile(128), tile(width), tile(width), whole(left)]
            + [whole(gain), whole(router)],
            out_specs=[tile(width), tile(width), whole(half), whole(half)],
            scratch_shapes=[
                pltpu.VMEM((tokens, width), jnp.bfloat16),
                pltpu.VMEM((width, 128), jnp.float32),
                pltpu.VMEM((1, width), jnp.float32),
            ],
        ),
        out_shape=[
            jax.ShapeDtypeStruct((tokens, width), jnp.bfloat16),
            jax.ShapeDtypeStruct((tokens, width), jnp.float32),
            half,
            half,
        ],
        compiler_params=pltpu.CompilerParams(vmem_limit_bytes=58 * 2**20),
        cost_estimate=pl.CostEstimate(flops=30 * 10**9, bytes_accessed=8 * 10**6, transcendentals=0),
        name="turn",
    )(order, a, b, c, rows, gates, resid, cots, left, gain, router)


def fold_kernel(pairs, order_ref, *refs):
    x_ref, y_ref, own_ref, beside_ref, above_ref = refs[2 * pairs :]
    step = pl.program_id(0)
    half = x_ref.shape[0] // 2
    low, high = slice(0, half), slice(half, 2 * half)
    places = (
        ((own_ref, low), (own_ref, high)),
        ((x_ref, high), (beside_ref, low)),
        ((above_ref, low), (y_ref, high)),
        ((x_ref, low), (y_ref, low)),
    )
    at = 0
    for i in range(pairs):
        value = refs[2 * i][...] + refs[2 * i + 1][...]
        columns = slice(at, at + value.shape[1])
        at += value.shape[1]
        for r, ((first, first_rows), (second, second_rows)) in enumerate(places):

            @pl.when(step == r)
            def _():
                first[first_rows, columns] = value[low]
                second[second_rows, columns] = value[high]


def fold(order, *operands):
    if lax.axis_size("shard") != 4:
        parts = [add_low(operands[i], operands[i + 1]) for i in range(0, len(operands), 2)]
        blocks = jnp.concatenate(parts, axis=1)
        return reduce_first(blocks.reshape(lax.axis_size("shard"), -1, blocks.shape[1]))
    rows = operands[0].shape[0] // 4
    columns = sum(v.shape[1] for v in operands[::2])
    given = [jax.ShapeDtypeStruct((n * rows // 2, columns), jnp.bfloat16) for n in (2, 2, 2, 1, 1)]
    x, y, own, beside, above = pl.pallas_call(
        lambda *refs: fold_kernel(len(operands) // 2, *refs),
        grid_spec=pltpu.PrefetchScalarGridSpec(
            num_scalar_prefetch=1,
            grid=(4,),
            in_specs=[pl.BlockSpec((rows, v.shape[1]), lambda i, o: (o[i], 0)) for v in operands],
            out_specs=[pl.BlockSpec(v.shape, lambda i, o: (0, 0)) for v in given],
        ),
        out_shape=given,
        compiler_params=pltpu.CompilerParams(vmem_limit_bytes=40 * 2**20),
        cost_estimate=pl.CostEstimate(flops=3 * 10**9, bytes_accessed=4 * 10**6, transcendentals=0),
        name="fold",
    )(order, *operands)
    return own, beside, above, across(x, 1), across(y, 2)


def finish_kernel(order_ref, one_mine, one_other, two_mine, two_other, mixer_ref, proj_ref, router_ref, second_ref, first_ref):
    lower = order_ref[order_ref.shape[0] - 1] == 0
    wide = jnp.float32
    half = proj_ref.shape[1] // 2
    groups = []
    for mine, other in ((one_mine, one_other), (two_mine, two_other)):
        a, b = mine[:, :640].astype(wide), other[:, :640].astype(wide)
        groups += [jnp.where(lower, a, b), jnp.where(lower, b, a)]
    for g, value in enumerate(groups):
        mixer_ref[:, 384 * g : 384 * (g + 1)] = value[:, :384]
        mixer_ref[:, 1536 + 128 * g : 1536 + 128 * (g + 1)] = value[:, 384:512]
        mixer_ref[:, 2048 + 128 * g : 2048 + 128 * (g + 1)] = value[:, 512:]
    a, b = one_mine[:, 640 : 640 + half].astype(wide), one_other[:, 640 : 640 + half].astype(wide)
    proj_ref[:, :half] = jnp.where(lower, a, b)
    proj_ref[:, half:] = jnp.where(lower, b, a)
    experts = router_ref.shape[0]
    size = (experts + 8, 128)
    pick = lax.broadcasted_iota(jnp.int32, size, 0) == lax.broadcasted_iota(jnp.int32, size, 1)
    pick = pick.astype(wide).astype(jnp.bfloat16)
    rows = dot(pick, one_mine[:, 640 + half :], NT)
    router_ref[...] = rows[:experts, :]
    second_ref[...] = rows[experts : experts + 1, :]
    first_ref[...] = dot(pick, two_mine[:, 640:], NT)[:1, :]


def finish(expert_count, order, one, two):
    rows = one[0].shape[0]
    block = 128 if rows % 128 == 0 else rows
    tall = [jax.ShapeDtypeStruct((rows, w), jnp.float32) for w in (2560, 1536)]
    flat = [jax.ShapeDtypeStruct((h, rows), jnp.float32) for h in (expert_count, 1, 1)]
    spec = lambda a: pl.BlockSpec((block, a.shape[1]), lambda i, o: (i, 0))
    flat_spec = lambda a: pl.BlockSpec((a.shape[0], block), lambda i, o: (0, i))
    operands = [*one, *two]
    return pl.pallas_call(
        finish_kernel,
        grid_spec=pltpu.PrefetchScalarGridSpec(
            num_scalar_prefetch=1,
            grid=(rows // block,),
            in_specs=[spec(v) for v in operands],
            out_specs=[spec(v) for v in tall] + [flat_spec(v) for v in flat],
        ),
        out_shape=tall + flat,
        cost_estimate=pl.CostEstimate(flops=10**9, bytes_accessed=4 * 10**6, transcendentals=0),
        name="finish",
    )(order, *operands)


def expert_kernel(counts, expert_count, order_ref, place_ref, xa_ref, u_ref, *rest):
    pieces, more = counts
    gates_p, ups_p, downs_p = (rest[i * pieces : (i + 1) * pieces] for i in range(3))
    rest = rest[3 * pieces + more :]
    (gt_ref, out_ref, x_ref, mid_ref, sides_ref, wg_ref, wu_ref, wd_ref, sems) = rest
    low = jnp.bfloat16
    extra = extra_rows(expert_count)
    step = pl.program_id(0)
    loads = [
        piece_copies(gates_p, order_ref, wg_ref, sems.at[0], 1, 0),
        piece_copies(ups_p, order_ref, wu_ref, sems.at[1], 1, 0),
        piece_copies(downs_p, order_ref, wd_ref, sems.at[2], 2, 0),
    ]

    @pl.when(step == 0)
    def _():
        for load in loads:
            for copy in load:
                copy.start()

    def arrive(number):
        @pl.when(step == 0)
        def _():
            for copy in loads[number]:
                copy.wait()

    rows, table, cots = xa_ref[:TILE, :], xa_ref[TILE:, :], u_ref[...]
    x_ref[...] = rows
    row = lax.broadcasted_iota(jnp.int32, (extra, 128), 0)
    lane = lax.broadcasted_iota(jnp.int32, (extra, 128), 1)
    expert = place_ref[1] * 2 + lane
    picks = []
    for block in range(expert_count // extra):
        hit = (lane < 2) & (row == expert - block * extra)
        picks.append(jnp.where(hit, 1.0, 0.0).astype(low))
    gates_wide = table_values(table, picks)
    arrive(0)
    gate_ins = [dot(rows, wg_ref[l], NN) for l in range(2)]
    arrive(1)
    up_ins = [dot(rows, wu_ref[l], NN) for l in range(2)]
    arrive(2)
    out = None
    taken = None
    sums = []
    for l in range(2):
        gates = gates_wide[:, l : l + 1]
        gate_in, up_in = gate_ins[l], up_ins[l]
        back = dot(cots, wd_ref[l], NT)
        sigma = 1.0 / (1.0 + jnp.exp(-gate_in))
        active = gate_in * sigma
        mid = active * up_in
        sums.append(jnp.sum(mid * back, axis=1, keepdims=True))
        mid_low = (mid * gates).astype(low)
        mid_ref[l] = mid_low
        part = dot(mid_low, wd_ref[l], NN)
        out = part if out is None else out + part
        back = back * gates
        grad_gate = (back * up_in * sigma * (1.0 + gate_in * (1.0 - sigma))).astype(low)
        grad_up = (back * active).astype(low)
        sides_ref[2 * l] = grad_gate
        sides_ref[2 * l + 1] = grad_up
        part = dot(grad_gate, wg_ref[l], NT) + dot(grad_up, wu_ref[l], NT)
        taken = part if taken is None else taken + part
    out_ref[...] = out.astype(low)
    gt_ref[:TILE, :] = taken.astype(low)
    wide = lax.broadcasted_iota(jnp.int32, (TILE, 128), 1)
    sums = jnp.where(wide == 0, sums[0], jnp.where(wide == 1, sums[1], 0.0))
    gt_ref[TILE:, :] = table_rows(sums, picks, rows.shape[1])


def expert_chunk(order, place, xa, cots, gates, ups, downs, expert_count, kept):
    total, width = cots.shape
    devices = lax.axis_size("expert")
    tokens = total // devices
    hidden = gates[0].shape[-1]
    steps = tokens // TILE
    low = jnp.bfloat16
    tall = TILE + extra_rows(expert_count)
    own = pl.BlockSpec((tall, width), lambda i, o, p: (i, 0))
    anywhere = pl.BlockSpec(memory_space=pltpu.HBM)
    big_row = pl.BlockSpec((TILE, width), lambda i, o, p: (p[0] * steps + i, 0))
    big = lambda n: pl.BlockSpec((n, TILE, hidden), lambda i, o, p: (0, p[0] * steps + i, 0))
    single = jax.ShapeDtypeStruct((steps * tall, width), low)
    shapes = [jax.ShapeDtypeStruct((total, width), low)] * 2
    shapes += [jax.ShapeDtypeStruct((n, total, hidden), low) for n in (2, 4)]
    operands = [order, place, xa, cots, *gates, *ups, *downs]
    in_specs = [own, big_row] + [anywhere] * (3 * len(gates))
    aliases = {}
    more = 0
    if kept is not None:
        more = len(shapes)
        aliases = {len(operands) + i: 1 + i for i in range(more)}
        operands += list(kept)
        in_specs += [anywhere] * more
    res = pl.pallas_call(
        lambda *refs: expert_kernel((len(gates), more), expert_count, *refs),
        grid_spec=pltpu.PrefetchScalarGridSpec(
            num_scalar_prefetch=2,
            grid=(steps,),
            in_specs=in_specs,
            out_specs=[own, big_row, big_row, big(2), big(4)],
            scratch_shapes=[
                pltpu.VMEM((2, width, hidden), low),
                pltpu.VMEM((2, width, hidden), low),
                pltpu.VMEM((2, hidden, width), low),
                pltpu.SemaphoreType.DMA((3,)),
            ],
        ),
        out_shape=[single] + shapes,
        input_output_aliases=aliases,
        compiler_params=pltpu.CompilerParams(vmem_limit_bytes=58 * 2**20),
        cost_estimate=pl.CostEstimate(flops=50 * 10**9, bytes_accessed=4 * 10**6, transcendentals=0),
        name="expert_chunk",
    )(*operands)
    return res[0], res[1:]


def wide_grad_kernel(on_rows, left_ref, right_ref, out_ref, acc_ref):
    step = pl.program_id(1)
    value = dot(left_ref[...], right_ref[...], TN)

    @pl.when(step == 0)
    def _():
        acc_ref[...] = value

    @pl.when(step > 0)
    def _():
        acc_ref[...] += value

    @pl.when(step == pl.num_programs(1) - 1)
    def _():
        rows, cols = out_ref.shape[-2:]
        for j in range(out_ref.shape[0]):
            if on_rows:
                part = acc_ref[j * rows : (j + 1) * rows, :]
            else:
                part = acc_ref[:, j * cols : (j + 1) * cols]
            out_ref[j] = part.astype(out_ref.dtype)


def weight_grad(left, right, parts, on_rows):
    count = left.shape[0] if left.ndim == 3 else right.shape[0]
    total, size_m = left.shape[-2:]
    size_n = right.shape[-1]
    block = 1024
    spec = lambda a: (
        pl.BlockSpec((None, block, a.shape[-1]), lambda l, k: (l, k, 0))
        if a.ndim == 3
        else pl.BlockSpec((block, a.shape[-1]), lambda l, k: (k, 0))
    )
    shape = (size_m // parts, size_n) if on_rows else (size_m, size_n // parts)
    return pl.pallas_call(
        lambda *refs: wide_grad_kernel(on_rows, *refs),
        grid=(count, total // block),
        in_specs=[spec(left), spec(right)],
        out_specs=pl.BlockSpec((parts, None) + shape, lambda l, k: (0, l, 0, 0)),
        out_shape=jax.ShapeDtypeStruct((parts, count) + shape, jnp.bfloat16),
        scratch_shapes=[pltpu.VMEM((size_m, size_n), jnp.float32)],
        compiler_params=pltpu.CompilerParams(vmem_limit_bytes=48 * 2**20),
        cost_estimate=pl.CostEstimate(flops=60 * 10**9, bytes_accessed=8 * 10**6, transcendentals=0),
        name="weight_grad",
    )(left, right)


def sorted_grad_kernel(on_rows, half, order_ref, left_ref, right_ref, own_ref, beside_ref, above_ref, x_ref, y_ref, acc_ref):
    index, step = pl.program_id(0), pl.program_id(1)
    value = dot(left_ref[...], right_ref[...], TN)

    @pl.when(step == 0)
    def _():
        acc_ref[...] = value

    @pl.when(step > 0)
    def _():
        acc_ref[...] += value

    def block(r):
        rows, cols = own_ref.shape
        size = rows if on_rows else cols
        place = pl.ds(pl.multiple_of(order_ref[r] * size, 128), size)
        part = acc_ref[place, :] if on_rows else acc_ref[:, place]
        return part.astype(own_ref.dtype)

    last = step == pl.num_programs(1) - 1

    @pl.when(last)
    def _():
        own_ref[...] = block(0)

    @pl.when(last & (index < half))
    def _():
        x_ref[0] = block(3)
        x_ref[1] = block(1)
        above_ref[...] = block(2)

    @pl.when(last & (index >= half))
    def _():
        y_ref[0] = block(3)
        y_ref[1] = block(2)
        beside_ref[...] = block(1)


def exchange_first(state):
    if len(state) == 1:
        return reduce_first(state[0])
    own, beside, above, x, y = state
    return own, beside, above, across(x, 1), across(y, 2)


def grad_exchange(left, right, order, on_rows, pick=0, stride=1):
    shards = lax.axis_size("shard")
    if shards != 4:
        return (weight_grad(left, right[pick::stride] if right.ndim == 3 else right, shards, on_rows),)
    count = left.shape[0] if left.ndim == 3 else right.shape[0] // stride
    half = count // 2
    total, size_m = left.shape[-2:]
    size_n = right.shape[-1]
    block = 1024
    spec = lambda a: (
        pl.BlockSpec((None, block, a.shape[-1]), lambda l, k, o: (l * stride + pick, k, 0))
        if a.ndim == 3
        else pl.BlockSpec((block, a.shape[-1]), lambda l, k, o: (k, 0))
    )
    shape = (size_m // 4, size_n) if on_rows else (size_m, size_n // 4)
    early = lambda l: jnp.minimum(l, half - 1)
    late = lambda l: jnp.maximum(l - half, 0)
    one = lambda f: pl.BlockSpec((None,) + shape, lambda l, k, o: (f(l), 0, 0))
    two = lambda f: pl.BlockSpec((2, None) + shape, lambda l, k, o: (0, f(l), 0, 0))
    low = lambda *lead: jax.ShapeDtypeStruct(lead + shape, jnp.bfloat16)
    own, beside, above, x, y = pl.pallas_call(
        lambda *refs: sorted_grad_kernel(on_rows, half, *refs),
        grid_spec=pltpu.PrefetchScalarGridSpec(
            num_scalar_prefetch=1,
            grid=(count, total // block),
            in_specs=[spec(left), spec(right)],
            out_specs=[one(lambda l: l), one(late), one(early), two(early), two(late)],
            scratch_shapes=[pltpu.VMEM((size_m, size_n), jnp.float32)],
        ),
        out_shape=[low(count), low(half), low(half), low(2, half), low(2, half)],
        compiler_params=pltpu.CompilerParams(vmem_limit_bytes=48 * 2**20),
        cost_estimate=pl.CostEstimate(flops=60 * 10**9, bytes_accessed=8 * 10**6, transcendentals=0),
        name="weight_grad",
    )(order, left, right)
    merged = lambda v: v.reshape((2 * half,) + shape)
    return own, beside, above, merged(x), merged(y)


def per_device(
    layer_input,
    out_cotangent,
    parents,
    routes,
    norm1_gain,
    qkv_weight,
    out_weight,
    norm2_gain,
    router_weight,
    gate_weight,
    up_weight,
    down_weight,
):
    low = jnp.bfloat16
    shards = lax.axis_size("shard")
    tokens, width = layer_input.shape
    expert_count = router_weight.shape[1]
    local_count = gate_weight.shape[0]
    chips = lax.axis_size("expert") // 2
    me = lax.axis_index("expert")
    core = me % 2
    order = shard_order()
    queries = HEADS * HEAD_DIM

    block = own_groups(qkv_weight, order)
    small = jnp.concatenate([router_weight, norm1_gain[:, None], norm2_gain[:, None]], axis=1).T
    small = gather_small(small)
    mixer_first = gather_first(block)
    router = jnp.pad(small[:expert_count], ((0, 128 - expert_count), (0, 0)))
    gain_one = small[expert_count].astype(jnp.float32)[None, :]
    gain_two = small[expert_count + 1].astype(jnp.float32)[None, :]
    activity = layer_input.astype(jnp.float32)
    hidden_one = (activity * inverse_rms(activity) * gain_one).astype(low)
    bias, cosine, sine = tree_tables(parents)
    mine = gather_second(mixer_first, 0)
    last_pieces, hidden_one, bias, cosine, sine = lax.optimization_barrier(
        (mine[3:], hidden_one, bias, cosine, sine)
    )
    mine = mine[:3] + last_pieces
    mixer_p = mine + [swap_core(p) for p in mine]
    block = lax.dynamic_slice_in_dim(out_weight, core * (out_weight.shape[0] // 2), out_weight.shape[0] // 2, 0)
    project_first = gather_first(after(block, *mine))

    cots = lax.all_gather(out_cotangent, "expert", axis=0, tiled=True)

    saved = None
    groups = []
    for call in range(2):
        groups.append(jnp.stack([2 * call + core, 2 * call + 1 - core]).astype(jnp.int32))
        saved = attend(hidden_one, mixer_p, call, order, groups[call], cosine, sine, bias, saved)
        if call == 0:
            project_first, saved = lax.optimization_barrier((project_first, saved))
            proj = gather_second(project_first, 0)
            near = swap_core(jnp.concatenate(proj[:3], axis=0))
            gates_first = gather_first(after(gate_weight, project_first))
    proj, near, saved = lax.optimization_barrier((proj, near, saved))
    far = [swap_core(p) for p in proj[3:]]
    ups_first = gather_first(after(up_weight, proj))
    far, gates_first, saved = lax.optimization_barrier((far, gates_first, saved))
    proj = proj + [near] + far
    attended, query, keys, values, log_total = saved
    resid, gates, sent_rows = project(
        attended, layer_input, routes, gain_two, router, expert_count, proj, len(mixer_p) // 2, order
    )
    onward = next_chip(sent_rows)
    ups_first, sent_rows = lax.optimization_barrier((ups_first, sent_rows))
    gates_p = gather_second(gates_first, 0)
    ups_first, down_block = lax.optimization_barrier((ups_first, after(down_weight, *gates_p)))
    downs_first = gather_first(down_block, True)
    ups_p = gather_second(ups_first, 0)
    downs_p = gather_second(downs_first, 0)
    rows = [sent_rows]
    rows.append(onward)
    beside = swap_core(rows[0])
    rows[0], rows[1], beside = lax.optimization_barrier((rows[0], rows[1], beside))
    kept = total = None
    for step in range(chips):
        ahead = next_chip(rows[step + 1]) if step + 2 < chips else None
        beside_next = swap_core(rows[step + 1]) if step + 1 < chips else None
        here = rows[step]
        if step > 1:
            here, beside, total = lax.optimization_barrier((here, beside, total))
        sent = next_chip(total) if step > 1 else None
        source = (me - 2 * step) % (2 * chips)
        place = lambda at: jnp.stack([at, me]).astype(jnp.int32)
        run = lambda at, value, kept: expert_chunk(
            order, place(at), value, cots, gates_p, ups_p, downs_p, expert_count, kept
        )
        other, kept = run(source ^ 1, beside, kept)
        other = swap_core(other)
        mine, kept = run(source, here, kept)
        mine, kept, ahead, beside, sent, other = lax.optimization_barrier(
            (mine, kept, ahead, beside_next, sent, other)
        )
        if ahead is not None:
            rows.append(ahead)
        pair = (mine, other)
        if step == 0:
            last = pair
        else:
            total = add_low(*pair, *(() if sent is None else (sent,)))
    out_all, all_rows, all_mid, all_sides = kept
    all_rows, total = lax.optimization_barrier((all_rows, total))
    sent = next_chip(total)
    gate_state = grad_exchange(all_rows, all_sides, order, True, 0, 2)
    gate_done, all_rows = lax.optimization_barrier((gate_state[0], all_rows))
    gate_state = exchange_first((gate_done,) + gate_state[1:])
    up_state = grad_exchange(all_rows, all_sides, order, True, 1, 2)
    sent, up_done, gate_state = lax.optimization_barrier((sent, up_state[0], gate_state))
    up_state = exchange_first((up_done,) + up_state[1:])
    branch_out = lax.psum_scatter(after(out_all, sent), "expert", scatter_dimension=0, tiled=True)
    grad_branch, grad_resid, out_mine, out_other = turn(
        expert_count, order, *last, sent, sent_rows, gates, resid, out_cotangent, attended, gain_two, router
    )
    grad_branch, up_state, out_other = lax.optimization_barrier((grad_branch, up_state, out_other))
    gate_state, up_state = reduce_second(gate_state), reduce_second(up_state)
    out_sent = swap_core(out_other)
    backward = lambda call, branch, *more: attend_back(
        call, branch, hidden_one, proj, mixer_p, order, groups[call],
        query, keys, values, log_total, cosine, sine, bias, *more,
    )
    wide, other, part = backward(0, grad_branch)
    grad_branch, wide, other, part, out_mine, out_sent, gate_state, up_state = lax.optimization_barrier(
        (grad_branch, wide, other, part, out_mine, out_sent, gate_state, up_state)
    )
    state_one = fold(order, wide, swap_core(other), out_mine, out_sent)
    grad_branch, folded = lax.optimization_barrier((grad_branch, state_one[0]))
    state_one = (folded,) + state_one[1:]
    wide, other, grad_input = backward(1, grad_branch, part, layer_input, grad_resid, gain_one)
    wide, other, grad_input, state_one, all_mid = lax.optimization_barrier(
        (wide, other, grad_input, state_one, all_mid)
    )
    state_one = reduce_second(state_one)
    state_two = fold(order, wide, swap_core(other))
    folded, state_one = lax.optimization_barrier((state_two[0], state_one))
    state_two = (folded,) + state_two[1:]
    one = reduce_last(state_one)
    all_mid, one, folded = lax.optimization_barrier((all_mid, one, state_two[0]))
    state_two = (folded,) + state_two[1:]
    one = chips_send(one)
    down_state = grad_exchange(all_mid, cots, order, False)
    kernel_done, state_two, one, gate_state, up_state = lax.optimization_barrier(
        (down_state[0], state_two, one, gate_state, up_state)
    )
    down_state = (kernel_done,) + down_state[1:]
    state_two = reduce_second(state_two)
    one = chips_gather(one)
    state_two, one, down_state = lax.optimization_barrier((state_two, one, down_state))
    two = chips_send(reduce_last(state_two))
    down_state = exchange_first(down_state)
    one = chips_order(one)
    two, down_state, one = lax.optimization_barrier((two, down_state, one))
    two = chips_gather(two)
    down_state = reduce_second(down_state)
    two, down_state, one = lax.optimization_barrier((two, down_state, one))
    two = chips_order(two)
    one = (one, swap_core(one))
    two = (two, swap_core(two))
    grad_gate = reduce_last(gate_state, jnp.float32)
    grad_up = reduce_last(up_state, jnp.float32)
    grad_down = reduce_last(down_state, jnp.float32)
    output = (resid + branch_out.astype(jnp.float32)).astype(low)
    grad_mixer, grad_projector, grad_router, grad_gain_two, grad_gain_one = finish(
        expert_count, order, one, two
    )
    return (
        output,
        grad_input,
        grad_gain_one[0],
        grad_mixer,
        grad_projector,
        grad_gain_two[0],
        grad_router.T,
        grad_gate,
        grad_up,
        grad_down,
    )


def solution(mesh):
    return jax.shard_map(
        per_device,
        mesh=mesh,
        in_specs=(
            P(("expert", "shard"), None),
            P(("expert", "shard"), None),
            P(("expert", "shard")),
            P(("expert", "shard"), None),
            P("shard"),
            P("shard", None),
            P("shard", None),
            P("shard"),
            P("shard", None),
            P("expert", "shard", None),
            P("expert", "shard", None),
            P("expert", None, "shard"),
        ),
        out_specs=(
            P(("expert", "shard"), None),
            P(("expert", "shard"), None),
            P("shard"),
            P("shard", None),
            P("shard", None),
            P("shard"),
            P("shard", None),
            P("expert", "shard", None),
            P("expert", "shard", None),
            P("expert", None, "shard"),
        ),
        check_vma=False,
    )
```
